32 devices in a mesh: dp: 4 (over z), expert: 8 (over y, x, core).
Axes of the slice: x: 2, y: 2, z: 4, core: 2. Of those that a mesh axis runs over, the one named last changes fastest.
Arguments:
- act_in: float32 [18912, 768], P(('dp', 'expert')), may hold values from -6 to 6
- w_qkv: float32 [2, 768, 2304], P(None, ('dp', 'expert')), may hold values from -0.21875 to 0.21875
- w_proj: float32 [2, 768, 768], P(None, None, ('dp', 'expert')), may hold values from -1.25 to 1.25
- w_up: float32 [768, 3072], P(('dp', 'expert')), may hold values from -0.21875 to 0.21875
- w_down: float32 [3072, 768], P(None, ('dp', 'expert')), may hold values from -0.109375 to 0.109375
- norm_gain: float32 [4, 768], P(None, ('dp', 'expert')), may hold values from 0.1 to 1.9
- norm_shift: float32 [4, 768], P(None, ('dp', 'expert')), may hold values from -3 to 3
- exp_in: float32 [16, 768, 3072], P('expert', 'dp'), may hold values from -0.21875 to 0.21875
- exp_out: float32 [16, 3072, 768], P('expert', None, 'dp'), may hold values from -0.109375 to 0.109375
- gate: float32 [18912, 2], P(('dp', 'expert')), may hold values from 0.2 to 1
- expert_index: int32 [18912, 2], P(('dp', 'expert')), may hold values from 0 to 15, all different within a row; in each aligned block of 591 rows (0 to 590, 591 to 1181, ...) at most 96 rows name the same one
- cotangent: float32 [18912, 768], P(('dp', 'expert')), may hold values from -6 to 6
Outputs:
- act_out: float32 [18912, 768], P(('dp', 'expert'))
- act_grad: float32 [18912, 768], P(('dp', 'expert'))
- grad_qkv: float32 [2, 768, 2304], P(None, ('dp', 'expert'))
- grad_proj: float32 [2, 768, 768], P(None, None, ('dp', 'expert'))
- grad_up: float32 [768, 3072], P(('dp', 'expert'))
- grad_down: float32 [3072, 768], P(None, ('dp', 'expert'))
- grad_gain: float32 [4, 768], P(None, ('dp', 'expert'))
- grad_shift: float32 [4, 768], P(None, ('dp', 'expert'))
- grad_exp_in: float32 [16, 768, 3072], P('expert', 'dp')
- grad_exp_out: float32 [16, 3072, 768], P('expert', None, 'dp')
- grad_gate: float32 [18912, 2], P(('dp', 'expert'))
The draws below stay inside these ranges and needn't reach their ends.
Inputs may be any that keep to these rules, and one draw needn't show every extreme that they name: `expert_index`: the 2 entries of a row differ. In each aligned block of 591 rows (the tokens of one device) no expert is named more than 96 times, a bound that some block reaches.
All inputs are finite; a program needn't handle non-finite values.
Results may differ from the reference program's by a relative error of at most 0.018.
The reference program's roundings to bfloat16 on the way count: a program that leaves them out, or rounds other values in their place, can miss the bound.
Values may be sent and summed in bfloat16 or wider, within the bound.
No kernel may reach another device: no remote copies, remote signals or barrier semaphores. Data moves between devices by JAX's collectives and lax.ppermute only.
A program may use at most 320 MiB of HBM per device.

```python
import math
import jax
import jax.numpy as jnp
import numpy as np
from jax import lax

D = 768
HEADS = 12
HEAD = 64
FF = 3072
SEQ = 197
TOP = 2
EXPERTS = 16
TOK_DEV = 591
IMAGES = 96
TOKENS = 18912
CAP = 96
N_DP = 4
N_EXPERT = 8


def strengthened(drawn, own_key, source, target, blocks, factor):
    owner, partner = [(jnp.arange(drawn.shape[dim]) // (drawn.shape[dim] // blocks)).reshape([-1 if axis == dim else 1 for axis in range(drawn.ndim)]) for dim in (source, target)]
    chosen = jax.random.permutation(own_key, blocks)[partner]
    strong = (owner == chosen) | (owner == (partner + blocks // 2) % blocks)
    return jnp.where(strong, factor * drawn, drawn)


def block_scale(key, extent, split, smallest, top_value):
    gain, own = 1.0, jax.random.fold_in(key, 6)
    for dim, shards_of in split:
        heights = jnp.exp(jax.random.uniform(jax.random.fold_in(own, dim), (shards_of,), jnp.float32, smallest / len(split), top_value / len(split)))
        gain = gain * jnp.repeat(heights, extent[dim] // shards_of).reshape([-1 if axis == dim else 1 for axis in range(len(extent))])
    return gain


def assign_block(key, own, number, rows, number_of, top, limit, lean):
    ranking = jax.random.permutation(key, number_of)
    crowded, common = portions_of(number_of, rows * top, limit, lean, True), portions_of(number_of, rows * top, limit, lean, False)
    places = jnp.arange(number_of)

    def named(lengths, offset_by):
        used = int((lengths > 0).sum())
        fixed = max(1, used // 4)
        passed = fixed + (places - fixed + offset_by * (used - fixed)) % max(1, number_of - fixed)
        return jnp.zeros((number_of,), jnp.int32).at[ranking[jnp.where(places < fixed, places, passed)]].set(jnp.asarray(lengths, jnp.int32))

    lengths = jnp.where(number % 4 == 0, named(crowded, number // 4), named(common, number - number // 4 - 1))
    mixed = jax.random.permutation(jax.random.fold_in(own, 3), number_of)
    donor, taker = mixed[0:number_of // 2 * 2:2], mixed[1:number_of // 2 * 2:2]
    margin = jnp.minimum(lengths[donor] - 1, limit - lengths[taker]) // 2
    margin = jnp.where((donor == ranking[0]) | (taker == ranking[0]) | (lengths[taker] == 0), 0, jnp.maximum(margin, 0))
    passed = jax.random.randint(jax.random.fold_in(own, 4), (number_of // 2,), 0, 1 << 20) % (margin + 1)
    lengths = lengths.at[donor].add(-passed).at[taker].add(passed)
    members = jnp.searchsorted(jnp.cumsum(lengths), jnp.arange(rows * top), side="right").astype(jnp.int32)
    listing = members.reshape(top, rows).T
    listing = listing[jax.random.permutation(jax.random.fold_in(own, 1), rows)]
    offset_by = jax.random.randint(jax.random.fold_in(own, 2), (rows, 1), 0, top)
    return jnp.take_along_axis(listing, (jnp.arange(top)[None, :] + offset_by) % top, axis=1)


def portions_of(number_of, total, limit, lean, full):
    loads = [(1 << 20) // math.isqrt(standing ** lean) + 1 for standing in range(1, number_of + 1)]
    largest = limit if full else min(limit, max(-(-total // number_of), total * loads[0] // sum(loads)))
    least = 1 if total - largest >= number_of - 1 else 0
    holding, rest = [largest] + [least] * (number_of - 1), total - largest - least * (number_of - 1)
    while rest > 0:
        candidates = [i for i in range(1, number_of) if holding[i] < largest] or [i for i in range(1, number_of) if holding[i] < limit]
        pool, budget = sum([loads[i] for i in candidates]), rest
        for i in candidates:
            addition = min(limit - holding[i], max(1, budget * loads[i] // pool), rest)
            holding[i] = holding[i] + addition
            rest = rest - addition
    return np.array(holding)


def scatter_about(key, dims, scale, reach, shards=(), kind=jnp.bfloat16):
    entries = scale * jax.random.normal(key, dims, jnp.float32)
    if shards:
        entries = entries * block_scale(key, dims, shards, -0.22, 0.18)
    return jnp.clip(entries, -reach, reach).astype(kind)


def heavy_noise(stream_key, extent, width, reach, split, heavy, kind=jnp.bfloat16):
    values = width * jax.random.normal(stream_key, extent, jnp.float32)
    if split:
        values = values * block_scale(stream_key, extent, split, -0.22, 0.18)
    return jnp.clip(strengthened(values, jax.random.fold_in(stream_key, 3), *heavy), -reach, reach).astype(kind)


def setup_inputs(seed: int = 0) -> dict:
    arg_keys = jax.random.split(jax.random.key(seed), 13)
    act_in = scatter_about(arg_keys[0], (TOKENS, D), 1.0, 6.0, ((0, 32),), jnp.float32)
    w_qkv = scatter_about(arg_keys[1], (2, D, 3 * D), D ** -0.5, 0.21875, ((1, 32),), jnp.float32)
    w_proj = scatter_about(arg_keys[2], (2, D, D), (D // 32) ** -0.5, 1.25, ((2, 32),), jnp.float32)
    w_up = scatter_about(arg_keys[3], (D, FF), D ** -0.5, 0.21875, ((0, 32),), jnp.float32)
    w_down = scatter_about(arg_keys[4], (FF, D), FF ** -0.5, 0.109375, ((1, 32),), jnp.float32)
    norm_gain = jnp.clip(1.0 + 0.18 * jax.random.normal(arg_keys[5], (4, D), jnp.float32), 0.1, 1.9)
    norm_shift = scatter_about(arg_keys[6], (4, D), 0.3, 3.0, ((1, 32),), jnp.float32)
    exp_in = scatter_about(arg_keys[7], (EXPERTS, D, FF), D ** -0.5, 0.21875, ((0, 8), (1, 4)), jnp.float32)
    exp_out = scatter_about(arg_keys[8], (EXPERTS, FF, D), FF ** -0.5, 0.109375, ((0, 8), (2, 4)), jnp.float32)
    gate = jnp.clip(jnp.exp(math.log(1.0) - 1.609438 * jax.random.uniform(arg_keys[9], (TOKENS, TOP), jnp.float32) ** block_scale(arg_keys[9], (TOKENS, TOP), ((0, 32),), -0.2, 0.2)), 0.2, 1.0)
    expert_index_keys = jax.random.split(jax.random.fold_in(arg_keys[10], 1), TOKENS // TOK_DEV)
    expert_index_turns = jax.random.permutation(jax.random.fold_in(arg_keys[10], 3), TOKENS // TOK_DEV)
    expert_index = jax.vmap(lambda own, number: assign_block(jax.random.fold_in(arg_keys[10], 2), own, number, TOK_DEV, EXPERTS, TOP, CAP, 1))(expert_index_keys, expert_index_turns).reshape((TOKENS, TOP))
    cotangent = heavy_noise(arg_keys[11], (TOKENS, D), 1.0, 6.0, ((0, 32),), (0, 1, 32, 2.75), jnp.float32)
    return {"act_in": act_in, "w_qkv": w_qkv, "w_proj": w_proj, "w_up": w_up, "w_down": w_down, "norm_gain": norm_gain, "norm_shift": norm_shift, "exp_in": exp_in, "exp_out": exp_out, "gate": gate, "expert_index": expert_index, "cotangent": cotangent}


@jax.custom_vjp
def low(v):
    return lax.optimization_barrier(v.astype(jnp.bfloat16)).astype(jnp.float32)

@jax.custom_vjp
def low_back(v):
    return v

def low_keep(v):
    return (low(v), None)

def low_pass(kept, grad):
    return (grad,)

def back_keep(v):
    return (v, None)

def back_low(kept, grad):
    return (low(grad),)
low.defvjp(low_keep, low_pass)
low_back.defvjp(back_keep, back_low)

def norm_rows(inputs, gain_row, shift_row):
    average = lax.optimization_barrier(jnp.mean(inputs, axis=-1, keepdims=True))
    centred = inputs - average
    spread = lax.optimization_barrier(jnp.mean(centred * centred, axis=-1, keepdims=True))
    return centred * lax.rsqrt(spread + 1e-06) * gain_row + shift_row

def product(left, right):
    return jnp.dot(left, right, precision=lax.Precision.HIGHEST, preferred_element_type=jnp.float32)

def attention_branch(normed, qkv_weight, proj_weight):
    score_scale = 1.0 / math.sqrt(HEAD)
    packed = low(low_back(product(low(normed), qkv_weight)))
    shaped = packed.reshape(IMAGES, SEQ, 3, HEADS, HEAD)
    scores = jnp.einsum('bqhd,bkhd->bhqk', shaped[:, :, 0], shaped[:, :, 1], precision=lax.Precision.HIGHEST) * score_scale
    attn_weights = low(jax.nn.softmax(low_back(scores), axis=-1))
    mixed_rows = jnp.einsum('bhqk,bkhd->bqhd', attn_weights, shaped[:, :, 2], precision=lax.Precision.HIGHEST)
    mixed_rows = low(low_back(mixed_rows.reshape(TOKENS, D)))
    return low_back(product(mixed_rows, proj_weight))

def dense_branch(normed, up_weight, down_weight):
    inner_rows = low_back(product(low(normed), up_weight))
    hidden_rows = low(jax.nn.gelu(inner_rows, approximate=False))
    return low_back(product(hidden_rows, down_weight))

def expert_apply(triple):
    rows_in, in_weight, out_weight = triple
    inner_rows = low_back(product(rows_in, in_weight))
    hidden_rows = low(jax.nn.gelu(inner_rows, approximate=False))
    return low(low_back(product(hidden_rows, out_weight)))

def slot_places(expert_index):
    blocks = N_DP * N_EXPERT
    flat_index = expert_index.reshape(blocks, TOK_DEV * TOP).astype(jnp.int32)
    onehot = (flat_index[:, :, None] == jnp.arange(EXPERTS, dtype=jnp.int32)[None, None, :]).astype(jnp.int32)
    before = jnp.cumsum(onehot, axis=1) - onehot
    slots = lax.optimization_barrier(jnp.sum(onehot * before, axis=2)).astype(jnp.int32)
    owner = jnp.arange(blocks, dtype=jnp.int32)[:, None]
    return ((owner * EXPERTS + flat_index) * CAP + slots).reshape(-1).astype(jnp.int32)

def reference(act_in, w_qkv, w_proj, w_up, w_down, norm_gain, norm_shift, exp_in, exp_out, gate, expert_index, cotangent):
    places = slot_places(expert_index)
    blocks = N_DP * N_EXPERT

    def forward(act_rows, qkv_master, proj_master, up_master, down_master, gain_master, shift_master, in_master, out_master, gate_master):
        qkv_low = low(qkv_master)
        proj_low = low(proj_master)
        up_low = low(up_master)
        down_low = low(down_master)
        gain_low = low(gain_master)
        shift_low = low(shift_master)
        in_low = low(in_master)
        out_low = low(out_master)
        stream = act_rows + attention_branch(norm_rows(act_rows, gain_low[0], shift_low[0]), qkv_low[0], proj_low[0])
        stream = stream + dense_branch(norm_rows(stream, gain_low[1], shift_low[1]), up_low, down_low)
        stream = stream + attention_branch(norm_rows(stream, gain_low[2], shift_low[2]), qkv_low[1], proj_low[1])
        sent_rows = low(norm_rows(stream, gain_low[3], shift_low[3]))
        repeated = jnp.repeat(sent_rows, TOP, axis=0)
        buffer_rows = jnp.zeros((blocks * EXPERTS * CAP, D), jnp.float32).at[places].set(repeated)
        buffer_rows = low_back(buffer_rows)
        grouped = buffer_rows.reshape(blocks, EXPERTS, CAP, D).transpose(1, 0, 2, 3).reshape(EXPERTS, blocks * CAP, D)
        results = lax.map(jax.checkpoint(expert_apply), (grouped, in_low, out_low))
        flat_back = results.reshape(EXPERTS, blocks, CAP, D).transpose(1, 0, 2, 3).reshape(blocks * EXPERTS * CAP, D)
        picked = flat_back[places].reshape(TOKENS, TOP, D)
        return stream + lax.optimization_barrier(jnp.sum(gate_master[:, :, None] * picked, axis=1))
    result, pull_back = jax.vjp(forward, act_in, w_qkv, w_proj, w_up, w_down, norm_gain, norm_shift, exp_in, exp_out, gate)
    grads = pull_back(cotangent)
    return (result, grads[0], grads[1], grads[2], grads[3], grads[4], grads[5], grads[6], grads[7], grads[8], grads[9])
```

```python
import math

import jax
import jax.numpy as jnp
from jax import lax
from jax.sharding import Mesh, PartitionSpec as P

D = 768
FF = 3072
HEADS = 12
HEAD = 64
SEQ = 197
TOP = 2
EXP_DEV = 2
TOK_DEV = 591
DP_AXES = ("dh", "dl")
ALL_AXES = ("dh", "dl", "expert")
TOKEN_AXES = ("dl", "expert")


def norm_rows(inputs, gain_row, shift_row):
    average = jnp.mean(inputs, axis=-1, keepdims=True)
    centred = inputs - average
    spread = jnp.mean(centred * centred, axis=-1, keepdims=True)
    return centred * lax.rsqrt(spread + 1e-06) * gain_row + shift_row


def gelu_exact(inputs):
    return jax.nn.gelu(inputs, approximate=False)


def gelu_grad(inputs, upstream):
    _, pull_back = jax.vjp(gelu_exact, inputs)
    return pull_back(upstream)[0]


def norm_grad(inputs, gain_row, shift_row, upstream):
    _, pull_back = jax.vjp(norm_rows, inputs, gain_row, shift_row)
    return pull_back(upstream)


def matmul_low(left, right):
    return jnp.dot(left, right, preferred_element_type=jnp.float32)


def gather_rows(part):
    return lax.all_gather(part, ALL_AXES, axis=0, tiled=True)


def scatter_rows(full):
    return lax.psum_scatter(
        full.astype(jnp.bfloat16), ALL_AXES, scatter_dimension=0, tiled=True
    ).astype(jnp.float32)


def split_heads(packed_rows):
    images = packed_rows.shape[0] // SEQ
    shaped = packed_rows.reshape(images, SEQ, 3, HEADS, HEAD)
    return (shaped[:, :, 0], shaped[:, :, 1], shaped[:, :, 2])


def attend_forward(normed_low, qkv_weight, proj_weight):
    score_scale = 1.0 / math.sqrt(HEAD)
    packed = matmul_low(normed_low, qkv_weight).astype(jnp.bfloat16)
    query_rows, key_rows, value_rows = split_heads(packed)
    scores = (
        jnp.einsum("bqhd,bkhd->bhqk", query_rows, key_rows, preferred_element_type=jnp.float32)
        * score_scale
    )
    row_peak = jnp.max(scores, axis=-1, keepdims=True)
    raised = jnp.exp(scores - row_peak)
    row_total = jnp.sum(raised, axis=-1, keepdims=True)
    attn_weights = raised / row_total
    log_total = row_peak + jnp.log(row_total)
    mixed_rows = jnp.einsum(
        "bhqk,bkhd->bqhd",
        attn_weights.astype(jnp.bfloat16),
        value_rows,
        preferred_element_type=jnp.float32,
    )
    mixed_rows = mixed_rows.astype(jnp.bfloat16).reshape(packed.shape[0], D)
    branch = matmul_low(mixed_rows, proj_weight)
    return (branch, (packed, log_total, mixed_rows))


def attend_backward(grad_branch, normed_low, qkv_weight, proj_weight, saved):
    score_scale = 1.0 / math.sqrt(HEAD)
    packed, log_total, mixed_rows = saved
    row_count = packed.shape[0]
    grad_low = grad_branch.astype(jnp.bfloat16)
    grad_proj = jnp.einsum("td,te->de", mixed_rows, grad_low, preferred_element_type=jnp.float32)
    grad_mixed = jnp.einsum("te,de->td", grad_low, proj_weight, preferred_element_type=jnp.float32)
    grad_mixed = grad_mixed.astype(jnp.bfloat16).reshape(row_count // SEQ, SEQ, HEADS, HEAD)
    query_rows, key_rows, value_rows = split_heads(packed)
    scores = (
        jnp.einsum("bqhd,bkhd->bhqk", query_rows, key_rows, preferred_element_type=jnp.float32)
        * score_scale
    )
    attn_weights = jnp.exp(scores - log_total)
    grad_weights = jnp.einsum(
        "bqhd,bkhd->bhqk", grad_mixed, value_rows, preferred_element_type=jnp.float32
    )
    grad_values = jnp.einsum(
        "bhqk,bqhd->bkhd",
        attn_weights.astype(jnp.bfloat16),
        grad_mixed,
        preferred_element_type=jnp.float32,
    )
    grad_scores = attn_weights * (
        grad_weights - jnp.sum(attn_weights * grad_weights, axis=-1, keepdims=True)
    )
    grad_scores = grad_scores.astype(jnp.bfloat16)
    grad_query = (
        jnp.einsum("bhqk,bkhd->bqhd", grad_scores, key_rows, preferred_element_type=jnp.float32)
        * score_scale
    )
    grad_keys = (
        jnp.einsum("bhqk,bqhd->bkhd", grad_scores, query_rows, preferred_element_type=jnp.float32)
        * score_scale
    )
    grad_packed = (
        jnp.stack([grad_query, grad_keys, grad_values], axis=2)
        .reshape(row_count, 3 * D)
        .astype(jnp.bfloat16)
    )
    grad_qkv = jnp.einsum("td,tf->df", normed_low, grad_packed, preferred_element_type=jnp.float32)
    grad_normed = jnp.einsum(
        "tf,df->td", grad_packed, qkv_weight, preferred_element_type=jnp.float32
    )
    return (grad_normed, grad_qkv, grad_proj)


def local(
    act_in,
    w_qkv,
    w_proj,
    w_up,
    w_down,
    norm_gain,
    norm_shift,
    exp_in,
    exp_out,
    gate,
    expert_index,
    cotangent,
):
    row_count = act_in.shape[0]
    groups = lax.axis_size("expert")
    experts_all = EXP_DEV * groups
    n_dp = lax.axis_size(DP_AXES)
    capacity = (TOP * TOK_DEV * 5 // (4 * experts_all) + 7) // 8 * 8
    low = jnp.bfloat16
    rows = w_up.shape[0]
    proj_t = jnp.swapaxes(w_proj, 1, 2).astype(low)
    qkv_low = w_qkv.astype(low)
    norms = jnp.concatenate([norm_gain.T, norm_shift.T], axis=1).astype(low)
    norms = jnp.pad(norms, ((0, 0), (0, 128 - norms.shape[1])))
    first = gather_rows(jnp.concatenate([qkv_low[0], proj_t[0], norms], axis=1))
    second = gather_rows(
        jnp.concatenate(
            [w_up.astype(low), w_down.T.astype(low), qkv_low[1], proj_t[1]], axis=1
        )
    )
    qkv_all = (first[:, : 3 * D], second[:, 2 * FF : 2 * FF + 3 * D])
    proj_all = (first[:, 3 * D : 4 * D].T, second[:, 2 * FF + 3 * D :].T)
    up_all, down_all = second[:, :FF], second[:, FF : 2 * FF].T
    norm_all = first[:, 4 * D : 4 * D + 8].astype(jnp.float32).T
    gain_full, shift_full = norm_all[:4], norm_all[4:]

    def fetch_expert(part):
        copies = jnp.tile(part.astype(low), (n_dp // EXP_DEV, 1, 1))
        return lax.all_to_all(copies, DP_AXES, 0, 0, tiled=True).reshape(D, FF)

    exp_in_all = fetch_expert(exp_in)
    exp_out_all = fetch_expert(jnp.swapaxes(exp_out, 1, 2)).T
    normed_a = norm_rows(act_in, gain_full[0], shift_full[0]).astype(jnp.bfloat16)
    branch_a, saved_a = attend_forward(normed_a, qkv_all[0], proj_all[0])
    after_a = act_in + branch_a
    normed_b = norm_rows(after_a, gain_full[1], shift_full[1]).astype(jnp.bfloat16)
    inner_rows = matmul_low(normed_b, up_all)
    hidden_low = gelu_exact(inner_rows).astype(jnp.bfloat16)
    after_b = after_a + matmul_low(hidden_low, down_all)
    normed_c = norm_rows(after_b, gain_full[2], shift_full[2]).astype(jnp.bfloat16)
    branch_c, saved_c = attend_forward(normed_c, qkv_all[1], proj_all[1])
    after_c = after_b + branch_c
    sent_low = norm_rows(after_c, gain_full[3], shift_full[3]).astype(jnp.bfloat16)
    flat_index = expert_index.reshape(-1)
    onehot = (flat_index[:, None] == jnp.arange(experts_all, dtype=jnp.int32)[None, :]).astype(
        jnp.int32
    )
    before = jnp.cumsum(onehot, axis=0) - onehot
    holder = (flat_index % EXP_DEV) * groups + flat_index // EXP_DEV
    places = holder * capacity + jnp.sum(onehot * before, axis=1)
    repeated = jnp.repeat(sent_low, TOP, axis=0)
    send_buffer = (
        jnp.zeros((experts_all * capacity, D), jnp.bfloat16)
        .at[places]
        .set(repeated)
        .reshape(experts_all, capacity, D)
    )
    arrived = lax.all_to_all(send_buffer, TOKEN_AXES, 0, 0, tiled=True).reshape(-1, D)
    expert_inner = jnp.einsum(
        "rd,df->rf", arrived, exp_in_all, preferred_element_type=jnp.float32
    )
    expert_hidden = gelu_exact(expert_inner).astype(jnp.bfloat16)
    expert_result = jnp.einsum(
        "rf,fd->rd", expert_hidden, exp_out_all, preferred_element_type=jnp.float32
    ).astype(jnp.bfloat16)
    returned = lax.all_to_all(
        expert_result.reshape(experts_all, capacity, D), TOKEN_AXES, 0, 0, tiled=True
    )
    picked = returned.reshape(-1, D)[places].astype(jnp.float32).reshape(row_count, TOP, D)
    act_out = after_c + jnp.sum(gate[:, :, None] * picked, axis=1)
    grad_gate = jnp.sum(cotangent[:, None, :] * picked, axis=2)
    grad_slots = (
        (gate[:, :, None] * cotangent[:, None, :]).astype(jnp.bfloat16).reshape(row_count * TOP, D)
    )
    grad_buffer = (
        jnp.zeros((experts_all * capacity, D), jnp.bfloat16)
        .at[places]
        .set(grad_slots)
        .reshape(experts_all, capacity, D)
    )
    grad_arrived = lax.all_to_all(grad_buffer, TOKEN_AXES, 0, 0, tiled=True).reshape(-1, D)
    local_exp_out = jnp.einsum(
        "rf,rd->fd", expert_hidden, grad_arrived, preferred_element_type=jnp.float32
    )
    grad_hidden = jnp.einsum(
        "rd,fd->rf", grad_arrived, exp_out_all, preferred_element_type=jnp.float32
    )
    grad_inner = gelu_grad(expert_inner, grad_hidden).astype(jnp.bfloat16)
    local_exp_in = jnp.einsum(
        "rd,rf->df", arrived, grad_inner, preferred_element_type=jnp.float32
    )
    grad_routed = jnp.einsum(
        "rf,df->rd", grad_inner, exp_in_all, preferred_element_type=jnp.float32
    ).astype(jnp.bfloat16)
    grad_home = lax.all_to_all(
        grad_routed.reshape(experts_all, capacity, D), TOKEN_AXES, 0, 0, tiled=True
    )
    grad_sent = jnp.sum(
        grad_home.reshape(-1, D)[places].astype(jnp.float32).reshape(row_count, TOP, D), axis=1
    )
    def share_expert(partial):
        pieces = partial.astype(low).reshape(n_dp, D // n_dp, FF)
        pieces = lax.all_to_all(pieces, DP_AXES, 0, 0, tiled=True)
        pieces = pieces.reshape(n_dp // EXP_DEV, EXP_DEV, D // n_dp, FF)
        return jnp.sum(pieces.astype(jnp.float32), axis=0)

    grad_exp_out = jnp.swapaxes(share_expert(local_exp_out.T), 1, 2)
    grad_exp_in = share_expert(local_exp_in)
    grad_after_c, gain_d, shift_d = norm_grad(after_c, gain_full[3], shift_full[3], grad_sent)
    grad_after_c = cotangent + grad_after_c
    grad_normed_c, qkv_grad_c, proj_grad_c = attend_backward(
        grad_after_c, normed_c, qkv_all[1], proj_all[1], saved_c
    )
    through_c, gain_c, shift_c = norm_grad(after_b, gain_full[2], shift_full[2], grad_normed_c)
    grad_after_b = grad_after_c + through_c
    grad_mlp = grad_after_b.astype(jnp.bfloat16)
    down_grad = jnp.einsum("tf,td->fd", hidden_low, grad_mlp, preferred_element_type=jnp.float32)
    grad_hidden_b = jnp.einsum("td,fd->tf", grad_mlp, down_all, preferred_element_type=jnp.float32)
    grad_inner_b = gelu_grad(inner_rows, grad_hidden_b).astype(jnp.bfloat16)
    up_grad = jnp.einsum("td,tf->df", normed_b, grad_inner_b, preferred_element_type=jnp.float32)
    grad_normed_b = jnp.einsum(
        "tf,df->td", grad_inner_b, up_all, preferred_element_type=jnp.float32
    )
    through_b, gain_b, shift_b = norm_grad(after_a, gain_full[1], shift_full[1], grad_normed_b)
    grad_after_a = grad_after_b + through_b
    grad_normed_a, qkv_grad_a, proj_grad_a = attend_backward(
        grad_after_a, normed_a, qkv_all[0], proj_all[0], saved_a
    )
    through_a, gain_a, shift_a = norm_grad(act_in, gain_full[0], shift_full[0], grad_normed_a)
    act_grad = grad_after_a + through_a
    late = scatter_rows(
        jnp.concatenate([up_grad, down_grad.T, qkv_grad_c, proj_grad_c.T], axis=1)
    )
    norm_grads = jnp.concatenate(
        [
            jnp.stack([gain_a, gain_b, gain_c, gain_d], axis=1),
            jnp.stack([shift_a, shift_b, shift_c, shift_d], axis=1),
            jnp.zeros((D, 120), jnp.float32),
        ],
        axis=1,
    )
    last = scatter_rows(jnp.concatenate([qkv_grad_a, proj_grad_a.T, norm_grads], axis=1))
    grad_qkv = jnp.stack([last[:, : 3 * D], late[:, 2 * FF : 2 * FF + 3 * D]])
    grad_proj = jnp.swapaxes(
        jnp.stack([last[:, 3 * D : 4 * D], late[:, 2 * FF + 3 * D :]]), 1, 2
    )
    return (
        act_out,
        act_grad,
        grad_qkv,
        grad_proj,
        late[:, :FF],
        late[:, FF : 2 * FF].T,
        last[:, 4 * D : 4 * D + 4].T,
        last[:, 4 * D + 4 : 4 * D + 8].T,
        grad_exp_in,
        grad_exp_out,
        grad_gate,
    )


def solution(mesh):
    n_dp, n_expert = mesh.devices.shape
    mesh = Mesh(mesh.devices.reshape(n_dp // EXP_DEV, EXP_DEV, n_expert), ALL_AXES)
    in_specs = (
        P(ALL_AXES, None),
        P(None, ALL_AXES, None),
        P(None, None, ALL_AXES),
        P(ALL_AXES, None),
        P(None, ALL_AXES),
        P(None, ALL_AXES),
        P(None, ALL_AXES),
        P("expert", DP_AXES, None),
        P("expert", None, DP_AXES),
        P(ALL_AXES, None),
        P(ALL_AXES, None),
        P(ALL_AXES, None),
    )
    out_specs = (
        P(ALL_AXES, None),
        P(ALL_AXES, None),
        P(None, ALL_AXES, None),
        P(None, None, ALL_AXES),
        P(ALL_AXES, None),
        P(None, ALL_AXES),
        P(None, ALL_AXES),
        P(None, ALL_AXES),
        P("expert", DP_AXES, None),
        P("expert", None, DP_AXES),
        P(ALL_AXES, None),
    )
    return jax.shard_map(local, mesh=mesh, in_specs=in_specs, out_specs=out_specs, check_vma=False)
```

```python
import functools
import math

import jax
import jax.numpy as jnp
from jax import lax
from jax.experimental import pallas as pl
from jax.experimental.pallas import tpu as pltpu
from jax.sharding import Mesh, PartitionSpec as P

D = 768
FF = 3072
HEADS = 12
HEAD = 64
SEQ = 197
LINES = 208
TOP = 2
EXP_DEV = 2
TOK_DEV = 591
EPS = 1e-06
LOW = jnp.bfloat16
WIDE = jnp.float32
SCALE = 1.0 / math.sqrt(HEAD)
RSQRT2 = 1.0 / math.sqrt(2.0)
RSQRT2PI = 1.0 / math.sqrt(2.0 * math.pi)
SLOT_TILE = 256
ROW_TILE = 256
HINT = 4


def mm(left, right):
    return jnp.dot(left, right, preferred_element_type=WIDE)


def mm_t(left, right):
    return lax.dot_general(left, right, (((1,), (1,)), ((), ())), preferred_element_type=WIDE)


def t_mm(left, right):
    return lax.dot_general(left, right, (((0,), (0,)), ((), ())), preferred_element_type=WIDE)


def norm_parts(inputs):
    average = jnp.mean(inputs, axis=-1, keepdims=True)
    centred = inputs - average
    spread = jnp.mean(centred * centred, axis=-1, keepdims=True)
    inverse = lax.rsqrt(spread + EPS)
    return centred * inverse, inverse


def norm_low(inputs, gain_ref, shift_ref):
    xhat, _ = norm_parts(inputs)
    return (xhat * gain_ref[...] + shift_ref[...]).astype(LOW)


def norm_backward(dnormed, xhat, inverse, gain_ref, residual, dx_ref, dgain_ref, dshift_ref):
    scaled = dnormed * gain_ref[...]
    mean = jnp.mean(scaled, axis=-1, keepdims=True)
    tilt = jnp.mean(scaled * xhat, axis=-1, keepdims=True)
    dx_ref[0] = residual + inverse * (scaled - mean - xhat * tilt)

    @pl.when(pl.program_id(0) == 0)
    def _():
        dgain_ref[...] = jnp.zeros_like(dgain_ref)
        dshift_ref[...] = jnp.zeros_like(dshift_ref)

    dgain_ref[...] += jnp.sum(dnormed * xhat, axis=0, keepdims=True)
    dshift_ref[...] += jnp.sum(dnormed, axis=0, keepdims=True)


def gelu_both(inner):
    phi = 0.5 + 0.5 * lax.erf(inner * RSQRT2)
    slope = phi + inner * (RSQRT2PI * jnp.exp(-0.5 * inner * inner))
    return (inner * phi).astype(LOW), slope.astype(LOW)


def softmax_rows(query, key):
    scores = mm_t(query, key) * SCALE
    lane = lax.broadcasted_iota(jnp.int32, scores.shape, 1)
    scores = jnp.where(lane < SEQ, scores, -jnp.inf)
    peak = jnp.max(scores, axis=-1, keepdims=True)
    raised = jnp.exp(scores - peak)
    total = jnp.sum(raised, axis=-1, keepdims=True)
    return raised * (1.0 / total)


def whole(shape):
    return pl.BlockSpec(shape, lambda *_: (0,) * len(shape))


def window(width, at):
    return pl.BlockSpec((D, width), lambda *_: (0, at))


def image(width):
    return pl.BlockSpec((1, LINES, width), lambda i: (i, 0, 0))


def params(megabytes):
    return pltpu.CompilerParams(vmem_limit_bytes=megabytes << 20)


def like(shape, kind):
    return jax.ShapeDtypeStruct(shape, kind)


def cost(flops, moved, raised=0):
    return pl.CostEstimate(
        flops=flops // HINT, bytes_accessed=moved // HINT, transcendentals=raised // HINT
    )


def attend_forward_body(x_ref, gain_ref, shift_ref, qkv_ref, proj_ref, out_ref, packed_ref, mixed_ref):
    x = x_ref[0]
    packed_ref[0] = mm(norm_low(x, gain_ref, shift_ref), qkv_ref[...]).astype(LOW)
    first = lax.broadcasted_iota(jnp.int32, (LINES, 2 * HEAD), 1) < HEAD
    zero = jnp.zeros((LINES, 2 * HEAD), LOW)
    for pair in range(HEADS // 2):
        at = pair * 2 * HEAD
        query = packed_ref[0, :, at : at + 2 * HEAD]
        key = packed_ref[0, :, D + at : D + at + 2 * HEAD]
        value = packed_ref[0, :, 2 * D + at : 2 * D + at + 2 * HEAD]
        low = mm(softmax_rows(jnp.where(first, query, zero), key).astype(LOW), value)
        high = mm(softmax_rows(jnp.where(first, zero, query), key).astype(LOW), value)
        mixed_ref[0, :, at : at + 2 * HEAD] = jnp.where(first, low, high).astype(LOW)
    out_ref[0] = x + mm_t(mixed_ref[0], proj_ref[...])


def attend_forward(x, gain, shift, block):
    images = x.shape[0]
    return pl.pallas_call(
        attend_forward_body,
        grid=(images,),
        in_specs=[image(D), whole((1, D)), whole((1, D)), window(3 * D, 0), window(D, 3)],
        out_specs=[image(D), image(3 * D), image(D)],
        out_shape=[
            like((images, LINES, D), WIDE),
            like((images, LINES, 3 * D), LOW),
            like((images, LINES, D), LOW),
        ],
        compiler_params=params(48),
        cost_estimate=cost(3_700_000_000, 13_000_000, 1_600_000),
        name="attend_forward",
    )(x, gain, shift, block, block)


def attend_backward_body(
    x_ref, dy_ref, packed_ref, gain_ref, shift_ref, qkv_ref, proj_ref,
    dx_ref, dpacked_ref, normed_ref, low_ref, dgain_ref, dshift_ref,
    dmixed_ref,
):
    dy = dy_ref[0]
    grad_low = dy.astype(LOW)
    low_ref[0] = grad_low
    dmixed_ref[...] = mm(grad_low, proj_ref[...]).astype(LOW)
    first = lax.broadcasted_iota(jnp.int32, (LINES, 2 * HEAD), 1) < HEAD
    zero = jnp.zeros((LINES, 2 * HEAD), LOW)

    def one(query, key, value, upstream):
        probs = softmax_rows(query, key)
        dprobs = mm_t(upstream, value)
        inner = jnp.sum(probs * dprobs, axis=-1, keepdims=True)
        dscores = (probs * (dprobs - inner)).astype(LOW)
        return t_mm(probs.astype(LOW), upstream), mm(dscores, key), t_mm(dscores, query)

    for pair in range(HEADS // 2):
        at = pair * 2 * HEAD
        query = packed_ref[0, :, at : at + 2 * HEAD]
        key = packed_ref[0, :, D + at : D + at + 2 * HEAD]
        value = packed_ref[0, :, 2 * D + at : 2 * D + at + 2 * HEAD]
        upstream = dmixed_ref[:, at : at + 2 * HEAD]
        dv0, dq0, dk0 = one(
            jnp.where(first, query, zero), key, value, jnp.where(first, upstream, zero)
        )
        dv1, dq1, dk1 = one(
            jnp.where(first, zero, query), key, value, jnp.where(first, zero, upstream)
        )
        dpacked_ref[0, :, at : at + 2 * HEAD] = (jnp.where(first, dq0, dq1) * SCALE).astype(LOW)
        dpacked_ref[0, :, D + at : D + at + 2 * HEAD] = ((dk0 + dk1) * SCALE).astype(LOW)
        dpacked_ref[0, :, 2 * D + at : 2 * D + at + 2 * HEAD] = (dv0 + dv1).astype(LOW)
    xhat, inverse = norm_parts(x_ref[0])
    normed_ref[0] = (xhat * gain_ref[...] + shift_ref[...]).astype(LOW)
    dnormed = mm_t(dpacked_ref[0], qkv_ref[...])
    norm_backward(dnormed, xhat, inverse, gain_ref, dy, dx_ref, dgain_ref, dshift_ref)


def attend_backward(x, dy, packed, gain, shift, block):
    images = x.shape[0]
    return pl.pallas_call(
        attend_backward_body,
        grid=(images,),
        in_specs=[
            image(D), image(D), image(3 * D), whole((1, D)), whole((1, D)),
            window(3 * D, 0), window(D, 3),
        ],
        out_specs=[image(D), image(3 * D), image(D), image(D), whole((1, D)), whole((1, D))],
        out_shape=[
            like((images, LINES, D), WIDE),
            like((images, LINES, 3 * D), LOW),
            like((images, LINES, D), LOW),
            like((images, LINES, D), LOW),
            like((1, D), WIDE),
            like((1, D), WIDE),
        ],
        scratch_shapes=[pltpu.VMEM((LINES, D), LOW)],
        compiler_params=params(48),
        cost_estimate=cost(4_000_000_000, 22_000_000, 1_600_000),
        name="attend_backward",
    )(x, dy, packed, gain, shift, block, block)


def mlp_forward_body(x_ref, gain_ref, shift_ref, up_ref, down_ref, out_ref, hidden_ref, slope_ref):
    x = x_ref[0]
    normed = norm_low(x, gain_ref, shift_ref)
    total = x
    step = FF // 4
    for at in range(0, FF, step):
        hidden, slope = gelu_both(mm(normed, up_ref[:, at : at + step]))
        hidden_ref[0, :, at : at + step] = hidden
        slope_ref[0, :, at : at + step] = slope
        total = total + mm_t(hidden, down_ref[:, at : at + step])
    out_ref[0] = total


def mlp_forward(x, gain, shift, block):
    images = x.shape[0]
    return pl.pallas_call(
        mlp_forward_body,
        grid=(images,),
        in_specs=[image(D), whole((1, D)), whole((1, D)), window(FF, 0), window(FF, 1)],
        out_specs=[image(D), image(FF), image(FF)],
        out_shape=[
            like((images, LINES, D), WIDE),
            like((images, LINES, FF), LOW),
            like((images, LINES, FF), LOW),
        ],
        compiler_params=params(56),
        cost_estimate=cost(5_900_000_000, 21_000_000, 4_000_000),
        name="mlp_forward",
    )(x, gain, shift, block, block)


def mlp_backward_body(
    x_ref, dy_ref, slope_ref, gain_ref, shift_ref, up_ref, down_ref,
    dx_ref, dinner_ref, normed_ref, low_ref, dgain_ref, dshift_ref,
):
    dy = dy_ref[0]
    grad_low = dy.astype(LOW)
    low_ref[0] = grad_low
    step = FF // 4
    dnormed = jnp.zeros((LINES, D), WIDE)
    for at in range(0, FF, step):
        dhidden = mm(grad_low, down_ref[:, at : at + step])
        dinner = (dhidden * slope_ref[0, :, at : at + step].astype(WIDE)).astype(LOW)
        dinner_ref[0, :, at : at + step] = dinner
        dnormed = dnormed + mm_t(dinner, up_ref[:, at : at + step])
    xhat, inverse = norm_parts(x_ref[0])
    normed_ref[0] = (xhat * gain_ref[...] + shift_ref[...]).astype(LOW)
    norm_backward(dnormed, xhat, inverse, gain_ref, dy, dx_ref, dgain_ref, dshift_ref)


def mlp_backward(x, dy, slope, gain, shift, block):
    images = x.shape[0]
    return pl.pallas_call(
        mlp_backward_body,
        grid=(images,),
        in_specs=[
            image(D), image(D), image(FF), whole((1, D)), whole((1, D)),
            window(FF, 0), window(FF, 1),
        ],
        out_specs=[image(D), image(FF), image(D), image(D), whole((1, D)), whole((1, D))],
        out_shape=[
            like((images, LINES, D), WIDE),
            like((images, LINES, FF), LOW),
            like((images, LINES, D), LOW),
            like((images, LINES, D), LOW),
            like((1, D), WIDE),
            like((1, D), WIDE),
        ],
        compiler_params=params(56),
        cost_estimate=cost(5_900_000_000, 25_000_000),
        name="mlp_backward",
    )(x, dy, slope, gain, shift, block, block)


def chosen(places_ref, tile):
    tokens = places_ref.shape[1]
    slot = pl.program_id(0) * tile + lax.broadcasted_iota(jnp.int32, (tile, tokens), 0)
    return [jnp.where(slot == places_ref[k : k + 1, :], 1.0, 0.0) for k in range(TOP)]


def dispatch_body(places_ref, x_ref, gain_ref, shift_ref, out_ref, sent_ref):
    @pl.when(pl.program_id(0) == 0)
    def _():
        sent_ref[...] = norm_low(x_ref[...], gain_ref, shift_ref)

    picks = chosen(places_ref, SLOT_TILE)
    out_ref[...] = mm((picks[0] + picks[1]).astype(LOW), sent_ref[...]).astype(LOW)


def dispatch(places, x, gain, shift, slots):
    tokens = x.shape[0]
    return pl.pallas_call(
        dispatch_body,
        grid=(slots // SLOT_TILE,),
        in_specs=[whole((TOP, tokens)), whole((tokens, D)), whole((1, D)), whole((1, D))],
        out_specs=pl.BlockSpec((SLOT_TILE, D), lambda i: (i, 0)),
        out_shape=like((slots, D), LOW),
        scratch_shapes=[pltpu.VMEM((tokens, D), LOW)],
        compiler_params=params(32),
        cost_estimate=cost(1_500_000_000, 4_500_000),
        name="dispatch",
    )(places, x, gain, shift)


def dispatch_grad_body(places_ref, gate_ref, cot_ref, out_ref, sent_ref):
    @pl.when(pl.program_id(0) == 0)
    def _():
        for k in range(TOP):
            sent_ref[k] = (gate_ref[:, k : k + 1] * cot_ref[...]).astype(LOW)

    picks = chosen(places_ref, SLOT_TILE)
    total = mm(picks[0].astype(LOW), sent_ref[0]) + mm(picks[1].astype(LOW), sent_ref[1])
    out_ref[...] = total.astype(LOW)


def dispatch_grad(places, gate, cot, slots):
    tokens = cot.shape[0]
    return pl.pallas_call(
        dispatch_grad_body,
        grid=(slots // SLOT_TILE,),
        in_specs=[whole((TOP, tokens)), whole((tokens, TOP)), whole((tokens, D))],
        out_specs=pl.BlockSpec((SLOT_TILE, D), lambda i: (i, 0)),
        out_shape=like((slots, D), LOW),
        scratch_shapes=[pltpu.VMEM((TOP, tokens, D), LOW)],
        compiler_params=params(32),
        cost_estimate=cost(3_000_000_000, 4_500_000),
        name="dispatch_grad",
    )(places, gate, cot)


def picker(places_ref, k, slots):
    lane = lax.broadcasted_iota(jnp.int32, (LINES, slots), 1)
    return jnp.where(lane == places_ref[0, :, k : k + 1], 1.0, 0.0)


def combine_body(places_ref, gate_ref, x_ref, cot_ref, home_ref, out_ref, dgate_ref):
    slots = home_ref.shape[0]
    total = x_ref[0]
    for k in range(TOP):
        picked = mm(picker(places_ref, k, slots).astype(LOW), home_ref[...])
        total = total + gate_ref[0, :, k : k + 1] * picked
        dgate_ref[0, :, k : k + 1] = jnp.sum(cot_ref[0] * picked, axis=-1, keepdims=True)
    out_ref[0] = total


def combine(places, gate, x, cot, home):
    images, slots = x.shape[0], home.shape[0]
    return pl.pallas_call(
        combine_body,
        grid=(images,),
        in_specs=[image(TOP), image(TOP), image(D), image(D), whole((slots, D))],
        out_specs=[image(D), image(TOP)],
        out_shape=[like((images, LINES, D), WIDE), like((images, LINES, TOP), WIDE)],
        compiler_params=params(32),
        cost_estimate=cost(3_000_000_000, 8_000_000),
        name="combine",
    )(places, gate, x, cot, home)


def return_grad_body(places_ref, x_ref, cot_ref, gain_ref, home_ref, dx_ref, dgain_ref, dshift_ref):
    slots = home_ref.shape[0]
    picks = (picker(places_ref, 0, slots) + picker(places_ref, 1, slots)).astype(LOW)
    dsent = mm(picks, home_ref[...])
    xhat, inverse = norm_parts(x_ref[0])
    norm_backward(dsent, xhat, inverse, gain_ref, cot_ref[0], dx_ref, dgain_ref, dshift_ref)


def return_grad(places, x, cot, gain, home):
    images, slots = x.shape[0], home.shape[0]
    return pl.pallas_call(
        return_grad_body,
        grid=(images,),
        in_specs=[image(TOP), image(D), image(D), whole((1, D)), whole((slots, D))],
        out_specs=[image(D), whole((1, D)), whole((1, D))],
        out_shape=[like((images, LINES, D), WIDE), like((1, D), WIDE), like((1, D), WIDE)],
        compiler_params=params(32),
        cost_estimate=cost(1_500_000_000, 8_000_000),
        name="return_grad",
    )(places, x, cot, gain, home)


def expert_forward_body(rows_ref, in_ref, hidden_ref, slope_ref):
    step = FF // 4
    for at in range(0, FF, step):
        hidden, slope = gelu_both(mm(rows_ref[...], in_ref[:, at : at + step]))
        hidden_ref[:, at : at + step] = hidden
        slope_ref[:, at : at + step] = slope


def tiled(width):
    return pl.BlockSpec((ROW_TILE, width), lambda i: (i, 0))


def expert_forward(rows, weight):
    count = rows.shape[0]
    return pl.pallas_call(
        expert_forward_body,
        grid=(count // ROW_TILE,),
        in_specs=[tiled(D), whole((D, FF))],
        out_specs=[tiled(FF), tiled(FF)],
        out_shape=[like((count, FF), LOW), like((count, FF), LOW)],
        compiler_params=params(48),
        cost_estimate=cost(7_200_000_000, 26_000_000, 9_000_000),
        name="expert_forward",
    )(rows, weight)


def expert_backward_body(grad_ref, slope_ref, in_ref, out_ref, dinner_ref, dx_ref):
    step = FF // 4
    total = jnp.zeros((ROW_TILE, D), WIDE)
    for at in range(0, FF, step):
        dhidden = mm(grad_ref[...], out_ref[:, at : at + step])
        dinner = (dhidden * slope_ref[:, at : at + step].astype(WIDE)).astype(LOW)
        dinner_ref[:, at : at + step] = dinner
        total = total + mm_t(dinner, in_ref[:, at : at + step])
    dx_ref[...] = total.astype(LOW)


def expert_backward(grad, slope, weight_in, weight_out_t):
    count = grad.shape[0]
    return pl.pallas_call(
        expert_backward_body,
        grid=(count // ROW_TILE,),
        in_specs=[tiled(D), tiled(FF), whole((D, FF)), whole((D, FF))],
        out_specs=[tiled(FF), tiled(D)],
        out_shape=[like((count, FF), LOW), like((count, D), LOW)],
        compiler_params=params(48),
        cost_estimate=cost(14_400_000_000, 33_000_000),
        name="expert_backward",
    )(grad, slope, weight_in, weight_out_t)


def join_body(at_ref, *refs):
    *parts, out_ref, sem = refs
    for index, part in enumerate(parts):
        rows, width = part.shape[1:]
        for block in range(part.shape[0]):
            down = pl.multiple_of(at_ref[index, 2 * block] * 16, 16)
            right = pl.multiple_of(at_ref[index, 2 * block + 1] * 128, 128)
            target = out_ref.at[pl.ds(down, rows), pl.ds(right, width)]
            pltpu.make_async_copy(part.at[block], target, sem).start()
    pltpu.make_async_copy(out_ref, out_ref, sem).wait()


def join(places, parts, width):
    return pl.pallas_call(
        join_body,
        in_specs=[pl.BlockSpec(memory_space=pltpu.SMEM)]
        + [pl.BlockSpec(memory_space=pl.ANY)] * len(parts),
        out_specs=pl.BlockSpec(memory_space=pltpu.VMEM),
        out_shape=like((D, width), LOW),
        scratch_shapes=[pltpu.SemaphoreType.DMA],
        compiler_params=params(32),
        cost_estimate=cost(0, 4 * D * width),
        name="join",
    )(places, *parts)


def flipped(index, first, second, axis):
    return jnp.where(
        index == 0,
        jnp.concatenate([first, second], axis=axis),
        jnp.concatenate([second, first], axis=axis),
    )


class Plan:
    def __init__(self, mesh):
        n_dp, n_expert = mesh.devices.shape
        self.n_dp, self.groups = n_dp, n_expert
        self.wide = (n_dp, n_expert) == (4, 8)
        expert_shape, expert = ((2, 2, 2), ("y", "x", "c")) if self.wide else ((n_expert,), ("expert",))
        self.dp = ("dh", "dl")
        self.expert = expert
        self.axes = self.dp + expert
        self.mesh = Mesh(mesh.devices.reshape((n_dp // 2, 2) + expert_shape), self.axes)

    def hop(self, value, axes, bit):
        size = lax.axis_size(axes)
        return lax.ppermute(value, axes, [(i, i ^ bit) for i in range(size)])

    def gather_depth(self, part, *gates):
        part = after(part, *gates)
        if not self.wide:
            return part
        half, quarter = self.cut(part)
        core = lax.axis_index("c")
        mine = lax.dynamic_slice_in_dim(part, core * half, half, 1)
        other = lax.dynamic_slice_in_dim(part, (1 - core) * half, half, 1)
        mine = flipped(core, mine, self.hop(other, "c", 1), 0)
        deep = self.deepen(mine)
        return lax.optimization_barrier((deep[:, :, :quarter], deep[:, :, quarter:]))

    def deepen(self, mine):
        pair = jnp.stack([mine, self.hop(mine, "dl", 1)])
        return jnp.concatenate([pair] + [self.hop(pair, "dh", k) for k in range(1, self.n_dp // 2)])

    def cut(self, part):
        return part.shape[1] // 2, part.shape[1] // 512 * 128

    def gather_side(self, pair, step, *gates):
        if not self.wide:
            return pair
        left, right, *_ = lax.optimization_barrier(tuple(pair) + gates)
        axes = ("x", "y") if step == 0 else ("y", "x")
        came = lax.optimization_barrier((self.hop(left, axes[0], 1), self.hop(right, axes[1], 1)))
        return tuple(jnp.concatenate([own, new]) for own, new in zip((left, right), came))

    def gather_core(self, pair, part):
        if not self.wide:
            return lax.all_gather(pair, self.axes, axis=0, tiled=True)
        left, right = pair
        rows, width = part.shape
        half, quarter = self.cut(part)
        core = lax.axis_index("c")
        far = lax.optimization_barrier((self.hop(left, "c", 1), self.hop(right, "c", 1)))
        steps = jnp.arange(16, dtype=jnp.int32)
        me = lax.axis_index(self.dp) * 4 + lax.axis_index("y") * 2 + lax.axis_index("x")
        first, second, turn = steps // 8, steps // 4 % 2, steps % 4
        left_at = (turn * 4 + first * 2 + second) ^ me
        right_at = (turn * 4 + second * 2 + first) ^ me

        def spots(at, side, side_core):
            across = jnp.broadcast_to((side_core * half + side * quarter) // 128, at.shape)
            return jnp.stack([at * (2 * rows // 16), across], axis=1).reshape(-1)

        places = jnp.stack(
            [
                spots(left_at, 0, core),
                spots(right_at, 1, core),
                spots(left_at, 0, 1 - core),
                spots(right_at, 1, 1 - core),
            ]
        ).astype(jnp.int32)
        return join(places, (left, right) + tuple(far), width)

    def scatter(self, full):
        if not self.wide:
            return lax.psum_scatter(full, self.axes, scatter_dimension=0, tiled=True).astype(WIDE)
        height, width = full.shape
        half, quarter = width // 2, width // 512 * 128
        core, y, x = lax.axis_index("c"), lax.axis_index("y"), lax.axis_index("x")
        across = self.hop(lax.dynamic_slice_in_dim(full, (1 - core) * half, half, 1), "c", 1)
        mine = self.plus(lax.dynamic_slice_in_dim(full, core * half, half, 1), across)
        mine = mine.reshape(self.n_dp, 2, 2, height // 16, half)

        def pick(value, at, axis):
            return lax.dynamic_index_in_dim(value, at, axis, keepdims=False)

        left, right = mine[..., :quarter], mine[..., quarter:]
        sent = lax.optimization_barrier((pick(left, 1 - y, 1), pick(right, 1 - x, 2)))
        came = lax.optimization_barrier((self.hop(sent[0], "y", 1), self.hop(sent[1], "x", 1)))
        left, right = self.plus(pick(left, y, 1), came[0]), self.plus(pick(right, x, 2), came[1])
        sent = lax.optimization_barrier((pick(left, 1 - x, 1), pick(right, 1 - y, 1)))
        came = lax.optimization_barrier((self.hop(sent[0], "x", 1), self.hop(sent[1], "y", 1)))
        left, right = self.plus(pick(left, x, 1), came[0]), self.plus(pick(right, y, 1), came[1])
        deep = jnp.concatenate([left, right], axis=2)
        deep = deep.reshape(2, 2, height // 16, half)
        high, low = lax.axis_index("dh"), lax.axis_index("dl")
        deep = self.plus(pick(deep, high, 0), self.hop(pick(deep, 1 - high, 0), "dh", 1))
        total = pick(deep, low, 0).astype(WIDE) + self.hop(pick(deep, 1 - low, 0), "dl", 1).astype(WIDE)
        rows = height // 32
        away = self.hop(lax.dynamic_slice_in_dim(total, (1 - core) * rows, rows, 0), "c", 1)
        return flipped(core, lax.dynamic_slice_in_dim(total, core * rows, rows, 0), away, 1)

    def plus(self, one, two):
        return (one.astype(WIDE) + two.astype(WIDE)).astype(LOW)

    def fetch_near(self, part):
        parity = lax.axis_index("dl")
        same, other = part[0], part[1]
        same, other = jnp.where(parity == 0, same, other), jnp.where(parity == 0, other, same)
        return jnp.stack([same, self.hop(other, "dl", 1)])

    def fetch_far(self, pair):
        return [self.hop(pair, "dh", k) for k in range(1, self.n_dp // 2)]

    def join_expert(self, pairs):
        turn = lax.axis_index(self.dp)
        rows, width = pairs[0].shape[1:]
        spots = []
        for k in range(self.n_dp // 2):
            near, far = turn ^ (2 * k), turn ^ (2 * k + 1)
            spots.append(jnp.stack([near * (rows // 16), 0 * turn, far * (rows // 16), 0 * turn]))
        return join(jnp.stack(spots).astype(jnp.int32), pairs, width)

    def share_far(self, partial, *gates):
        half = self.n_dp // 2
        pieces = after(partial, *gates).reshape(half, 2, D // self.n_dp, FF)
        high = lax.axis_index("dh")
        total = lax.dynamic_index_in_dim(pieces, high, 0, keepdims=False).astype(WIDE)
        for k in range(1, half):
            piece = lax.dynamic_index_in_dim(pieces, high ^ k, 0, keepdims=False)
            total = total + self.hop(piece, "dh", k).astype(WIDE)
        return total.astype(LOW)

    def share_near(self, pair):
        parity = lax.axis_index("dl")
        own = lax.dynamic_index_in_dim(pair, parity, 0).astype(WIDE)
        other = self.hop(lax.dynamic_index_in_dim(pair, 1 - parity, 0), "dl", 1).astype(WIDE)
        return flipped(parity, own, other, 0)

    def to_experts(self, rows):
        chunks = rows.reshape(2 * self.groups, -1, D)
        return lax.all_to_all(chunks, ("dl",) + self.expert, 0, 0, tiled=True).reshape(-1, D)


def after(value, *others):
    return lax.optimization_barrier((value,) + others)[0]


def padded(rows, fill=0):
    shaped = rows.reshape(rows.shape[0] // SEQ, SEQ, rows.shape[1])
    return jnp.pad(shaped, ((0, 0), (0, LINES - SEQ), (0, 0)), constant_values=fill)


def unpadded(lines):
    return lines[:, :SEQ].reshape(-1, lines.shape[2])


def flat(lines):
    return lines.reshape(-1, lines.shape[2])


def local(plan, act_in, w_qkv, w_proj, w_up, w_down, norm_gain, norm_shift, exp_in, exp_out, gate, expert_index, cotangent):
    experts_all = EXP_DEV * plan.groups
    capacity = (TOP * TOK_DEV * 5 // (4 * experts_all) + 7) // 8 * 8
    slots = experts_all * capacity
    proj_t = jnp.swapaxes(w_proj, 1, 2).astype(LOW)
    qkv_low = w_qkv.astype(LOW)
    norms = jnp.concatenate([norm_gain, norm_shift]).T.astype(LOW)
    norms = jnp.pad(norms, ((0, 0), (0, 256 - norms.shape[1])))
    part_a = jnp.concatenate([qkv_low[0], proj_t[0], norms], axis=1)
    part_b = jnp.concatenate([w_up.astype(LOW), w_down.T.astype(LOW)], axis=1)
    part_c = jnp.concatenate([qkv_low[1], proj_t[1]], axis=1)
    deep_a = plan.gather_depth(part_a)
    in_near = plan.fetch_near(after(exp_in.astype(LOW), deep_a))
    out_near = plan.fetch_near(after(jnp.swapaxes(exp_out, 1, 2).astype(LOW), in_near))
    in_far = plan.fetch_far(in_near)
    out_far = plan.fetch_far(after(out_near, in_far))
    deep_b = plan.gather_depth(part_b, deep_a)
    deep_c = plan.gather_depth(part_c, deep_b)
    one_a = plan.gather_side(deep_a, 0)
    two_a = plan.gather_side(one_a, 1)
    block_a = plan.gather_core(two_a, part_a)
    norms = block_a[:, 4 * D : 4 * D + 8].astype(WIDE).T
    gain, shift = norms[:4, None], norms[4:, None]
    one_b = plan.gather_side(deep_b, 0, two_a)

    flat_index = expert_index.reshape(-1)
    onehot = (flat_index[:, None] == jnp.arange(experts_all, dtype=jnp.int32)).astype(jnp.int32)
    before = jnp.cumsum(onehot, axis=0) - onehot
    holder = (flat_index % EXP_DEV) * plan.groups + flat_index // EXP_DEV
    spots = (holder * capacity + jnp.sum(onehot * before, axis=1)).reshape(-1, TOP)
    spots = padded(spots, -1)
    spot_rows = flat(spots).T
    gates, cot, x_a = padded(gate), padded(cotangent), padded(act_in)

    grad_rows = plan.to_experts(dispatch_grad(spot_rows, flat(gates), flat(cot), slots))

    x_b, packed_a, mixed_a = attend_forward(after(x_a, in_near), gain[0], shift[0], block_a)
    two_b = plan.gather_side(one_b, 1, x_b)
    block_b = plan.gather_core(two_b, part_b)
    one_c = plan.gather_side(deep_c, 0, two_b)
    x_c, hidden_b, slope_b = mlp_forward(after(x_b, out_near), gain[1], shift[1], block_b)
    two_c = plan.gather_side(one_c, 1)
    block_c = plan.gather_core(two_c, part_c)
    x_d, packed_c, mixed_c = attend_forward(x_c, gain[2], shift[2], block_c)
    sent = dispatch(spot_rows, flat(after(x_d, in_far, grad_rows)), gain[3], shift[3], slots)
    rows = plan.to_experts(sent)

    weight_in = plan.join_expert([in_near] + in_far)
    hidden, slope = expert_forward(rows, weight_in)
    down_partial = t_mm(grad_rows, hidden).astype(LOW)
    weight_out = plan.join_expert([out_near] + after(out_far, hidden, down_partial))
    dinner, droutes = expert_backward(grad_rows, slope, weight_in, weight_out)
    routes_home = plan.to_experts(droutes)
    result = mm_t(hidden, weight_out).astype(LOW)
    home = plan.to_experts(result)
    down_pair = plan.share_far(down_partial, weight_out)
    in_partial = t_mm(rows, dinner).astype(LOW)
    in_pair = plan.share_far(in_partial)

    act_out, grad_gate = combine(spots, gates, x_d, cot, home)
    dx_d, gain_d, shift_d = return_grad(spots, x_d, cot, gain[3], routes_home)
    dx_c, dpacked_c, normed_c, low_c, gain_c, shift_c = attend_backward(
        x_c, dx_d, packed_c, gain[2], shift[2], block_c
    )
    sum_c = jnp.concatenate(
        [t_mm(flat(normed_c), flat(dpacked_c)), t_mm(flat(low_c), flat(mixed_c))], axis=1
    )
    mine_c = plan.scatter(sum_c.astype(LOW))
    dx_b, dinner_b, normed_b, low_b, gain_b, shift_b = mlp_backward(
        x_b, dx_c, slope_b, gain[1], shift[1], block_b
    )
    sum_b = jnp.concatenate(
        [t_mm(flat(normed_b), flat(dinner_b)), t_mm(flat(low_b), flat(hidden_b))], axis=1
    )
    mine_b = plan.scatter(sum_b.astype(LOW))
    dx_a, dpacked_a, normed_a, low_a, gain_a, shift_a = attend_backward(
        x_a, after(dx_b, mine_c), packed_a, gain[0], shift[0], block_a
    )
    norm_grads = jnp.concatenate(
        [gain_a, gain_b, gain_c, gain_d, shift_a, shift_b, shift_c, shift_d]
    )
    norm_grads = jnp.pad(norm_grads.T, ((0, 0), (0, 248)))
    sum_a = jnp.concatenate(
        [t_mm(flat(normed_a), flat(dpacked_a)), t_mm(flat(low_a), flat(mixed_a)), norm_grads], axis=1
    )
    mine_a = plan.scatter(after(sum_a.astype(LOW), down_pair))
    grad_exp_out = jnp.swapaxes(plan.share_near(down_pair), 1, 2)
    grad_exp_in = plan.share_near(in_pair)

    grad_qkv = jnp.stack([mine_a[:, : 3 * D], mine_c[:, : 3 * D]])
    grad_proj = jnp.stack([mine_a[:, 3 * D : 4 * D], mine_c[:, 3 * D :]])
    return (
        unpadded(act_out),
        unpadded(dx_a),
        grad_qkv,
        jnp.swapaxes(grad_proj, 1, 2),
        mine_b[:, :FF],
        mine_b[:, FF:].T,
        mine_a[:, 4 * D : 4 * D + 4].T,
        mine_a[:, 4 * D + 4 : 4 * D + 8].T,
        grad_exp_in,
        grad_exp_out,
        unpadded(grad_gate),
    )


def solution(mesh):
    plan = Plan(mesh)
    rows, dp, expert = plan.axes, plan.dp, plan.expert
    in_specs = (
        P(rows, None),
        P(None, rows, None),
        P(None, None, rows),
        P(rows, None),
        P(None, rows),
        P(None, rows),
        P(None, rows),
        P(expert, dp, None),
        P(expert, None, dp),
        P(rows, None),
        P(rows, None),
        P(rows, None),
    )
    out_specs = (
        P(rows, None),
        P(rows, None),
        P(None, rows, None),
        P(None, None, rows),
        P(rows, None),
        P(None, rows),
        P(None, rows),
        P(None, rows),
        P(expert, dp, None),
        P(expert, None, dp),
        P(rows, None),
    )
    return jax.shard_map(
        functools.partial(local, plan),
        mesh=plan.mesh,
        in_specs=in_specs,
        out_specs=out_specs,
        check_vma=False,
    )
```

```python
import functools
import math

import jax
import jax.numpy as jnp
import numpy as np
from jax import lax
from jax.experimental import pallas as pl
from jax.experimental.pallas import tpu as pltpu
from jax.sharding import Mesh, PartitionSpec as P

D = 768
FF = 3072
HEADS = 12
HEAD = 64
SEQ = 197
LINES = 208
TOP = 2
EXP_DEV = 2
TOK_DEV = 591
EPS = 1e-06
LOW = jnp.bfloat16
WIDE = jnp.float32
SCALE = 1.0 / math.sqrt(HEAD)
RSQRT2 = 1.0 / math.sqrt(2.0)
RSQRT2PI = 1.0 / math.sqrt(2.0 * math.pi)
SLOT_TILE = 256
ROW_TILE = 256
WIDTH_TILE = 768
HINT = 4


def mm(left, right):
    return jnp.dot(left, right, preferred_element_type=WIDE)


def mm_t(left, right):
    return lax.dot_general(left, right, (((1,), (1,)), ((), ())), preferred_element_type=WIDE)


def t_mm(left, right):
    return lax.dot_general(left, right, (((0,), (0,)), ((), ())), preferred_element_type=WIDE)


def norm_parts(inputs):
    average = jnp.mean(inputs, axis=-1, keepdims=True)
    centred = inputs - average
    spread = jnp.mean(centred * centred, axis=-1, keepdims=True)
    inverse = lax.rsqrt(spread + EPS)
    return centred * inverse, inverse


def norm_low(inputs, gain_ref, shift_ref):
    xhat, _ = norm_parts(inputs)
    return (xhat * gain_ref[...] + shift_ref[...]).astype(LOW)


def norm_backward(dnormed, xhat, inverse, gain_ref, residual, dx_ref, dgain_ref, dshift_ref):
    scaled = dnormed * gain_ref[...]
    mean = jnp.mean(scaled, axis=-1, keepdims=True)
    tilt = jnp.mean(scaled * xhat, axis=-1, keepdims=True)
    dx_ref[0] = residual + inverse * (scaled - mean - xhat * tilt)

    @pl.when(pl.program_id(0) == 0)
    def _():
        dgain_ref[...] = jnp.zeros_like(dgain_ref)
        dshift_ref[...] = jnp.zeros_like(dshift_ref)

    dgain_ref[...] += jnp.sum(dnormed * xhat, axis=0, keepdims=True)
    dshift_ref[...] += jnp.sum(dnormed, axis=0, keepdims=True)


def gelu_both(inner):
    phi = 0.5 + 0.5 * lax.erf(inner * RSQRT2)
    slope = phi + inner * (RSQRT2PI * jnp.exp(-0.5 * inner * inner))
    return (inner * phi).astype(LOW), slope.astype(LOW)


def softmax_rows(query, key):
    scores = mm_t(query, key) * SCALE
    lane = lax.broadcasted_iota(jnp.int32, scores.shape, 1)
    scores = jnp.where(lane < SEQ, scores, -jnp.inf)
    peak = jnp.max(scores, axis=-1, keepdims=True)
    raised = jnp.exp(scores - peak)
    total = jnp.sum(raised, axis=-1, keepdims=True)
    return raised * (1.0 / total)


def whole(shape):
    return pl.BlockSpec(shape, lambda *_: (0,) * len(shape))


def window(width, at):
    return pl.BlockSpec((D, width), lambda *_: (0, at))


def image(width):
    return pl.BlockSpec((1, LINES, width), lambda i: (i, 0, 0))


def params(megabytes):
    return pltpu.CompilerParams(vmem_limit_bytes=megabytes << 20)


def like(shape, kind):
    return jax.ShapeDtypeStruct(shape, kind)


def cost(flops, moved, raised=0):
    return pl.CostEstimate(
        flops=flops // HINT, bytes_accessed=moved // HINT, transcendentals=raised // HINT
    )


def attend_forward_body(x_ref, gain_ref, shift_ref, qkv_ref, proj_ref, out_ref, packed_ref, mixed_ref):
    x = x_ref[0]
    packed_ref[0] = mm(norm_low(x, gain_ref, shift_ref), qkv_ref[...]).astype(LOW)
    first = lax.broadcasted_iota(jnp.int32, (LINES, 2 * HEAD), 1) < HEAD
    zero = jnp.zeros((LINES, 2 * HEAD), LOW)
    for pair in range(HEADS // 2):
        at = pair * 2 * HEAD
        query = packed_ref[0, :, at : at + 2 * HEAD]
        key = packed_ref[0, :, D + at : D + at + 2 * HEAD]
        value = packed_ref[0, :, 2 * D + at : 2 * D + at + 2 * HEAD]
        low = mm(softmax_rows(jnp.where(first, query, zero), key).astype(LOW), value)
        high = mm(softmax_rows(jnp.where(first, zero, query), key).astype(LOW), value)
        mixed_ref[0, :, at : at + 2 * HEAD] = jnp.where(first, low, high).astype(LOW)
    out_ref[0] = x + mm_t(mixed_ref[0], proj_ref[...])


def attend_forward(x, gain, shift, block):
    images = x.shape[0]
    return pl.pallas_call(
        attend_forward_body,
        grid=(images,),
        in_specs=[image(D), whole((1, D)), whole((1, D)), window(3 * D, 0), window(D, 3)],
        out_specs=[image(D), image(3 * D), image(D)],
        out_shape=[
            like((images, LINES, D), WIDE),
            like((images, LINES, 3 * D), LOW),
            like((images, LINES, D), LOW),
        ],
        compiler_params=params(48),
        cost_estimate=cost(3_700_000_000, 13_000_000, 1_600_000),
        name="attend_forward",
    )(x, gain, shift, block, block)


def attend_backward_body(
    x_ref, dy_ref, packed_ref, gain_ref, shift_ref, qkv_ref, proj_ref,
    dx_ref, dpacked_ref, normed_ref, low_ref, dgain_ref, dshift_ref,
    dmixed_ref,
):
    dy = dy_ref[0]
    grad_low = dy.astype(LOW)
    low_ref[0] = grad_low
    dmixed_ref[...] = mm(grad_low, proj_ref[...]).astype(LOW)
    first = lax.broadcasted_iota(jnp.int32, (LINES, 2 * HEAD), 1) < HEAD
    zero = jnp.zeros((LINES, 2 * HEAD), LOW)

    def one(query, key, value, upstream):
        probs = softmax_rows(query, key)
        dprobs = mm_t(upstream, value)
        inner = jnp.sum(probs * dprobs, axis=-1, keepdims=True)
        dscores = (probs * (dprobs - inner)).astype(LOW)
        return t_mm(probs.astype(LOW), upstream), mm(dscores, key), t_mm(dscores, query)

    for pair in range(HEADS // 2):
        at = pair * 2 * HEAD
        query = packed_ref[0, :, at : at + 2 * HEAD]
        key = packed_ref[0, :, D + at : D + at + 2 * HEAD]
        value = packed_ref[0, :, 2 * D + at : 2 * D + at + 2 * HEAD]
        upstream = dmixed_ref[:, at : at + 2 * HEAD]
        dv0, dq0, dk0 = one(
            jnp.where(first, query, zero), key, value, jnp.where(first, upstream, zero)
        )
        dv1, dq1, dk1 = one(
            jnp.where(first, zero, query), key, value, jnp.where(first, zero, upstream)
        )
        dpacked_ref[0, :, at : at + 2 * HEAD] = (jnp.where(first, dq0, dq1) * SCALE).astype(LOW)
        dpacked_ref[0, :, D + at : D + at + 2 * HEAD] = ((dk0 + dk1) * SCALE).astype(LOW)
        dpacked_ref[0, :, 2 * D + at : 2 * D + at + 2 * HEAD] = (dv0 + dv1).astype(LOW)
    xhat, inverse = norm_parts(x_ref[0])
    normed_ref[0] = (xhat * gain_ref[...] + shift_ref[...]).astype(LOW)
    dnormed = mm_t(dpacked_ref[0], qkv_ref[...])
    norm_backward(dnormed, xhat, inverse, gain_ref, dy, dx_ref, dgain_ref, dshift_ref)


def attend_backward(x, dy, packed, gain, shift, block):
    images = x.shape[0]
    return pl.pallas_call(
        attend_backward_body,
        grid=(images,),
        in_specs=[
            image(D), image(D), image(3 * D), whole((1, D)), whole((1, D)),
            window(3 * D, 0), window(D, 3),
        ],
        out_specs=[image(D), image(3 * D), image(D), image(D), whole((1, D)), whole((1, D))],
        out_shape=[
            like((images, LINES, D), WIDE),
            like((images, LINES, 3 * D), LOW),
            like((images, LINES, D), LOW),
            like((images, LINES, D), LOW),
            like((1, D), WIDE),
            like((1, D), WIDE),
        ],
        scratch_shapes=[pltpu.VMEM((LINES, D), LOW)],
        compiler_params=params(48),
        cost_estimate=cost(4_000_000_000, 22_000_000, 1_600_000),
        name="attend_backward",
    )(x, dy, packed, gain, shift, block, block)


def mlp_forward_body(x_ref, gain_ref, shift_ref, up_ref, down_ref, out_ref, hidden_ref, slope_ref):
    x = x_ref[0]
    normed = norm_low(x, gain_ref, shift_ref)
    total = x
    step = FF // 4
    for at in range(0, FF, step):
        hidden, slope = gelu_both(mm(normed, up_ref[:, at : at + step]))
        hidden_ref[0, :, at : at + step] = hidden
        slope_ref[0, :, at : at + step] = slope
        total = total + mm_t(hidden, down_ref[:, at : at + step])
    out_ref[0] = total


def mlp_forward(x, gain, shift, block):
    images = x.shape[0]
    return pl.pallas_call(
        mlp_forward_body,
        grid=(images,),
        in_specs=[image(D), whole((1, D)), whole((1, D)), window(FF, 0), window(FF, 1)],
        out_specs=[image(D), image(FF), image(FF)],
        out_shape=[
            like((images, LINES, D), WIDE),
            like((images, LINES, FF), LOW),
            like((images, LINES, FF), LOW),
        ],
        compiler_params=params(56),
        cost_estimate=cost(5_900_000_000, 21_000_000, 4_000_000),
        name="mlp_forward",
    )(x, gain, shift, block, block)


def mlp_backward_body(
    x_ref, dy_ref, slope_ref, gain_ref, shift_ref, up_ref, down_ref,
    dx_ref, dinner_ref, normed_ref, low_ref, dgain_ref, dshift_ref,
):
    dy = dy_ref[0]
    grad_low = dy.astype(LOW)
    low_ref[0] = grad_low
    step = FF // 4
    dnormed = jnp.zeros((LINES, D), WIDE)
    for at in range(0, FF, step):
        dhidden = mm(grad_low, down_ref[:, at : at + step])
        dinner = (dhidden * slope_ref[0, :, at : at + step].astype(WIDE)).astype(LOW)
        dinner_ref[0, :, at : at + step] = dinner
        dnormed = dnormed + mm_t(dinner, up_ref[:, at : at + step])
    xhat, inverse = norm_parts(x_ref[0])
    normed_ref[0] = (xhat * gain_ref[...] + shift_ref[...]).astype(LOW)
    norm_backward(dnormed, xhat, inverse, gain_ref, dy, dx_ref, dgain_ref, dshift_ref)


def mlp_backward(x, dy, slope, gain, shift, block):
    images = x.shape[0]
    return pl.pallas_call(
        mlp_backward_body,
        grid=(images,),
        in_specs=[
            image(D), image(D), image(FF), whole((1, D)), whole((1, D)),
            window(FF, 0), window(FF, 1),
        ],
        out_specs=[image(D), image(FF), image(D), image(D), whole((1, D)), whole((1, D))],
        out_shape=[
            like((images, LINES, D), WIDE),
            like((images, LINES, FF), LOW),
            like((images, LINES, D), LOW),
            like((images, LINES, D), LOW),
            like((1, D), WIDE),
            like((1, D), WIDE),
        ],
        compiler_params=params(56),
        cost_estimate=cost(5_900_000_000, 25_000_000),
        name="mlp_backward",
    )(x, dy, slope, gain, shift, block, block)


def chosen(places_ref, tile):
    tokens = places_ref.shape[1]
    slot = pl.program_id(0) * tile + lax.broadcasted_iota(jnp.int32, (tile, tokens), 0)
    return [jnp.where(slot == places_ref[k : k + 1, :], 1.0, 0.0) for k in range(TOP)]


def dispatch_body(places_ref, x_ref, gain_ref, shift_ref, out_ref, sent_ref):
    @pl.when(pl.program_id(0) == 0)
    def _():
        sent_ref[...] = norm_low(x_ref[...], gain_ref, shift_ref)

    picks = chosen(places_ref, SLOT_TILE)
    out_ref[...] = mm((picks[0] + picks[1]).astype(LOW), sent_ref[...]).astype(LOW)


def dispatch(places, x, gain, shift, slots):
    tokens = x.shape[0]
    return pl.pallas_call(
        dispatch_body,
        grid=(slots // SLOT_TILE,),
        in_specs=[whole((TOP, tokens)), whole((tokens, D)), whole((1, D)), whole((1, D))],
        out_specs=pl.BlockSpec((SLOT_TILE, D), lambda i: (i, 0)),
        out_shape=like((slots, D), LOW),
        scratch_shapes=[pltpu.VMEM((tokens, D), LOW)],
        compiler_params=params(32),
        cost_estimate=cost(1_500_000_000, 4_500_000),
        name="dispatch",
    )(places, x, gain, shift)


def dispatch_grad_body(places_ref, gate_ref, cot_ref, out_ref, sent_ref):
    @pl.when(pl.program_id(0) == 0)
    def _():
        for k in range(TOP):
            sent_ref[k] = (gate_ref[:, k : k + 1] * cot_ref[...]).astype(LOW)

    picks = chosen(places_ref, SLOT_TILE)
    total = mm(picks[0].astype(LOW), sent_ref[0]) + mm(picks[1].astype(LOW), sent_ref[1])
    out_ref[...] = total.astype(LOW)


def dispatch_grad(places, gate, cot, slots):
    tokens = cot.shape[0]
    return pl.pallas_call(
        dispatch_grad_body,
        grid=(slots // SLOT_TILE,),
        in_specs=[whole((TOP, tokens)), whole((tokens, TOP)), whole((tokens, D))],
        out_specs=pl.BlockSpec((SLOT_TILE, D), lambda i: (i, 0)),
        out_shape=like((slots, D), LOW),
        scratch_shapes=[pltpu.VMEM((TOP, tokens, D), LOW)],
        compiler_params=params(32),
        cost_estimate=cost(3_000_000_000, 4_500_000),
        name="dispatch_grad",
    )(places, gate, cot)


def picker(places_ref, k, slots):
    lane = lax.broadcasted_iota(jnp.int32, (LINES, slots), 1)
    return jnp.where(lane == places_ref[0, :, k : k + 1], 1.0, 0.0)


def combine_body(places_ref, gate_ref, x_ref, cot_ref, home_ref, out_ref, dgate_ref):
    slots = home_ref.shape[0]
    total = x_ref[0]
    for k in range(TOP):
        picked = mm(picker(places_ref, k, slots).astype(LOW), home_ref[...])
        total = total + gate_ref[0, :, k : k + 1] * picked
        dgate_ref[0, :, k : k + 1] = jnp.sum(cot_ref[0] * picked, axis=-1, keepdims=True)
    out_ref[0] = total


def combine(places, gate, x, cot, home):
    images, slots = x.shape[0], home.shape[0]
    return pl.pallas_call(
        combine_body,
        grid=(images,),
        in_specs=[image(TOP), image(TOP), image(D), image(D), whole((slots, D))],
        out_specs=[image(D), image(TOP)],
        out_shape=[like((images, LINES, D), WIDE), like((images, LINES, TOP), WIDE)],
        compiler_params=params(32),
        cost_estimate=cost(3_000_000_000, 8_000_000),
        name="combine",
    )(places, gate, x, cot, home)


def return_grad_body(places_ref, x_ref, cot_ref, gain_ref, home_ref, dx_ref, dgain_ref, dshift_ref):
    slots = home_ref.shape[0]
    picks = (picker(places_ref, 0, slots) + picker(places_ref, 1, slots)).astype(LOW)
    dsent = mm(picks, home_ref[...])
    xhat, inverse = norm_parts(x_ref[0])
    norm_backward(dsent, xhat, inverse, gain_ref, cot_ref[0], dx_ref, dgain_ref, dshift_ref)


def return_grad(places, x, cot, gain, home):
    images, slots = x.shape[0], home.shape[0]
    return pl.pallas_call(
        return_grad_body,
        grid=(images,),
        in_specs=[image(TOP), image(D), image(D), whole((1, D)), whole((slots, D))],
        out_specs=[image(D), whole((1, D)), whole((1, D))],
        out_shape=[like((images, LINES, D), WIDE), like((1, D), WIDE), like((1, D), WIDE)],
        compiler_params=params(32),
        cost_estimate=cost(1_500_000_000, 8_000_000),
        name="return_grad",
    )(places, x, cot, gain, home)


def expert_forward_body(rows_ref, in_ref, hidden_ref, slope_ref):
    step = FF // 4
    for at in range(0, FF, step):
        hidden, slope = gelu_both(mm(rows_ref[...], in_ref[:, at : at + step]))
        hidden_ref[:, at : at + step] = hidden
        slope_ref[:, at : at + step] = slope


def tiled(width):
    return pl.BlockSpec((ROW_TILE, width), lambda i: (i, 0))


def expert_forward(rows, weight):
    count = rows.shape[0]
    return pl.pallas_call(
        expert_forward_body,
        grid=(count // ROW_TILE,),
        in_specs=[tiled(D), whole((D, FF))],
        out_specs=[tiled(FF), tiled(FF)],
        out_shape=[like((count, FF), LOW), like((count, FF), LOW)],
        compiler_params=params(48),
        cost_estimate=cost(7_200_000_000, 26_000_000, 9_000_000),
        name="expert_forward",
    )(rows, weight)


def expert_backward_body(grad_ref, slope_ref, in_ref, out_ref, dinner_ref, dx_ref):
    step = FF // 4
    total = jnp.zeros((ROW_TILE, D), WIDE)
    for at in range(0, FF, step):
        dhidden = mm(grad_ref[...], out_ref[:, at : at + step])
        dinner = (dhidden * slope_ref[:, at : at + step].astype(WIDE)).astype(LOW)
        dinner_ref[:, at : at + step] = dinner
        total = total + mm_t(dinner, in_ref[:, at : at + step])
    dx_ref[...] = total.astype(LOW)


def expert_backward(grad, slope, weight_in, weight_out_t):
    count = grad.shape[0]
    return pl.pallas_call(
        expert_backward_body,
        grid=(count // ROW_TILE,),
        in_specs=[tiled(D), tiled(FF), whole((D, FF)), whole((D, FF))],
        out_specs=[tiled(FF), tiled(D)],
        out_shape=[like((count, FF), LOW), like((count, D), LOW)],
        compiler_params=params(48),
        cost_estimate=cost(14_400_000_000, 33_000_000),
        name="expert_backward",
    )(grad, slope, weight_in, weight_out_t)


def weight_grad_body(tiles, starts, split, at_ref, *refs):
    count = len(starts)
    lefts, rights = refs[:count], refs[count : 2 * count]
    outs, turned = refs[2 * count : -count], refs[-count:]
    step = pl.program_id(0)
    tile = lax.rem(step + at_ref[0], tiles)

    @pl.when(step == 0)
    def _():
        for left, scratch in zip(lefts, turned):
            scratch[...] = left[...].T

    for index, (left, right) in enumerate(zip(turned, rights)):
        stop = (starts + (tiles,))[index + 1]

        @pl.when((tile >= starts[index]) & (tile < stop))
        def _(left=left, right=right):
            value = mm(left[...], right[...]).astype(LOW)
            if split:

                @pl.when(step < tiles // 2)
                def _():
                    outs[0][...] = value

                @pl.when(step >= tiles // 2)
                def _():
                    outs[1][...] = value
            else:
                outs[0][...] = value


def weight_grad(split, core, *pairs):
    width = WIDTH_TILE
    tokens = pairs[0][0].shape[0]
    counts = [right.shape[1] // width for _, right in pairs]
    starts = tuple(int(n) for n in np.cumsum([0] + counts[:-1]))
    tiles = sum(counts)
    first = ((1 - core) * (tiles // 2) if split else 0 * core).astype(jnp.int32).reshape(1)

    def right_spec(start, count):
        def at(step, at_ref):
            return 0, jnp.clip(lax.rem(step + at_ref[0], tiles) - start, 0, count - 1)

        return pl.BlockSpec((tokens, width), at)

    half = tiles // 2
    if split:
        out_specs = [
            pl.BlockSpec((D, width), lambda step, _: (0, jnp.minimum(step, half - 1))),
            pl.BlockSpec((D, width), lambda step, _: (0, jnp.maximum(step - half, 0))),
        ]
        out_shape = [like((D, half * width), LOW)] * 2
    else:
        out_specs = [pl.BlockSpec((D, width), lambda step, _: (0, step))]
        out_shape = [like((D, tiles * width), LOW)]
    return pl.pallas_call(
        functools.partial(weight_grad_body, tiles, starts, split),
        grid_spec=pltpu.PrefetchScalarGridSpec(
            num_scalar_prefetch=1,
            grid=(tiles,),
            in_specs=[whole((tokens, D)) for _ in pairs]
            + [right_spec(start, count) for start, count in zip(starts, counts)],
            out_specs=out_specs,
            scratch_shapes=[pltpu.VMEM((D, tokens), LOW) for _ in pairs],
        ),
        out_shape=out_shape,
        compiler_params=params(48),
        cost_estimate=cost(2 * D * tokens * tiles * width, 3 * D * tiles * width),
        name="weight_grad",
    )(first, *[left for left, _ in pairs], *[right for _, right in pairs])


def join_body(at_ref, *refs):
    *parts, out_ref, sem = refs
    for index, part in enumerate(parts):
        rows, width = part.shape[1:]
        for block in range(part.shape[0]):
            down = pl.multiple_of(at_ref[index, 2 * block] * 16, 16)
            right = pl.multiple_of(at_ref[index, 2 * block + 1] * 128, 128)
            target = out_ref.at[pl.ds(down, rows), pl.ds(right, width)]
            pltpu.make_async_copy(part.at[block], target, sem).start()
    pltpu.make_async_copy(out_ref, out_ref, sem).wait()


def join(places, parts, width):
    return pl.pallas_call(
        join_body,
        in_specs=[pl.BlockSpec(memory_space=pltpu.SMEM)]
        + [pl.BlockSpec(memory_space=pl.ANY)] * len(parts),
        out_specs=pl.BlockSpec(memory_space=pltpu.VMEM),
        out_shape=like((D, width), LOW),
        scratch_shapes=[pltpu.SemaphoreType.DMA],
        compiler_params=params(32),
        cost_estimate=cost(0, 4 * D * width),
        name="join",
    )(places, *parts)


def pick(value, at, axis):
    return lax.dynamic_index_in_dim(value, at, axis, keepdims=False)


def flipped(index, first, second, axis):
    return jnp.where(
        index == 0,
        jnp.concatenate([first, second], axis=axis),
        jnp.concatenate([second, first], axis=axis),
    )


class Plan:
    def __init__(self, mesh):
        n_dp, n_expert = mesh.devices.shape
        self.n_dp, self.groups = n_dp, n_expert
        self.wide = (n_dp, n_expert) == (4, 8)
        expert_shape, expert = ((2, 2, 2), ("y", "x", "c")) if self.wide else ((n_expert,), ("expert",))
        self.dp = ("dh", "dl")
        self.expert = expert
        self.axes = self.dp + expert
        self.mesh = Mesh(mesh.devices.reshape((n_dp // 2, 2) + expert_shape), self.axes)

    def hop(self, value, axes, bit):
        size = lax.axis_size(axes)
        return lax.ppermute(value, axes, [(i, i ^ bit) for i in range(size)])

    def gather_depth(self, parts):
        if not self.wide:
            return jnp.concatenate(parts, axis=1)
        core = lax.axis_index("c")
        sides = [
            jnp.concatenate(
                [
                    lax.dynamic_slice_in_dim(part, side * self.cut(part)[0], self.cut(part)[0], 1)
                    for part in parts
                ],
                axis=1,
            )
            for side in (core, 1 - core)
        ]
        mine = flipped(core, sides[0], self.hop(sides[1], "c", 1), 0)
        return lax.all_gather(mine[None], self.dp, axis=0, tiled=True)

    def gather_split(self, deep, parts):
        if not self.wide:
            ends = np.cumsum([part.shape[1] for part in parts])
            return [deep[:, end - part.shape[1] : end] for end, part in zip(ends, parts)]
        pairs, at = [], 0
        for part in parts:
            half, quarter = self.cut(part)
            pairs.append((deep[:, :, at : at + quarter], deep[:, :, at + quarter : at + half]))
            at += half
        return pairs

    def cut(self, part):
        return part.shape[1] // 2, part.shape[1] // 512 * 128

    def gather_side(self, pair, step):
        if not self.wide:
            return pair
        left, right = lax.optimization_barrier(tuple(pair))
        axes = ("x", "y") if step == 0 else ("y", "x")
        came = lax.optimization_barrier((self.hop(left, axes[0], 1), self.hop(right, axes[1], 1)))
        return tuple(jnp.concatenate([own, new]) for own, new in zip((left, right), came))

    def gather_core(self, pair):
        if not self.wide:
            return pair
        return tuple(pair) + tuple(self.hop(value, "c", 1) for value in pair)

    def gather_join(self, four, part):
        if not self.wide:
            return lax.all_gather(four, self.axes, axis=0, tiled=True)
        rows, width = part.shape
        half, quarter = self.cut(part)
        core = lax.axis_index("c")
        steps = jnp.arange(16, dtype=jnp.int32)
        me = lax.axis_index("y") * 2 + lax.axis_index("x")
        first, second, turn = steps // 8, steps // 4 % 2, steps % 4
        left_at = (turn * 4 + first * 2 + second) ^ me
        right_at = (turn * 4 + second * 2 + first) ^ me

        def spots(at, side, side_core):
            across = jnp.broadcast_to((side_core * half + side * quarter) // 128, at.shape)
            return jnp.stack([at * (2 * rows // 16), across], axis=1).reshape(-1)

        places = jnp.stack(
            [
                spots(left_at, 0, core),
                spots(right_at, 1, core),
                spots(left_at, 0, 1 - core),
                spots(right_at, 1, 1 - core),
            ]
        ).astype(jnp.int32)
        return join(places, four, width)

    def scatter_swap(self, halves):
        if not self.wide:
            return halves[0]
        other, mine = halves
        height, half = mine.shape
        quarter = half // 256 * 128
        mine = self.plus(mine, self.hop(other, "c", 1))
        mine = mine.reshape(self.n_dp, 2, 2, height // 16, half)
        return mine[..., :quarter], mine[..., quarter:]

    def scatter_side(self, pair, step):
        if not self.wide:
            return pair
        y, x = lax.axis_index("y"), lax.axis_index("x")
        turns = ((("y", y, 1), ("x", x, 2)), (("x", x, 1), ("y", y, 1)))[step]
        kept = [pick(value, at, axis) for value, (_, at, axis) in zip(pair, turns)]
        sent = [pick(value, 1 - at, axis) for value, (_, at, axis) in zip(pair, turns)]
        sent = lax.optimization_barrier(tuple(sent))
        came = [self.hop(value, name, 1) for value, (name, _, _) in zip(sent, turns)]
        came = lax.optimization_barrier(tuple(came))
        return tuple(self.plus(one, two) for one, two in zip(kept, came))

    def scatter_far(self, pair, side):
        if not self.wide:
            return pair
        deep = pair[side].reshape((2, 2) + pair[side].shape[1:])
        high = lax.axis_index("dh")
        return self.plus(pick(deep, high, 0), self.hop(pick(deep, 1 - high, 0), "dh", 1))

    def scatter_merge(self, left, right):
        return jnp.concatenate([left, right], axis=2) if self.wide else left

    def scatter_small(self, values):
        devices = self.n_dp * self.groups
        pieces = lax.all_to_all(values.reshape(devices, -1), self.axes, 0, 0, tiled=True)
        return jnp.sum(pieces, axis=0).reshape(-1, values.shape[1])

    def scatter_near(self, deep):
        if not self.wide:
            return deep
        low = lax.axis_index("dl")
        return pick(deep, low, 0).astype(WIDE) + self.hop(pick(deep, 1 - low, 0), "dl", 1).astype(WIDE)

    def scatter_core(self, total):
        if not self.wide:
            return lax.psum_scatter(total, self.axes, scatter_dimension=0, tiled=True).astype(WIDE)
        core, rows = lax.axis_index("c"), total.shape[0] // 2
        away = self.hop(lax.dynamic_slice_in_dim(total, (1 - core) * rows, rows, 0), "c", 1)
        return flipped(core, lax.dynamic_slice_in_dim(total, core * rows, rows, 0), away, 1)

    def plus(self, one, two):
        return (one.astype(WIDE) + two.astype(WIDE)).astype(LOW)

    def fetch_near(self, part):
        parity = lax.axis_index("dl")
        same, other = part[0], part[1]
        same, other = jnp.where(parity == 0, same, other), jnp.where(parity == 0, other, same)
        pair = flipped(parity, same[None], self.hop(other, "dl", 1)[None], 0)
        return pair.reshape(-1, part.shape[2])

    def fetch_far(self, pair, *gates):
        return lax.all_gather(after(pair, *gates), "dh", axis=0, tiled=True)

    def share_far(self, partial, *gates):
        return lax.psum_scatter(after(partial, *gates), "dh", scatter_dimension=0, tiled=True)

    def share_near(self, pair):
        pair = pair.reshape(2, -1, pair.shape[1])
        parity = lax.axis_index("dl")
        own = lax.dynamic_index_in_dim(pair, parity, 0).astype(WIDE)
        other = self.hop(lax.dynamic_index_in_dim(pair, 1 - parity, 0), "dl", 1).astype(WIDE)
        return flipped(parity, own, other, 0)

    def to_experts(self, rows):
        chunks = rows.reshape(2 * self.groups, -1, D)
        return lax.all_to_all(chunks, ("dl",) + self.expert, 0, 0, tiled=True).reshape(-1, D)


def after(value, *others):
    return lax.optimization_barrier((value,) + others)[0]


def fenced(ready, body, *operands):
    shapes = jax.eval_shape(body, *operands)
    empty = lambda *_: jax.tree.map(lambda leaf: jnp.zeros(leaf.shape, leaf.dtype), shapes)
    return lax.cond(ready, body, empty, *operands)


def padded(rows, fill=0):
    shaped = rows.reshape(rows.shape[0] // SEQ, SEQ, rows.shape[1])
    return jnp.pad(shaped, ((0, 0), (0, LINES - SEQ), (0, 0)), constant_values=fill)


def unpadded(lines):
    return lines[:, :SEQ].reshape(-1, lines.shape[2])


def flat(lines):
    return lines.reshape(-1, lines.shape[2])


def local(plan, act_in, w_qkv, w_proj, w_up, w_down, norm_gain, norm_shift, exp_in, exp_out, gate, expert_index, cotangent):
    experts_all = EXP_DEV * plan.groups
    capacity = (TOP * TOK_DEV * 5 // (4 * experts_all) + 7) // 8 * 8
    slots = experts_all * capacity
    proj_t = jnp.swapaxes(w_proj, 1, 2).astype(LOW)
    qkv_low = w_qkv.astype(LOW)
    norms = jnp.concatenate([norm_gain, norm_shift]).T.astype(LOW)
    norms = jnp.pad(norms, ((0, 0), (0, 256 - norms.shape[1])))
    part_a = jnp.concatenate([qkv_low[0], proj_t[0], norms], axis=1)
    part_b = jnp.concatenate([w_up.astype(LOW), w_down.T.astype(LOW)], axis=1)
    part_c = jnp.concatenate([qkv_low[1], proj_t[1]], axis=1)
    ready = expert_index[0, 0] >= 0
    bar = lax.optimization_barrier
    core = lax.axis_index("c") if plan.wide else 0 * expert_index[0, 0]
    parts = (part_a, part_b, part_c)
    in_near = plan.fetch_near(exp_in.astype(LOW))
    deep = plan.gather_depth(parts)

    def prepare(expert_index, gate, cotangent, act_in):
        flat_index = expert_index.reshape(-1)
        onehot = (flat_index[:, None] == jnp.arange(experts_all, dtype=jnp.int32)).astype(jnp.int32)
        before = jnp.cumsum(onehot, axis=0) - onehot
        holder = (flat_index % EXP_DEV) * plan.groups + flat_index // EXP_DEV
        spots = (holder * capacity + jnp.sum(onehot * before, axis=1)).reshape(-1, TOP)
        spots = padded(spots, -1)
        gates, cot, x_a = padded(gate), padded(cotangent), padded(act_in)
        grad_sent = dispatch_grad(flat(spots).T, flat(gates), flat(cot), slots)
        return spots, gates, cot, x_a, grad_sent

    spots, gates, cot, x_a, grad_sent = fenced(
        ready, prepare, expert_index, gate, cotangent, act_in
    )
    spot_rows = flat(spots).T

    out_low = jnp.swapaxes(exp_out, 1, 2).astype(LOW)
    in_near, out_low, x_a, grad_sent, deep = bar((in_near, out_low, x_a, grad_sent, deep))
    weight_in = plan.fetch_far(in_near)
    out_near = plan.fetch_near(out_low)

    def zeroth_part(deep, parts):
        pair_a, pair_b, pair_c = plan.gather_split(deep, parts)
        one_a = bar(plan.gather_side(pair_a, 0))
        two_a = bar(plan.gather_side(one_a, 1))
        pair_b, two_a = bar((pair_b, two_a))
        four_a, one_b = bar((plan.gather_core(two_a), plan.gather_side(pair_b, 0)))
        return four_a, one_b, pair_c

    four_a, one_b, pair_c = fenced(ready, zeroth_part, deep, parts)
    four_a, out_near = bar((four_a, out_near))
    weight_out = plan.fetch_far(out_near)

    def first_part(four_a, one_b, part_a, x_a):
        block_a = plan.gather_join(four_a, part_a)
        norms = block_a[:, 4 * D : 4 * D + 8].astype(WIDE).T
        gain, shift = norms[:4, None], norms[4:, None]
        x_b, packed_a, mixed_a = attend_forward(x_a, gain[0], shift[0], block_a)
        two_b, x_b = bar((plan.gather_side(one_b, 1), x_b))
        return gain, shift, block_a, x_b, packed_a, mixed_a, two_b

    gain, shift, block_a, x_b, packed_a, mixed_a, two_b = fenced(
        ready, first_part, four_a, one_b, part_a, x_a
    )

    def second_part(x_b, gain, shift, two_b, pair_c, part_b, part_c, spot_rows, grad_sent):
        grad_rows = plan.to_experts(grad_sent)
        four_b, one_c = bar((plan.gather_core(two_b), plan.gather_side(pair_c, 0)))
        block_b = plan.gather_join(four_b, part_b)
        x_c, hidden_b, slope_b = mlp_forward(x_b, gain[1], shift[1], block_b)
        two_c, x_c = bar((plan.gather_side(one_c, 1), x_c))
        block_c = plan.gather_join(bar(plan.gather_core(two_c)), part_c)
        x_d, packed_c, mixed_c = attend_forward(x_c, gain[2], shift[2], block_c)
        x_d, grad_rows = bar((x_d, grad_rows))
        rows = plan.to_experts(dispatch(spot_rows, flat(x_d), gain[3], shift[3], slots))
        return block_b, block_c, x_c, x_d, hidden_b, slope_b, packed_c, mixed_c, rows, grad_rows

    block_b, block_c, x_c, x_d, hidden_b, slope_b, packed_c, mixed_c, rows, grad_rows = fenced(
        ready, second_part, x_b, gain, shift, two_b, pair_c, part_b, part_c, spot_rows, grad_sent
    )
    hidden, slope = expert_forward(rows, weight_in)
    (down_partial,) = weight_grad(False, core, (grad_rows, hidden))
    down_pair = plan.share_far(down_partial)

    def experts_backward(rows, grad_rows, hidden, slope, weight_in, weight_out):
        dinner, droutes = expert_backward(grad_rows, slope, weight_in, weight_out)
        routes_home = plan.to_experts(droutes)
        (in_partial,) = weight_grad(False, core, (after(rows, droutes), dinner))
        result = mm_t(after(hidden, in_partial), weight_out).astype(LOW)
        routes_home, result = bar((routes_home, result))
        return routes_home, in_partial, result

    routes_home, in_partial, result = fenced(
        ready, experts_backward, rows, grad_rows, hidden, slope, weight_in,
        after(weight_out, down_partial),
    )
    in_pair = plan.share_far(in_partial)

    def third_part(
        gain, shift, block_b, block_c, x_b, x_c, x_d, packed_c, mixed_c, hidden_b, slope_b, spots,
        cot, routes_home, result,
    ):
        home = plan.to_experts(result)
        dx_d, gain_d, shift_d = return_grad(spots, x_d, cot, gain[3], routes_home)
        dx_c, dpacked_c, normed_c, low_c, gain_c, shift_c = attend_backward(
            x_c, dx_d, packed_c, gain[2], shift[2], block_c
        )
        sum_c = weight_grad(
            plan.wide, core, (flat(normed_c), flat(dpacked_c)), (flat(low_c), flat(mixed_c))
        )
        sum_c, dx_c = bar((sum_c, dx_c))
        dx_b, dinner_b, normed_b, low_b, gain_b, shift_b = mlp_backward(
            x_b, dx_c, slope_b, gain[1], shift[1], block_b
        )
        pair_c, dx_b, dinner_b, home = bar((plan.scatter_swap(sum_c), dx_b, dinner_b, home))
        sum_b = weight_grad(
            plan.wide, core, (flat(normed_b), flat(dinner_b)), (flat(low_b), flat(hidden_b))
        )
        pair_c, sum_b = bar((plan.scatter_side(pair_c, 0), sum_b))
        pair_c, pair_b = bar((plan.scatter_side(pair_c, 1), plan.scatter_swap(sum_b)))
        gains, shifts = (gain_b, gain_c, gain_d), (shift_b, shift_c, shift_d)
        return pair_c, pair_b, dx_b, gains, shifts, home

    pair_c, pair_b, dx_b, gains, shifts, home = fenced(
        ready, third_part, gain, shift, block_b, block_c, x_b, x_c, x_d, packed_c, mixed_c,
        hidden_b, slope_b, spots, cot, routes_home, result,
    )

    def fourth_part(
        gain, shift, block_a, x_a, packed_a, mixed_a, pair_c, pair_b, dx_b, gains, shifts, down_pair,
    ):
        dx_a, dpacked_a, normed_a, low_a, gain_a, shift_a = attend_backward(
            x_a, dx_b, packed_a, gain[0], shift[0], block_a
        )
        grad_out = plan.share_near(down_pair)
        pair_b, far_c, dx_a, dpacked_a, grad_out = bar(
            (
                plan.scatter_side(pair_b, 0),
                plan.scatter_merge(plan.scatter_far(pair_c, 0), plan.scatter_far(pair_c, 1)),
                dx_a,
                dpacked_a,
                grad_out,
            )
        )
        norm_grads = jnp.concatenate((gain_a,) + gains + (shift_a,) + shifts).T
        sum_a = weight_grad(
            plan.wide, core, (flat(normed_a), flat(dpacked_a)), (flat(low_a), flat(mixed_a))
        )
        pair_b, near_c, sum_a = bar((plan.scatter_side(pair_b, 1), plan.scatter_near(far_c), sum_a))
        pair_a, left_b, mine_c = bar(
            (plan.scatter_swap(sum_a), plan.scatter_far(pair_b, 0), plan.scatter_core(near_c))
        )
        pair_a, right_b = bar((plan.scatter_side(pair_a, 0), plan.scatter_far(pair_b, 1)))
        far_b = plan.scatter_merge(left_b, right_b)
        return unpadded(dx_a), norm_grads, pair_a, far_b, mine_c, grad_out

    dx_a, norm_grads, pair_a, far_b, mine_c, grad_exp_out = fenced(
        ready, fourth_part, gain, shift, block_a, x_a, packed_a, mixed_a, pair_c, pair_b, dx_b,
        gains, shifts, down_pair,
    )

    def fifth_part(pair_a, far_b, in_pair, norm_grads, spots, gates, x_d, cot, home):
        grad_exp_in = plan.share_near(in_pair)
        mine_norms = plan.scatter_small(norm_grads)
        act_out, grad_gate = combine(spots, gates, x_d, cot, home)
        pair_a, near_b, act_out = bar(
            (plan.scatter_side(pair_a, 1), plan.scatter_near(far_b), act_out)
        )
        far_a = plan.scatter_merge(plan.scatter_far(pair_a, 0), plan.scatter_far(pair_a, 1))
        far_a, mine_b, grad_exp_in, mine_norms = bar(
            (far_a, plan.scatter_core(near_b), grad_exp_in, mine_norms)
        )
        mine_a = plan.scatter_core(plan.scatter_near(far_a))
        return mine_a, mine_b, mine_norms, grad_exp_in, unpadded(act_out), unpadded(grad_gate)

    mine_a, mine_b, mine_norms, grad_exp_in, act_out, grad_gate = fenced(
        ready, fifth_part, pair_a, far_b, in_pair, norm_grads, spots, gates, x_d, cot, home
    )
    grad_exp_out = jnp.swapaxes(grad_exp_out, 1, 2)

    grad_qkv = jnp.stack([mine_a[:, : 3 * D], mine_c[:, : 3 * D]])
    grad_proj = jnp.stack([mine_a[:, 3 * D :], mine_c[:, 3 * D :]])
    return (
        act_out,
        dx_a,
        grad_qkv,
        jnp.swapaxes(grad_proj, 1, 2),
        mine_b[:, :FF],
        mine_b[:, FF:].T,
        mine_norms[:, :4].T,
        mine_norms[:, 4:8].T,
        grad_exp_in,
        grad_exp_out,
        grad_gate,
    )


def solution(mesh):
    plan = Plan(mesh)
    rows, dp, expert = plan.axes, plan.dp, plan.expert
    in_specs = (
        P(rows, None),
        P(None, rows, None),
        P(None, None, rows),
        P(rows, None),
        P(None, rows),
        P(None, rows),
        P(None, rows),
        P(expert, dp, None),
        P(expert, None, dp),
        P(rows, None),
        P(rows, None),
        P(rows, None),
    )
    out_specs = (
        P(rows, None),
        P(rows, None),
        P(None, rows, None),
        P(None, None, rows),
        P(rows, None),
        P(None, rows),
        P(None, rows),
        P(None, rows),
        P(expert, dp, None),
        P(expert, None, dp),
        P(rows, None),
    )
    return jax.shard_map(
        functools.partial(local, plan),
        mesh=plan.mesh,
        in_specs=in_specs,
        out_specs=out_specs,
        check_vma=False,
    )
```

```python
import functools
import math

import jax
import jax.numpy as jnp
import numpy as np
from jax import lax
from jax.experimental import pallas as pl
from jax.experimental.pallas import tpu as pltpu
from jax.sharding import Mesh, PartitionSpec as P

D = 768
FF = 3072
HEADS = 12
HEAD = 64
SEQ = 197
LINES = 208
TOP = 2
EXP_DEV = 2
TOK_DEV = 591
EPS = 1e-06
LOW = jnp.bfloat16
WIDE = jnp.float32
SCALE = 1.0 / math.sqrt(HEAD)
RSQRT2 = 1.0 / math.sqrt(2.0)
RSQRT2PI = 1.0 / math.sqrt(2.0 * math.pi)
SLOT_TILE = 256
ROW_TILE = 256
WIDTH_TILE = 768
HINT = 4


def mm(left, right):
    return jnp.dot(left, right, preferred_element_type=WIDE)


def mm_t(left, right):
    return lax.dot_general(left, right, (((1,), (1,)), ((), ())), preferred_element_type=WIDE)


def t_mm(left, right):
    return lax.dot_general(left, right, (((0,), (0,)), ((), ())), preferred_element_type=WIDE)


def norm_parts(inputs):
    average = jnp.mean(inputs, axis=-1, keepdims=True)
    centred = inputs - average
    spread = jnp.mean(centred * centred, axis=-1, keepdims=True)
    inverse = lax.rsqrt(spread + EPS)
    return centred * inverse, inverse


def norm_low(inputs, gain_ref, shift_ref):
    xhat, _ = norm_parts(inputs)
    return (xhat * gain_ref[...] + shift_ref[...]).astype(LOW)


def norm_backward(dnormed, xhat, inverse, gain_ref, residual, dx_ref, dgain_ref, dshift_ref):
    scaled = dnormed * gain_ref[...]
    mean = jnp.mean(scaled, axis=-1, keepdims=True)
    tilt = jnp.mean(scaled * xhat, axis=-1, keepdims=True)
    dx_ref[0] = residual + inverse * (scaled - mean - xhat * tilt)

    @pl.when(pl.program_id(0) == 0)
    def _():
        dgain_ref[...] = jnp.zeros_like(dgain_ref)
        dshift_ref[...] = jnp.zeros_like(dshift_ref)

    dgain_ref[...] += jnp.sum(dnormed * xhat, axis=0, keepdims=True)
    dshift_ref[...] += jnp.sum(dnormed, axis=0, keepdims=True)


def gelu_both(inner):
    phi = 0.5 + 0.5 * lax.erf(inner * RSQRT2)
    slope = phi + inner * (RSQRT2PI * jnp.exp(-0.5 * inner * inner))
    return (inner * phi).astype(LOW), slope.astype(LOW)


def softmax_rows(query, key):
    scores = mm_t(query, key) * SCALE
    lane = lax.broadcasted_iota(jnp.int32, scores.shape, 1)
    scores = jnp.where(lane < SEQ, scores, -jnp.inf)
    peak = jnp.max(scores, axis=-1, keepdims=True)
    raised = jnp.exp(scores - peak)
    total = jnp.sum(raised, axis=-1, keepdims=True)
    return raised * (1.0 / total)


def whole(shape):
    return pl.BlockSpec(shape, lambda *_: (0,) * len(shape))


def window(width, at):
    return pl.BlockSpec((D, width), lambda *_: (0, at))


def image(width):
    return pl.BlockSpec((1, LINES, width), lambda i: (i, 0, 0))


def params(megabytes):
    return pltpu.CompilerParams(vmem_limit_bytes=megabytes << 20)


def like(shape, kind):
    return jax.ShapeDtypeStruct(shape, kind)


def cost(flops, moved, raised=0):
    return pl.CostEstimate(
        flops=flops // HINT, bytes_accessed=moved // HINT, transcendentals=raised // HINT
    )


def attend_forward_body(x_ref, gain_ref, shift_ref, qkv_ref, proj_ref, out_ref, packed_ref, mixed_ref):
    x = x_ref[0]
    packed_ref[0] = mm(norm_low(x, gain_ref, shift_ref), qkv_ref[...]).astype(LOW)
    first = lax.broadcasted_iota(jnp.int32, (LINES, 2 * HEAD), 1) < HEAD
    zero = jnp.zeros((LINES, 2 * HEAD), LOW)
    for pair in range(HEADS // 2):
        at = pair * 2 * HEAD
        query = packed_ref[0, :, at : at + 2 * HEAD]
        key = packed_ref[0, :, D + at : D + at + 2 * HEAD]
        value = packed_ref[0, :, 2 * D + at : 2 * D + at + 2 * HEAD]
        low = mm(softmax_rows(jnp.where(first, query, zero), key).astype(LOW), value)
        high = mm(softmax_rows(jnp.where(first, zero, query), key).astype(LOW), value)
        mixed_ref[0, :, at : at + 2 * HEAD] = jnp.where(first, low, high).astype(LOW)
    out_ref[0] = x + mm_t(mixed_ref[0], proj_ref[...])


def attend_forward(x, gain, shift, block):
    images = x.shape[0]
    return pl.pallas_call(
        attend_forward_body,
        grid=(images,),
        in_specs=[image(D), whole((1, D)), whole((1, D)), window(3 * D, 0), window(D, 3)],
        out_specs=[image(D), image(3 * D), image(D)],
        out_shape=[
            like((images, LINES, D), WIDE),
            like((images, LINES, 3 * D), LOW),
            like((images, LINES, D), LOW),
        ],
        compiler_params=params(48),
        cost_estimate=cost(3_700_000_000, 13_000_000, 1_600_000),
        name="attend_forward",
    )(x, gain, shift, block, block)


def attend_backward_body(
    x_ref, dy_ref, packed_ref, gain_ref, shift_ref, qkv_ref, proj_ref,
    dx_ref, dpacked_ref, normed_ref, low_ref, dgain_ref, dshift_ref,
    dmixed_ref,
):
    dy = dy_ref[0]
    grad_low = dy.astype(LOW)
    low_ref[0] = grad_low
    dmixed_ref[...] = mm(grad_low, proj_ref[...]).astype(LOW)
    first = lax.broadcasted_iota(jnp.int32, (LINES, 2 * HEAD), 1) < HEAD
    zero = jnp.zeros((LINES, 2 * HEAD), LOW)

    def one(query, key, value, upstream):
        probs = softmax_rows(query, key)
        dprobs = mm_t(upstream, value)
        inner = jnp.sum(probs * dprobs, axis=-1, keepdims=True)
        dscores = (probs * (dprobs - inner)).astype(LOW)
        return t_mm(probs.astype(LOW), upstream), mm(dscores, key), t_mm(dscores, query)

    for pair in range(HEADS // 2):
        at = pair * 2 * HEAD
        query = packed_ref[0, :, at : at + 2 * HEAD]
        key = packed_ref[0, :, D + at : D + at + 2 * HEAD]
        value = packed_ref[0, :, 2 * D + at : 2 * D + at + 2 * HEAD]
        upstream = dmixed_ref[:, at : at + 2 * HEAD]
        dv0, dq0, dk0 = one(
            jnp.where(first, query, zero), key, value, jnp.where(first, upstream, zero)
        )
        dv1, dq1, dk1 = one(
            jnp.where(first, zero, query), key, value, jnp.where(first, zero, upstream)
        )
        dpacked_ref[0, :, at : at + 2 * HEAD] = (jnp.where(first, dq0, dq1) * SCALE).astype(LOW)
        dpacked_ref[0, :, D + at : D + at + 2 * HEAD] = ((dk0 + dk1) * SCALE).astype(LOW)
        dpacked_ref[0, :, 2 * D + at : 2 * D + at + 2 * HEAD] = (dv0 + dv1).astype(LOW)
    xhat, inverse = norm_parts(x_ref[0])
    normed_ref[0] = (xhat * gain_ref[...] + shift_ref[...]).astype(LOW)
    dnormed = mm_t(dpacked_ref[0], qkv_ref[...])
    norm_backward(dnormed, xhat, inverse, gain_ref, dy, dx_ref, dgain_ref, dshift_ref)


def attend_backward(x, dy, packed, gain, shift, block):
    images = x.shape[0]
    return pl.pallas_call(
        attend_backward_body,
        grid=(images,),
        in_specs=[
            image(D), image(D), image(3 * D), whole((1, D)), whole((1, D)),
            window(3 * D, 0), window(D, 3),
        ],
        out_specs=[image(D), image(3 * D), image(D), image(D), whole((1, D)), whole((1, D))],
        out_shape=[
            like((images, LINES, D), WIDE),
            like((images, LINES, 3 * D), LOW),
            like((images, LINES, D), LOW),
            like((images, LINES, D), LOW),
            like((1, D), WIDE),
            like((1, D), WIDE),
        ],
        scratch_shapes=[pltpu.VMEM((LINES, D), LOW)],
        compiler_params=params(48),
        cost_estimate=cost(4_000_000_000, 22_000_000, 1_600_000),
        name="attend_backward",
    )(x, dy, packed, gain, shift, block, block)


def mlp_forward_body(x_ref, gain_ref, shift_ref, up_ref, down_ref, out_ref, hidden_ref, slope_ref):
    x = x_ref[0]
    normed = norm_low(x, gain_ref, shift_ref)
    total = x
    step = FF // 4
    for at in range(0, FF, step):
        hidden, slope = gelu_both(mm(normed, up_ref[:, at : at + step]))
        hidden_ref[0, :, at : at + step] = hidden
        slope_ref[0, :, at : at + step] = slope
        total = total + mm_t(hidden, down_ref[:, at : at + step])
    out_ref[0] = total


def mlp_forward(x, gain, shift, block):
    images = x.shape[0]
    return pl.pallas_call(
        mlp_forward_body,
        grid=(images,),
        in_specs=[image(D), whole((1, D)), whole((1, D)), window(FF, 0), window(FF, 1)],
        out_specs=[image(D), image(FF), image(FF)],
        out_shape=[
            like((images, LINES, D), WIDE),
            like((images, LINES, FF), LOW),
            like((images, LINES, FF), LOW),
        ],
        compiler_params=params(56),
        cost_estimate=cost(5_900_000_000, 21_000_000, 4_000_000),
        name="mlp_forward",
    )(x, gain, shift, block, block)


def mlp_backward_body(
    x_ref, dy_ref, slope_ref, gain_ref, shift_ref, up_ref, down_ref,
    dx_ref, dinner_ref, normed_ref, low_ref, dgain_ref, dshift_ref,
):
    dy = dy_ref[0]
    grad_low = dy.astype(LOW)
    low_ref[0] = grad_low
    step = FF // 4
    dnormed = jnp.zeros((LINES, D), WIDE)
    for at in range(0, FF, step):
        dhidden = mm(grad_low, down_ref[:, at : at + step])
        dinner = (dhidden * slope_ref[0, :, at : at + step].astype(WIDE)).astype(LOW)
        dinner_ref[0, :, at : at + step] = dinner
        dnormed = dnormed + mm_t(dinner, up_ref[:, at : at + step])
    xhat, inverse = norm_parts(x_ref[0])
    normed_ref[0] = (xhat * gain_ref[...] + shift_ref[...]).astype(LOW)
    norm_backward(dnormed, xhat, inverse, gain_ref, dy, dx_ref, dgain_ref, dshift_ref)


def mlp_backward(x, dy, slope, gain, shift, block):
    images = x.shape[0]
    return pl.pallas_call(
        mlp_backward_body,
        grid=(images,),
        in_specs=[
            image(D), image(D), image(FF), whole((1, D)), whole((1, D)),
            window(FF, 0), window(FF, 1),
        ],
        out_specs=[image(D), image(FF), image(D), image(D), whole((1, D)), whole((1, D))],
        out_shape=[
            like((images, LINES, D), WIDE),
            like((images, LINES, FF), LOW),
            like((images, LINES, D), LOW),
            like((images, LINES, D), LOW),
            like((1, D), WIDE),
            like((1, D), WIDE),
        ],
        compiler_params=params(56),
        cost_estimate=cost(5_900_000_000, 25_000_000),
        name="mlp_backward",
    )(x, dy, slope, gain, shift, block, block)


def chosen(places_ref, tile):
    tokens = places_ref.shape[1]
    slot = pl.program_id(0) * tile + lax.broadcasted_iota(jnp.int32, (tile, tokens), 0)
    return [jnp.where(slot == places_ref[k : k + 1, :], 1.0, 0.0) for k in range(TOP)]


def dispatch_body(places_ref, x_ref, gain_ref, shift_ref, out_ref, sent_ref):
    @pl.when(pl.program_id(0) == 0)
    def _():
        sent_ref[...] = norm_low(x_ref[...], gain_ref, shift_ref)

    picks = chosen(places_ref, SLOT_TILE)
    out_ref[...] = mm((picks[0] + picks[1]).astype(LOW), sent_ref[...]).astype(LOW)


def dispatch(places, x, gain, shift, slots):
    tokens = x.shape[0]
    return pl.pallas_call(
        dispatch_body,
        grid=(slots // SLOT_TILE,),
        in_specs=[whole((TOP, tokens)), whole((tokens, D)), whole((1, D)), whole((1, D))],
        out_specs=pl.BlockSpec((SLOT_TILE, D), lambda i: (i, 0)),
        out_shape=like((slots, D), LOW),
        scratch_shapes=[pltpu.VMEM((tokens, D), LOW)],
        compiler_params=params(32),
        cost_estimate=cost(1_500_000_000, 4_500_000),
        name="dispatch",
    )(places, x, gain, shift)


def dispatch_grad_body(places_ref, gate_ref, cot_ref, out_ref, sent_ref):
    @pl.when(pl.program_id(0) == 0)
    def _():
        for k in range(TOP):
            sent_ref[k] = (gate_ref[:, k : k + 1] * cot_ref[...]).astype(LOW)

    picks = chosen(places_ref, SLOT_TILE)
    total = mm(picks[0].astype(LOW), sent_ref[0]) + mm(picks[1].astype(LOW), sent_ref[1])
    out_ref[...] = total.astype(LOW)


def dispatch_grad(places, gate, cot, slots):
    tokens = cot.shape[0]
    return pl.pallas_call(
        dispatch_grad_body,
        grid=(slots // SLOT_TILE,),
        in_specs=[whole((TOP, tokens)), whole((tokens, TOP)), whole((tokens, D))],
        out_specs=pl.BlockSpec((SLOT_TILE, D), lambda i: (i, 0)),
        out_shape=like((slots, D), LOW),
        scratch_shapes=[pltpu.VMEM((TOP, tokens, D), LOW)],
        compiler_params=params(32),
        cost_estimate=cost(3_000_000_000, 4_500_000),
        name="dispatch_grad",
    )(places, gate, cot)


def picker(places_ref, k, slots):
    lane = lax.broadcasted_iota(jnp.int32, (LINES, slots), 1)
    return jnp.where(lane == places_ref[0, :, k : k + 1], 1.0, 0.0)


def combine_body(places_ref, gate_ref, x_ref, cot_ref, home_ref, out_ref, dgate_ref):
    slots = home_ref.shape[0]
    total = x_ref[0]
    for k in range(TOP):
        picked = mm(picker(places_ref, k, slots).astype(LOW), home_ref[...])
        total = total + gate_ref[0, :, k : k + 1] * picked
        dgate_ref[0, :, k : k + 1] = jnp.sum(cot_ref[0] * picked, axis=-1, keepdims=True)
    out_ref[0] = total


def combine(places, gate, x, cot, home):
    images, slots = x.shape[0], home.shape[0]
    return pl.pallas_call(
        combine_body,
        grid=(images,),
        in_specs=[image(TOP), image(TOP), image(D), image(D), whole((slots, D))],
        out_specs=[image(D), image(TOP)],
        out_shape=[like((images, LINES, D), WIDE), like((images, LINES, TOP), WIDE)],
        compiler_params=params(32),
        cost_estimate=cost(3_000_000_000, 8_000_000),
        name="combine",
    )(places, gate, x, cot, home)


def return_grad_body(places_ref, x_ref, cot_ref, gain_ref, home_ref, dx_ref, dgain_ref, dshift_ref):
    slots = home_ref.shape[0]
    picks = (picker(places_ref, 0, slots) + picker(places_ref, 1, slots)).astype(LOW)
    dsent = mm(picks, home_ref[...])
    xhat, inverse = norm_parts(x_ref[0])
    norm_backward(dsent, xhat, inverse, gain_ref, cot_ref[0], dx_ref, dgain_ref, dshift_ref)


def return_grad(places, x, cot, gain, home):
    images, slots = x.shape[0], home.shape[0]
    return pl.pallas_call(
        return_grad_body,
        grid=(images,),
        in_specs=[image(TOP), image(D), image(D), whole((1, D)), whole((slots, D))],
        out_specs=[image(D), whole((1, D)), whole((1, D))],
        out_shape=[like((images, LINES, D), WIDE), like((1, D), WIDE), like((1, D), WIDE)],
        compiler_params=params(32),
        cost_estimate=cost(1_500_000_000, 8_000_000),
        name="return_grad",
    )(places, x, cot, gain, home)


def expert_forward_body(rows_ref, in_ref, hidden_ref, slope_ref):
    step = FF // 4
    for at in range(0, FF, step):
        hidden, slope = gelu_both(mm(rows_ref[...], in_ref[:, at : at + step]))
        hidden_ref[:, at : at + step] = hidden
        slope_ref[:, at : at + step] = slope


def tiled(width):
    return pl.BlockSpec((ROW_TILE, width), lambda i: (i, 0))


def expert_forward(rows, weight):
    count = rows.shape[0]
    return pl.pallas_call(
        expert_forward_body,
        grid=(count // ROW_TILE,),
        in_specs=[tiled(D), whole((D, FF))],
        out_specs=[tiled(FF), tiled(FF)],
        out_shape=[like((count, FF), LOW), like((count, FF), LOW)],
        compiler_params=params(48),
        cost_estimate=cost(7_200_000_000, 26_000_000, 9_000_000),
        name="expert_forward",
    )(rows, weight)


def expert_backward_body(grad_ref, slope_ref, in_ref, out_ref, dinner_ref, dx_ref):
    step = FF // 4
    total = jnp.zeros((ROW_TILE, D), WIDE)
    for at in range(0, FF, step):
        dhidden = mm(grad_ref[...], out_ref[:, at : at + step])
        dinner = (dhidden * slope_ref[:, at : at + step].astype(WIDE)).astype(LOW)
        dinner_ref[:, at : at + step] = dinner
        total = total + mm_t(dinner, in_ref[:, at : at + step])
    dx_ref[...] = total.astype(LOW)


def expert_backward(grad, slope, weight_in, weight_out_t):
    count = grad.shape[0]
    return pl.pallas_call(
        expert_backward_body,
        grid=(count // ROW_TILE,),
        in_specs=[tiled(D), tiled(FF), whole((D, FF)), whole((D, FF))],
        out_specs=[tiled(FF), tiled(D)],
        out_shape=[like((count, FF), LOW), like((count, D), LOW)],
        compiler_params=params(48),
        cost_estimate=cost(14_400_000_000, 33_000_000),
        name="expert_backward",
    )(grad, slope, weight_in, weight_out_t)


def weight_grad_body(tiles, starts, split, at_ref, *refs):
    count = len(starts)
    lefts, rights = refs[:count], refs[count : 2 * count]
    outs, turned = refs[2 * count : -count], refs[-count:]
    step = pl.program_id(0)
    tile = lax.rem(step + at_ref[0], tiles)

    @pl.when(step == 0)
    def _():
        for left, scratch in zip(lefts, turned):
            scratch[...] = left[...].T

    for index, (left, right) in enumerate(zip(turned, rights)):
        stop = (starts + (tiles,))[index + 1]

        @pl.when((tile >= starts[index]) & (tile < stop))
        def _(left=left, right=right):
            value = mm(left[...], right[...]).astype(LOW)
            if split:

                @pl.when(step < tiles // 2)
                def _():
                    outs[0][...] = value

                @pl.when(step >= tiles // 2)
                def _():
                    outs[1][...] = value
            else:
                outs[0][...] = value


def weight_grad(split, core, *pairs):
    width = WIDTH_TILE
    tokens = pairs[0][0].shape[0]
    counts = [right.shape[1] // width for _, right in pairs]
    starts = tuple(int(n) for n in np.cumsum([0] + counts[:-1]))
    tiles = sum(counts)
    first = ((1 - core) * (tiles // 2) if split else 0 * core).astype(jnp.int32).reshape(1)

    def right_spec(start, count):
        def at(step, at_ref):
            return 0, jnp.clip(lax.rem(step + at_ref[0], tiles) - start, 0, count - 1)

        return pl.BlockSpec((tokens, width), at)

    half = tiles // 2
    if split:
        out_specs = [
            pl.BlockSpec((D, width), lambda step, _: (0, jnp.minimum(step, half - 1))),
            pl.BlockSpec((D, width), lambda step, _: (0, jnp.maximum(step - half, 0))),
        ]
        out_shape = [like((D, half * width), LOW)] * 2
    else:
        out_specs = [pl.BlockSpec((D, width), lambda step, _: (0, step))]
        out_shape = [like((D, tiles * width), LOW)]
    return pl.pallas_call(
        functools.partial(weight_grad_body, tiles, starts, split),
        grid_spec=pltpu.PrefetchScalarGridSpec(
            num_scalar_prefetch=1,
            grid=(tiles,),
            in_specs=[whole((tokens, D)) for _ in pairs]
            + [right_spec(start, count) for start, count in zip(starts, counts)],
            out_specs=out_specs,
            scratch_shapes=[pltpu.VMEM((D, tokens), LOW) for _ in pairs],
        ),
        out_shape=out_shape,
        compiler_params=params(48),
        cost_estimate=cost(2 * D * tokens * tiles * width, 3 * D * tiles * width),
        name="weight_grad",
    )(first, *[left for left, _ in pairs], *[right for _, right in pairs])


def join_body(at_ref, *refs):
    *parts, out_ref, sem = refs
    for index, part in enumerate(parts):
        rows, width = part.shape[1:]
        for block in range(part.shape[0]):
            down = pl.multiple_of(at_ref[index, 2 * block] * 16, 16)
            right = pl.multiple_of(at_ref[index, 2 * block + 1] * 128, 128)
            target = out_ref.at[pl.ds(down, rows), pl.ds(right, width)]
            pltpu.make_async_copy(part.at[block], target, sem).start()
    pltpu.make_async_copy(out_ref, out_ref, sem).wait()


def join(places, parts, width):
    return pl.pallas_call(
        join_body,
        in_specs=[pl.BlockSpec(memory_space=pltpu.SMEM)]
        + [pl.BlockSpec(memory_space=pl.ANY)] * len(parts),
        out_specs=pl.BlockSpec(memory_space=pltpu.VMEM),
        out_shape=like((D, width), LOW),
        scratch_shapes=[pltpu.SemaphoreType.DMA],
        compiler_params=params(32),
        cost_estimate=cost(0, 4 * D * width),
        name="join",
    )(places, *parts)


def pick(value, at, axis):
    return lax.dynamic_index_in_dim(value, at, axis, keepdims=False)


def flipped(index, first, second, axis):
    return jnp.where(
        index == 0,
        jnp.concatenate([first, second], axis=axis),
        jnp.concatenate([second, first], axis=axis),
    )


class Plan:
    def __init__(self, mesh):
        n_dp, n_expert = mesh.devices.shape
        self.n_dp, self.groups = n_dp, n_expert
        self.wide = (n_dp, n_expert) == (4, 8)
        expert_shape, expert = ((2, 2, 2), ("y", "x", "c")) if self.wide else ((n_expert,), ("expert",))
        self.dp = ("dh", "dl")
        self.expert = expert
        self.axes = self.dp + expert
        self.mesh = Mesh(mesh.devices.reshape((2, n_dp // 2) + expert_shape), self.axes)

    def hop(self, value, axes, bit):
        size = lax.axis_size(axes)
        return lax.ppermute(value, axes, [(i, i ^ bit) for i in range(size)])

    def gather_depth(self, parts):
        if not self.wide:
            return jnp.concatenate(parts, axis=1)
        core = lax.axis_index("c")
        sides = [
            jnp.concatenate(
                [
                    lax.dynamic_slice_in_dim(part, side * self.cut(part)[0], self.cut(part)[0], 1)
                    for part in parts
                ],
                axis=1,
            )
            for side in (core, 1 - core)
        ]
        mine = flipped(core, sides[0], self.hop(sides[1], "c", 1), 0)
        return lax.all_gather(mine[None], self.dp, axis=0, tiled=True)

    def gather_split(self, deep, parts):
        if not self.wide:
            ends = np.cumsum([part.shape[1] for part in parts])
            return [deep[:, end - part.shape[1] : end] for end, part in zip(ends, parts)]
        pairs, at = [], 0
        for part in parts:
            half, quarter = self.cut(part)
            pairs.append((deep[:, :, at : at + quarter], deep[:, :, at + quarter : at + half]))
            at += half
        return pairs

    def cut(self, part):
        return part.shape[1] // 2, part.shape[1] // 512 * 128

    def gather_side(self, pair, step):
        if not self.wide:
            return pair
        left, right = lax.optimization_barrier(tuple(pair))
        axes = ("x", "y") if step == 0 else ("y", "x")
        came = lax.optimization_barrier((self.hop(left, axes[0], 1), self.hop(right, axes[1], 1)))
        return tuple(jnp.concatenate([own, new]) for own, new in zip((left, right), came))

    def gather_core(self, pair):
        if not self.wide:
            return pair
        return tuple(pair) + tuple(self.hop(value, "c", 1) for value in pair)

    def gather_join(self, four, part):
        if not self.wide:
            return lax.all_gather(four, self.axes, axis=0, tiled=True)
        rows, width = part.shape
        half, quarter = self.cut(part)
        core = lax.axis_index("c")
        steps = jnp.arange(16, dtype=jnp.int32)
        me = lax.axis_index("y") * 2 + lax.axis_index("x")
        first, second, turn = steps // 8, steps // 4 % 2, steps % 4
        left_at = (turn * 4 + first * 2 + second) ^ me
        right_at = (turn * 4 + second * 2 + first) ^ me

        def spots(at, side, side_core):
            across = jnp.broadcast_to((side_core * half + side * quarter) // 128, at.shape)
            return jnp.stack([at * (2 * rows // 16), across], axis=1).reshape(-1)

        places = jnp.stack(
            [
                spots(left_at, 0, core),
                spots(right_at, 1, core),
                spots(left_at, 0, 1 - core),
                spots(right_at, 1, 1 - core),
            ]
        ).astype(jnp.int32)
        return join(places, four, width)

    def scatter_swap(self, halves):
        if not self.wide:
            return halves[0]
        other, mine = halves
        height, half = mine.shape
        quarter = half // 256 * 128
        mine = self.plus(mine, self.hop(other, "c", 1))
        mine = mine.reshape(self.n_dp, 2, 2, height // 16, half)
        return mine[..., :quarter], mine[..., quarter:]

    def scatter_side(self, pair, step):
        if not self.wide:
            return pair
        y, x = lax.axis_index("y"), lax.axis_index("x")
        turns = ((("y", y, 1), ("x", x, 2)), (("x", x, 1), ("y", y, 1)))[step]
        kept = [pick(value, at, axis) for value, (_, at, axis) in zip(pair, turns)]
        sent = [pick(value, 1 - at, axis) for value, (_, at, axis) in zip(pair, turns)]
        sent = lax.optimization_barrier(tuple(sent))
        came = [self.hop(value, name, 1) for value, (name, _, _) in zip(sent, turns)]
        came = lax.optimization_barrier(tuple(came))
        return tuple(self.plus(one, two) for one, two in zip(kept, came))

    def scatter_stack(self, *pairs):
        if not self.wide:
            return jnp.concatenate(pairs, axis=1)
        return jnp.concatenate([value for pair in pairs for value in pair], axis=2)

    def scatter_send(self, deep):
        if not self.wide:
            return deep, deep[:1, :1]
        deep = deep.reshape((2, 2) + deep.shape[1:])
        high = lax.axis_index("dh")
        return pick(deep, high, 0), self.hop(pick(deep, 1 - high, 0), "dh", 1)

    def scatter_add(self, own, far):
        return self.plus(own, far) if self.wide else own

    def small_send(self, values):
        devices = self.n_dp * self.groups
        return lax.all_to_all(values.reshape(devices, -1), self.axes, 0, 0, tiled=True)

    def small_sum(self, pieces):
        return jnp.sum(pieces, axis=0).reshape(-1, 8)

    def scatter_unstack(self, rows, *widths):
        if not self.wide:
            return jnp.split(rows, np.cumsum(widths[:-1]), axis=1)
        out, at, half = [], 0, rows.shape[1] // 2
        for width in widths:
            left = rows[:, at : at + width // 2]
            right = rows[:, half + at : half + at + width // 2]
            out.append(jnp.concatenate([left, right], axis=1))
            at += width // 2
        return out

    def scatter_near(self, deep):
        if not self.wide:
            return deep
        low = lax.axis_index("dl")
        return pick(deep, low, 0).astype(WIDE) + self.hop(pick(deep, 1 - low, 0), "dl", 1).astype(WIDE)

    def scatter_core(self, total):
        if not self.wide:
            return lax.psum_scatter(total, self.axes, scatter_dimension=0, tiled=True).astype(WIDE)
        core, rows = lax.axis_index("c"), total.shape[0] // 2
        away = self.hop(lax.dynamic_slice_in_dim(total, (1 - core) * rows, rows, 0), "c", 1)
        return flipped(core, lax.dynamic_slice_in_dim(total, core * rows, rows, 0), away, 1)

    def plus(self, one, two):
        return (one.astype(WIDE) + two.astype(WIDE)).astype(LOW)

    def fetch_near(self, part):
        upper = lax.axis_index("dh")
        same, other = part[0], part[1]
        same, other = jnp.where(upper == 0, same, other), jnp.where(upper == 0, other, same)
        return flipped(upper, same[None], self.hop(other, "dh", 1)[None], 0)

    def fetch_far(self, pair, *gates):
        pieces = lax.all_gather(after(pair, *gates), "dl", axis=1, tiled=True)
        return pieces.reshape(D, FF)

    def share_far(self, partial, *gates):
        pieces = after(partial, *gates).reshape(2, D // 2, FF)
        return lax.psum_scatter(pieces, "dl", scatter_dimension=1, tiled=True)

    def share_send(self, pair):
        upper = lax.axis_index("dh")
        own = lax.dynamic_index_in_dim(pair, upper, 0)
        return own, self.hop(lax.dynamic_index_in_dim(pair, 1 - upper, 0), "dh", 1)

    def share_sum(self, own, other):
        return flipped(lax.axis_index("dh"), own.astype(WIDE), other.astype(WIDE), 0)

    def to_experts(self, rows):
        chunks = rows.reshape(2 * self.groups, -1, D)
        return lax.all_to_all(chunks, ("dh",) + self.expert, 0, 0, tiled=True).reshape(-1, D)


def after(value, *others):
    return lax.optimization_barrier((value,) + others)[0]


def fenced(ready, body, *operands):
    shapes = jax.eval_shape(body, *operands)
    empty = lambda *_: jax.tree.map(lambda leaf: jnp.zeros(leaf.shape, leaf.dtype), shapes)
    return lax.cond(ready, body, empty, *operands)


def padded(rows, fill=0):
    shaped = rows.reshape(rows.shape[0] // SEQ, SEQ, rows.shape[1])
    return jnp.pad(shaped, ((0, 0), (0, LINES - SEQ), (0, 0)), constant_values=fill)


def unpadded(lines):
    return lines[:, :SEQ].reshape(-1, lines.shape[2])


def flat(lines):
    return lines.reshape(-1, lines.shape[2])


def local(plan, act_in, w_qkv, w_proj, w_up, w_down, norm_gain, norm_shift, exp_in, exp_out, gate, expert_index, cotangent):
    experts_all = EXP_DEV * plan.groups
    capacity = (TOP * TOK_DEV * 5 // (4 * experts_all) + 7) // 8 * 8
    slots = experts_all * capacity
    proj_t = jnp.swapaxes(w_proj, 1, 2).astype(LOW)
    qkv_low = w_qkv.astype(LOW)
    norms = jnp.concatenate([norm_gain, norm_shift]).T.astype(LOW)
    norms = jnp.pad(norms, ((0, 0), (0, 256 - norms.shape[1])))
    part_a = jnp.concatenate([qkv_low[0], proj_t[0], norms], axis=1)
    part_b = jnp.concatenate([w_up.astype(LOW), w_down.T.astype(LOW)], axis=1)
    part_c = jnp.concatenate([qkv_low[1], proj_t[1]], axis=1)
    ready = expert_index[0, 0] >= 0
    bar = lax.optimization_barrier
    core = lax.axis_index("c") if plan.wide else 0 * expert_index[0, 0]
    parts = (part_a, part_b, part_c)
    in_low = exp_in.astype(LOW)
    deep = plan.gather_depth(parts)

    def prepare(expert_index, gate, cotangent, act_in):
        flat_index = expert_index.reshape(-1)
        onehot = (flat_index[:, None] == jnp.arange(experts_all, dtype=jnp.int32)).astype(jnp.int32)
        before = jnp.cumsum(onehot, axis=0) - onehot
        holder = (flat_index % EXP_DEV) * plan.groups + flat_index // EXP_DEV
        spots = (holder * capacity + jnp.sum(onehot * before, axis=1)).reshape(-1, TOP)
        spots = padded(spots, -1)
        gates, cot, x_a = padded(gate), padded(cotangent), padded(act_in)
        grad_sent = dispatch_grad(flat(spots).T, flat(gates), flat(cot), slots)
        return spots, gates, cot, x_a, grad_sent

    spots, gates, cot, x_a, grad_sent = fenced(
        ready, prepare, expert_index, gate, cotangent, act_in
    )
    spot_rows = flat(spots).T

    out_low = jnp.swapaxes(exp_out, 1, 2).astype(LOW)
    in_low, x_a, grad_sent, deep = bar((in_low, x_a, grad_sent, deep))
    in_near = plan.fetch_near(in_low)

    def zeroth_part(deep, parts):
        pair_a, pair_b, pair_c = plan.gather_split(deep, parts)
        one_a = bar(plan.gather_side(pair_a, 0))
        two_a = bar(plan.gather_side(one_a, 1))
        pair_b, two_a = bar((pair_b, two_a))
        four_a, one_b = bar((plan.gather_core(two_a), plan.gather_side(pair_b, 0)))
        return four_a, one_b, pair_c

    four_a, one_b, pair_c = fenced(ready, zeroth_part, deep, parts)
    four_a, in_near, out_low = bar((four_a, in_near, out_low))
    weight_in = plan.fetch_far(in_near)
    out_near = plan.fetch_near(out_low)

    def first_part(four_a, one_b, part_a, x_a):
        block_a = plan.gather_join(four_a, part_a)
        norms = block_a[:, 4 * D : 4 * D + 8].astype(WIDE).T
        gain, shift = norms[:4, None], norms[4:, None]
        x_b, packed_a, mixed_a = attend_forward(x_a, gain[0], shift[0], block_a)
        two_b, x_b = bar((plan.gather_side(one_b, 1), x_b))
        return gain, shift, block_a, x_b, packed_a, mixed_a, two_b

    gain, shift, block_a, x_b, packed_a, mixed_a, two_b = fenced(
        ready, first_part, four_a, one_b, part_a, x_a
    )

    two_b, out_near = bar((two_b, out_near))
    weight_out = plan.fetch_far(out_near)

    def second_part(x_b, gain, shift, two_b, pair_c, part_b, part_c, spot_rows, grad_sent):
        four_b, one_c, grad_sent = bar(
            (plan.gather_core(two_b), plan.gather_side(pair_c, 0), grad_sent)
        )
        grad_rows = plan.to_experts(grad_sent)
        block_b = plan.gather_join(four_b, part_b)
        x_c, hidden_b, slope_b = mlp_forward(x_b, gain[1], shift[1], block_b)
        two_c, x_c = bar((plan.gather_side(one_c, 1), x_c))
        block_c = plan.gather_join(bar(plan.gather_core(two_c)), part_c)
        x_d, packed_c, mixed_c = attend_forward(x_c, gain[2], shift[2], block_c)
        x_d, grad_rows = bar((x_d, grad_rows))
        rows = plan.to_experts(dispatch(spot_rows, flat(x_d), gain[3], shift[3], slots))
        return block_b, block_c, x_c, x_d, hidden_b, slope_b, packed_c, mixed_c, rows, grad_rows

    block_b, block_c, x_c, x_d, hidden_b, slope_b, packed_c, mixed_c, rows, grad_rows = fenced(
        ready, second_part, x_b, gain, shift, two_b, pair_c, part_b, part_c, spot_rows, grad_sent
    )
    hidden, slope = expert_forward(rows, weight_in)


    def experts_backward(grad_rows, hidden, slope, weight_in, weight_out):
        dinner, droutes = expert_backward(grad_rows, slope, weight_in, weight_out)
        (down_partial,) = weight_grad(False, core, (grad_rows, after(hidden, droutes)))
        return dinner, droutes, down_partial

    dinner, droutes, down_partial = fenced(
        ready, experts_backward, grad_rows, hidden, slope, weight_in, weight_out
    )
    down_pair = plan.share_far(down_partial)

    def experts_return(rows, dinner, droutes, hidden, weight_out):
        routes_home = plan.to_experts(droutes)
        (in_partial,) = weight_grad(False, core, (rows, dinner))
        result = mm_t(after(hidden, in_partial), weight_out).astype(LOW)
        routes_home, result = bar((routes_home, result))
        return routes_home, in_partial, result

    routes_home, in_partial, result = fenced(
        ready, experts_return, rows, dinner, droutes, hidden, weight_out
    )
    in_pair = plan.share_far(in_partial)
    home = plan.to_experts(after(result, routes_home))

    def third_part(gain, shift, block_c, x_c, x_d, packed_c, mixed_c, spots, cot, routes_home):
        dx_d, gain_d, shift_d = return_grad(spots, x_d, cot, gain[3], routes_home)
        dx_c, dpacked_c, normed_c, low_c, gain_c, shift_c = attend_backward(
            x_c, dx_d, packed_c, gain[2], shift[2], block_c
        )
        sum_c = weight_grad(
            plan.wide, core, (flat(normed_c), flat(dpacked_c)), (flat(low_c), flat(mixed_c))
        )
        return sum_c, dx_c, (gain_c, gain_d), (shift_c, shift_d)

    sum_c, dx_c, gains, shifts = fenced(
        ready, third_part, gain, shift, block_c, x_c, x_d, packed_c, mixed_c, spots, cot, routes_home
    )
    dx_c, down_pair = bar((dx_c, down_pair))
    down_own, down_other = plan.share_send(down_pair)

    def fourth_part(gain, shift, block_b, x_b, dx_c, sum_c, hidden_b, slope_b):
        dx_b, dinner_b, normed_b, low_b, gain_b, shift_b = mlp_backward(
            x_b, dx_c, slope_b, gain[1], shift[1], block_b
        )
        pair_c, dx_b, dinner_b = bar((plan.scatter_swap(sum_c), dx_b, dinner_b))
        sum_b = weight_grad(
            plan.wide, core, (flat(normed_b), flat(dinner_b)), (flat(low_b), flat(hidden_b))
        )
        pair_c, sum_b = bar((plan.scatter_side(pair_c, 0), sum_b))
        pair_c, pair_b = bar((plan.scatter_side(pair_c, 1), plan.scatter_swap(sum_b)))
        return pair_c, pair_b, dx_b, gain_b, shift_b

    pair_c, pair_b, dx_b, gain_b, shift_b = fenced(
        ready, fourth_part, gain, shift, block_b, x_b, dx_c, sum_c, hidden_b, slope_b
    )
    dx_b, home, down_other = bar((dx_b, home, down_other))

    def attend_part(gain, shift, block_a, x_a, packed_a, mixed_a, pair_b, dx_b):
        dx_a, dpacked_a, normed_a, low_a, gain_a, shift_a = attend_backward(
            x_a, dx_b, packed_a, gain[0], shift[0], block_a
        )
        pair_b, dx_a = bar((plan.scatter_side(pair_b, 0), dx_a))
        return dx_a, dpacked_a, normed_a, low_a, gain_a, shift_a, pair_b

    dx_a, dpacked_a, normed_a, low_a, gain_a, shift_a, pair_b = fenced(
        ready, attend_part, gain, shift, block_a, x_a, packed_a, mixed_a, pair_b, dx_b
    )
    pair_b, in_pair = bar((pair_b, in_pair))
    in_own, in_other = plan.share_send(in_pair)

    def combine_part(dpacked_a, normed_a, low_a, mixed_a, pair_b, pair_c, norms, x_d, spots, gates, cot, home):
        norm_grads = jnp.concatenate(norms).T
        act_out, grad_gate = combine(spots, gates, x_d, cot, home)
        sum_a = weight_grad(
            plan.wide, core, (flat(normed_a), flat(dpacked_a)), (flat(low_a), flat(mixed_a))
        )
        pair_b, sum_a, act_out = bar((plan.scatter_side(pair_b, 1), sum_a, act_out))
        return norm_grads, sum_a, plan.scatter_stack(pair_b, pair_c), act_out, grad_gate

    norm_grads, sum_a, deep_bc, act_out, grad_gate = fenced(
        ready, combine_part, dpacked_a, normed_a, low_a, mixed_a, pair_b, pair_c,
        (gain_a, gain_b) + gains + (shift_a, shift_b) + shifts, x_d, spots, gates, cot, home,
    )
    own_bc, far_bc = plan.scatter_send(deep_bc)


    def fifth_part(sum_a, act_out, grad_gate, dx_a):
        pair_a = bar(plan.scatter_swap(sum_a))
        pair_a = bar(plan.scatter_side(pair_a, 0))
        deep_a = plan.scatter_stack(plan.scatter_side(pair_a, 1))
        return deep_a, unpadded(act_out), unpadded(grad_gate), unpadded(dx_a)

    deep_a, act_out, grad_gate, dx_a = fenced(
        ready, fifth_part, sum_a, act_out, grad_gate, dx_a
    )
    deep_a, own_bc, far_bc, in_other = bar((deep_a, own_bc, far_bc, in_other))

    def sixth_part(deep_a, own_bc, far_bc, norm_grads, shares):
        norm_pieces = plan.small_send(norm_grads)
        own_a, far_a = plan.scatter_send(deep_a)
        near_bc = plan.scatter_near(plan.scatter_add(own_bc, far_bc))
        near_bc, far_a = bar((near_bc, far_a))
        grad_exp_in, grad_exp_out = [plan.share_sum(*share) for share in shares]
        near_a, mine_bc = bar(
            (plan.scatter_near(plan.scatter_add(own_a, far_a)), plan.scatter_core(near_bc))
        )
        mine_norms = plan.small_sum(norm_pieces)
        return plan.scatter_core(near_a), mine_bc, mine_norms, grad_exp_in, grad_exp_out

    mine_a, mine_bc, mine_norms, grad_exp_in, grad_exp_out = fenced(
        ready, sixth_part, deep_a, own_bc, far_bc, norm_grads,
        ((in_own, in_other), (down_own, down_other)),
    )
    mine_b, mine_c = plan.scatter_unstack(mine_bc, 2 * FF, 4 * D)
    grad_exp_out = jnp.swapaxes(grad_exp_out, 1, 2)

    grad_qkv = jnp.stack([mine_a[:, : 3 * D], mine_c[:, : 3 * D]])
    grad_proj = jnp.stack([mine_a[:, 3 * D :], mine_c[:, 3 * D :]])
    return (
        act_out,
        dx_a,
        grad_qkv,
        jnp.swapaxes(grad_proj, 1, 2),
        mine_b[:, :FF],
        mine_b[:, FF:].T,
        mine_norms[:, :4].T,
        mine_norms[:, 4:].T,
        grad_exp_in,
        grad_exp_out,
        grad_gate,
    )


def solution(mesh):
    plan = Plan(mesh)
    rows, dp, expert = plan.axes, plan.dp, plan.expert
    in_specs = (
        P(rows, None),
        P(None, rows, None),
        P(None, None, rows),
        P(rows, None),
        P(None, rows),
        P(None, rows),
        P(None, rows),
        P(expert, dp, None),
        P(expert, None, dp),
        P(rows, None),
        P(rows, None),
        P(rows, None),
    )
    out_specs = (
        P(rows, None),
        P(rows, None),
        P(None, rows, None),
        P(None, None, rows),
        P(rows, None),
        P(None, rows),
        P(None, rows),
        P(None, rows),
        P(expert, dp, None),
        P(expert, None, dp),
        P(rows, None),
    )
    return jax.shard_map(
        functools.partial(local, plan),
        mesh=plan.mesh,
        in_specs=in_specs,
        out_specs=out_specs,
        check_vma=False,
    )
```

```python
import functools
import math

import jax
import jax.numpy as jnp
import numpy as np
from jax import lax
from jax.experimental import pallas as pl
from jax.experimental.pallas import tpu as pltpu
from jax.sharding import Mesh, PartitionSpec as P

D = 768
FF = 3072
HEADS = 12
HEAD = 64
SEQ = 197
LINES = 208
TOP = 2
EXP_DEV = 2
TOK_DEV = 591
EPS = 1e-06
LOW = jnp.bfloat16
WIDE = jnp.float32
SCALE = 1.0 / math.sqrt(HEAD)
RSQRT2 = 1.0 / math.sqrt(2.0)
RSQRT2PI = 1.0 / math.sqrt(2.0 * math.pi)
SLOT_TILE = 256
ROW_TILE = 256
WIDTH_TILE = 768
HINT = 4


def mm(left, right):
    return jnp.dot(left, right, preferred_element_type=WIDE)


def mm_t(left, right):
    return lax.dot_general(left, right, (((1,), (1,)), ((), ())), preferred_element_type=WIDE)


def t_mm(left, right):
    return lax.dot_general(left, right, (((0,), (0,)), ((), ())), preferred_element_type=WIDE)


def norm_parts(inputs):
    average = jnp.mean(inputs, axis=-1, keepdims=True)
    centred = inputs - average
    spread = jnp.mean(centred * centred, axis=-1, keepdims=True)
    inverse = lax.rsqrt(spread + EPS)
    return centred * inverse, inverse


def norm_low(inputs, gain_ref, shift_ref):
    xhat, _ = norm_parts(inputs)
    return (xhat * gain_ref[...] + shift_ref[...]).astype(LOW)


def norm_backward(dnormed, xhat, inverse, gain_ref, residual, dx_ref, dgain_ref, dshift_ref):
    scaled = dnormed * gain_ref[...]
    mean = jnp.mean(scaled, axis=-1, keepdims=True)
    tilt = jnp.mean(scaled * xhat, axis=-1, keepdims=True)
    dx_ref[0] = residual + inverse * (scaled - mean - xhat * tilt)

    @pl.when(pl.program_id(0) == 0)
    def _():
        dgain_ref[...] = jnp.zeros_like(dgain_ref)
        dshift_ref[...] = jnp.zeros_like(dshift_ref)

    dgain_ref[...] += jnp.sum(dnormed * xhat, axis=0, keepdims=True)
    dshift_ref[...] += jnp.sum(dnormed, axis=0, keepdims=True)


def gelu_both(inner):
    phi = 0.5 + 0.5 * lax.erf(inner * RSQRT2)
    slope = phi + inner * (RSQRT2PI * jnp.exp(-0.5 * inner * inner))
    return (inner * phi).astype(LOW), slope.astype(LOW)


def softmax_rows(query, key):
    scores = mm_t(query, key) * SCALE
    lane = lax.broadcasted_iota(jnp.int32, scores.shape, 1)
    scores = jnp.where(lane < SEQ, scores, -jnp.inf)
    peak = jnp.max(scores, axis=-1, keepdims=True)
    raised = jnp.exp(scores - peak)
    total = jnp.sum(raised, axis=-1, keepdims=True)
    return raised * (1.0 / total)


def whole(shape):
    return pl.BlockSpec(shape, lambda *_: (0,) * len(shape))


def window(width, at):
    return pl.BlockSpec((D, width), lambda *_: (0, at))


def image(width):
    return pl.BlockSpec((1, LINES, width), lambda i: (i, 0, 0))


def params(megabytes):
    return pltpu.CompilerParams(vmem_limit_bytes=megabytes << 20)


def like(shape, kind):
    return jax.ShapeDtypeStruct(shape, kind)


def cost(flops, moved, raised=0):
    return pl.CostEstimate(
        flops=flops // HINT, bytes_accessed=moved // HINT, transcendentals=raised // HINT
    )


def attend_forward_body(x_ref, gain_ref, shift_ref, qkv_ref, proj_ref, out_ref, packed_ref, mixed_ref):
    x = x_ref[0]
    packed_ref[0] = mm(norm_low(x, gain_ref, shift_ref), qkv_ref[...]).astype(LOW)
    first = lax.broadcasted_iota(jnp.int32, (LINES, 2 * HEAD), 1) < HEAD
    zero = jnp.zeros((LINES, 2 * HEAD), LOW)
    for pair in range(HEADS // 2):
        at = pair * 2 * HEAD
        query = packed_ref[0, :, at : at + 2 * HEAD]
        key = packed_ref[0, :, D + at : D + at + 2 * HEAD]
        value = packed_ref[0, :, 2 * D + at : 2 * D + at + 2 * HEAD]
        low = mm(softmax_rows(jnp.where(first, query, zero), key).astype(LOW), value)
        high = mm(softmax_rows(jnp.where(first, zero, query), key).astype(LOW), value)
        mixed_ref[0, :, at : at + 2 * HEAD] = jnp.where(first, low, high).astype(LOW)
    out_ref[0] = x + mm_t(mixed_ref[0], proj_ref[...])


def attend_forward(x, gain, shift, block):
    images = x.shape[0]
    return pl.pallas_call(
        attend_forward_body,
        grid=(images,),
        in_specs=[image(D), whole((1, D)), whole((1, D)), window(3 * D, 0), window(D, 3)],
        out_specs=[image(D), image(3 * D), image(D)],
        out_shape=[
            like((images, LINES, D), WIDE),
            like((images, LINES, 3 * D), LOW),
            like((images, LINES, D), LOW),
        ],
        compiler_params=params(48),
        cost_estimate=cost(3_700_000_000, 13_000_000, 1_600_000),
        name="attend_forward",
    )(x, gain, shift, block, block)


def attend_backward_body(
    x_ref, dy_ref, packed_ref, gain_ref, shift_ref, qkv_ref, proj_ref,
    dx_ref, dpacked_ref, normed_ref, low_ref, dgain_ref, dshift_ref,
    dmixed_ref,
):
    dy = dy_ref[0]
    grad_low = dy.astype(LOW)
    low_ref[0] = grad_low
    dmixed_ref[...] = mm(grad_low, proj_ref[...]).astype(LOW)
    first = lax.broadcasted_iota(jnp.int32, (LINES, 2 * HEAD), 1) < HEAD
    zero = jnp.zeros((LINES, 2 * HEAD), LOW)

    def one(query, key, value, upstream):
        probs = softmax_rows(query, key)
        dprobs = mm_t(upstream, value)
        inner = jnp.sum(probs * dprobs, axis=-1, keepdims=True)
        dscores = (probs * (dprobs - inner)).astype(LOW)
        return t_mm(probs.astype(LOW), upstream), mm(dscores, key), t_mm(dscores, query)

    for pair in range(HEADS // 2):
        at = pair * 2 * HEAD
        query = packed_ref[0, :, at : at + 2 * HEAD]
        key = packed_ref[0, :, D + at : D + at + 2 * HEAD]
        value = packed_ref[0, :, 2 * D + at : 2 * D + at + 2 * HEAD]
        upstream = dmixed_ref[:, at : at + 2 * HEAD]
        dv0, dq0, dk0 = one(
            jnp.where(first, query, zero), key, value, jnp.where(first, upstream, zero)
        )
        dv1, dq1, dk1 = one(
            jnp.where(first, zero, query), key, value, jnp.where(first, zero, upstream)
        )
        dpacked_ref[0, :, at : at + 2 * HEAD] = (jnp.where(first, dq0, dq1) * SCALE).astype(LOW)
        dpacked_ref[0, :, D + at : D + at + 2 * HEAD] = ((dk0 + dk1) * SCALE).astype(LOW)
        dpacked_ref[0, :, 2 * D + at : 2 * D + at + 2 * HEAD] = (dv0 + dv1).astype(LOW)
    xhat, inverse = norm_parts(x_ref[0])
    normed_ref[0] = (xhat * gain_ref[...] + shift_ref[...]).astype(LOW)
    dnormed = mm_t(dpacked_ref[0], qkv_ref[...])
    norm_backward(dnormed, xhat, inverse, gain_ref, dy, dx_ref, dgain_ref, dshift_ref)


def attend_backward(x, dy, packed, gain, shift, block):
    images = x.shape[0]
    return pl.pallas_call(
        attend_backward_body,
        grid=(images,),
        in_specs=[
            image(D), image(D), image(3 * D), whole((1, D)), whole((1, D)),
            window(3 * D, 0), window(D, 3),
        ],
        out_specs=[image(D), image(3 * D), image(D), image(D), whole((1, D)), whole((1, D))],
        out_shape=[
            like((images, LINES, D), WIDE),
            like((images, LINES, 3 * D), LOW),
            like((images, LINES, D), LOW),
            like((images, LINES, D), LOW),
            like((1, D), WIDE),
            like((1, D), WIDE),
        ],
        scratch_shapes=[pltpu.VMEM((LINES, D), LOW)],
        compiler_params=params(48),
        cost_estimate=cost(4_000_000_000, 22_000_000, 1_600_000),
        name="attend_backward",
    )(x, dy, packed, gain, shift, block, block)


def mlp_forward_body(x_ref, gain_ref, shift_ref, up_ref, down_ref, out_ref, hidden_ref, slope_ref):
    x = x_ref[0]
    normed = norm_low(x, gain_ref, shift_ref)
    total = x
    step = FF // 4
    for at in range(0, FF, step):
        hidden, slope = gelu_both(mm(normed, up_ref[:, at : at + step]))
        hidden_ref[0, :, at : at + step] = hidden
        slope_ref[0, :, at : at + step] = slope
        total = total + mm_t(hidden, down_ref[:, at : at + step])
    out_ref[0] = total


def mlp_forward(x, gain, shift, block):
    images = x.shape[0]
    return pl.pallas_call(
        mlp_forward_body,
        grid=(images,),
        in_specs=[image(D), whole((1, D)), whole((1, D)), window(FF, 0), window(FF, 1)],
        out_specs=[image(D), image(FF), image(FF)],
        out_shape=[
            like((images, LINES, D), WIDE),
            like((images, LINES, FF), LOW),
            like((images, LINES, FF), LOW),
        ],
        compiler_params=params(56),
        cost_estimate=cost(5_900_000_000, 21_000_000, 4_000_000),
        name="mlp_forward",
    )(x, gain, shift, block, block)


def mlp_backward_body(
    x_ref, dy_ref, slope_ref, gain_ref, shift_ref, up_ref, down_ref,
    dx_ref, dinner_ref, normed_ref, low_ref, dgain_ref, dshift_ref,
):
    dy = dy_ref[0]
    grad_low = dy.astype(LOW)
    low_ref[0] = grad_low
    step = FF // 4
    dnormed = jnp.zeros((LINES, D), WIDE)
    for at in range(0, FF, step):
        dhidden = mm(grad_low, down_ref[:, at : at + step])
        dinner = (dhidden * slope_ref[0, :, at : at + step].astype(WIDE)).astype(LOW)
        dinner_ref[0, :, at : at + step] = dinner
        dnormed = dnormed + mm_t(dinner, up_ref[:, at : at + step])
    xhat, inverse = norm_parts(x_ref[0])
    normed_ref[0] = (xhat * gain_ref[...] + shift_ref[...]).astype(LOW)
    norm_backward(dnormed, xhat, inverse, gain_ref, dy, dx_ref, dgain_ref, dshift_ref)


def mlp_backward(x, dy, slope, gain, shift, block):
    images = x.shape[0]
    return pl.pallas_call(
        mlp_backward_body,
        grid=(images,),
        in_specs=[
            image(D), image(D), image(FF), whole((1, D)), whole((1, D)),
            window(FF, 0), window(FF, 1),
        ],
        out_specs=[image(D), image(FF), image(D), image(D), whole((1, D)), whole((1, D))],
        out_shape=[
            like((images, LINES, D), WIDE),
            like((images, LINES, FF), LOW),
            like((images, LINES, D), LOW),
            like((images, LINES, D), LOW),
            like((1, D), WIDE),
            like((1, D), WIDE),
        ],
        compiler_params=params(56),
        cost_estimate=cost(5_900_000_000, 25_000_000),
        name="mlp_backward",
    )(x, dy, slope, gain, shift, block, block)


def chosen(places_ref, tile):
    tokens = places_ref.shape[1]
    slot = pl.program_id(0) * tile + lax.broadcasted_iota(jnp.int32, (tile, tokens), 0)
    return [jnp.where(slot == places_ref[k : k + 1, :], 1.0, 0.0) for k in range(TOP)]


def dispatch_body(places_ref, x_ref, gain_ref, shift_ref, out_ref, sent_ref):
    @pl.when(pl.program_id(0) == 0)
    def _():
        sent_ref[...] = norm_low(x_ref[...], gain_ref, shift_ref)

    picks = chosen(places_ref, SLOT_TILE)
    out_ref[...] = mm((picks[0] + picks[1]).astype(LOW), sent_ref[...]).astype(LOW)


def dispatch(places, x, gain, shift, slots):
    tokens = x.shape[0]
    return pl.pallas_call(
        dispatch_body,
        grid=(slots // SLOT_TILE,),
        in_specs=[whole((TOP, tokens)), whole((tokens, D)), whole((1, D)), whole((1, D))],
        out_specs=pl.BlockSpec((SLOT_TILE, D), lambda i: (i, 0)),
        out_shape=like((slots, D), LOW),
        scratch_shapes=[pltpu.VMEM((tokens, D), LOW)],
        compiler_params=params(32),
        cost_estimate=cost(1_500_000_000, 4_500_000),
        name="dispatch",
    )(places, x, gain, shift)


def dispatch_grad_body(places_ref, gate_ref, cot_ref, out_ref, sent_ref):
    @pl.when(pl.program_id(0) == 0)
    def _():
        for k in range(TOP):
            sent_ref[k] = (gate_ref[:, k : k + 1] * cot_ref[...]).astype(LOW)

    picks = chosen(places_ref, SLOT_TILE)
    total = mm(picks[0].astype(LOW), sent_ref[0]) + mm(picks[1].astype(LOW), sent_ref[1])
    out_ref[...] = total.astype(LOW)


def dispatch_grad(places, gate, cot, slots):
    tokens = cot.shape[0]
    return pl.pallas_call(
        dispatch_grad_body,
        grid=(slots // SLOT_TILE,),
        in_specs=[whole((TOP, tokens)), whole((tokens, TOP)), whole((tokens, D))],
        out_specs=pl.BlockSpec((SLOT_TILE, D), lambda i: (i, 0)),
        out_shape=like((slots, D), LOW),
        scratch_shapes=[pltpu.VMEM((TOP, tokens, D), LOW)],
        compiler_params=params(32),
        cost_estimate=cost(3_000_000_000, 4_500_000),
        name="dispatch_grad",
    )(places, gate, cot)


def picker(places_ref, k, slots):
    lane = lax.broadcasted_iota(jnp.int32, (LINES, slots), 1)
    return jnp.where(lane == places_ref[0, :, k : k + 1], 1.0, 0.0)


def combine_body(places_ref, gate_ref, x_ref, cot_ref, home_ref, out_ref, dgate_ref):
    slots = home_ref.shape[0]
    total = x_ref[0]
    for k in range(TOP):
        picked = mm(picker(places_ref, k, slots).astype(LOW), home_ref[...])
        total = total + gate_ref[0, :, k : k + 1] * picked
        dgate_ref[0, :, k : k + 1] = jnp.sum(cot_ref[0] * picked, axis=-1, keepdims=True)
    out_ref[0] = total


def combine(places, gate, x, cot, home):
    images, slots = x.shape[0], home.shape[0]
    return pl.pallas_call(
        combine_body,
        grid=(images,),
        in_specs=[image(TOP), image(TOP), image(D), image(D), whole((slots, D))],
        out_specs=[image(D), image(TOP)],
        out_shape=[like((images, LINES, D), WIDE), like((images, LINES, TOP), WIDE)],
        compiler_params=params(32),
        cost_estimate=cost(3_000_000_000, 8_000_000),
        name="combine",
    )(places, gate, x, cot, home)


def return_grad_body(places_ref, x_ref, cot_ref, gain_ref, home_ref, dx_ref, dgain_ref, dshift_ref):
    slots = home_ref.shape[0]
    picks = (picker(places_ref, 0, slots) + picker(places_ref, 1, slots)).astype(LOW)
    dsent = mm(picks, home_ref[...])
    xhat, inverse = norm_parts(x_ref[0])
    norm_backward(dsent, xhat, inverse, gain_ref, cot_ref[0], dx_ref, dgain_ref, dshift_ref)


def return_grad(places, x, cot, gain, home):
    images, slots = x.shape[0], home.shape[0]
    return pl.pallas_call(
        return_grad_body,
        grid=(images,),
        in_specs=[image(TOP), image(D), image(D), whole((1, D)), whole((slots, D))],
        out_specs=[image(D), whole((1, D)), whole((1, D))],
        out_shape=[like((images, LINES, D), WIDE), like((1, D), WIDE), like((1, D), WIDE)],
        compiler_params=params(32),
        cost_estimate=cost(1_500_000_000, 8_000_000),
        name="return_grad",
    )(places, x, cot, gain, home)


def expert_forward_body(rows_ref, in_ref, hidden_ref, slope_ref):
    step = FF // 4
    for at in range(0, FF, step):
        hidden, slope = gelu_both(mm(rows_ref[...], in_ref[:, at : at + step]))
        hidden_ref[:, at : at + step] = hidden
        slope_ref[:, at : at + step] = slope


def tiled(width):
    return pl.BlockSpec((ROW_TILE, width), lambda i: (i, 0))


def expert_forward(rows, weight):
    count = rows.shape[0]
    return pl.pallas_call(
        expert_forward_body,
        grid=(count // ROW_TILE,),
        in_specs=[tiled(D), whole((D, FF))],
        out_specs=[tiled(FF), tiled(FF)],
        out_shape=[like((count, FF), LOW), like((count, FF), LOW)],
        compiler_params=params(48),
        cost_estimate=cost(7_200_000_000, 26_000_000, 9_000_000),
        name="expert_forward",
    )(rows, weight)


def expert_backward_body(grad_ref, slope_ref, in_ref, out_ref, dinner_ref, dx_ref):
    step = FF // 4
    total = jnp.zeros((ROW_TILE, D), WIDE)
    for at in range(0, FF, step):
        dhidden = mm(grad_ref[...], out_ref[:, at : at + step])
        dinner = (dhidden * slope_ref[:, at : at + step].astype(WIDE)).astype(LOW)
        dinner_ref[:, at : at + step] = dinner
        total = total + mm_t(dinner, in_ref[:, at : at + step])
    dx_ref[...] = total.astype(LOW)


def expert_backward(grad, slope, weight_in, weight_out_t):
    count = grad.shape[0]
    return pl.pallas_call(
        expert_backward_body,
        grid=(count // ROW_TILE,),
        in_specs=[tiled(D), tiled(FF), whole((D, FF)), whole((D, FF))],
        out_specs=[tiled(FF), tiled(D)],
        out_shape=[like((count, FF), LOW), like((count, D), LOW)],
        compiler_params=params(48),
        cost_estimate=cost(14_400_000_000, 33_000_000),
        name="expert_backward",
    )(grad, slope, weight_in, weight_out_t)


def weight_grad_body(tiles, starts, split, at_ref, *refs):
    count = len(starts)
    lefts, rights = refs[:count], refs[count : 2 * count]
    outs, turned = refs[2 * count : -count], refs[-count:]
    step = pl.program_id(0)
    tile = lax.rem(step + at_ref[0], tiles)

    @pl.when(step == 0)
    def _():
        for left, scratch in zip(lefts, turned):
            scratch[...] = left[...].T

    for index, (left, right) in enumerate(zip(turned, rights)):
        stop = (starts + (tiles,))[index + 1]

        @pl.when((tile >= starts[index]) & (tile < stop))
        def _(left=left, right=right):
            value = mm(left[...], right[...]).astype(LOW)
            if split:

                @pl.when(step < tiles // 2)
                def _():
                    outs[0][...] = value

                @pl.when(step >= tiles // 2)
                def _():
                    outs[1][...] = value
            else:
                outs[0][...] = value


def weight_grad(split, core, *pairs):
    width = WIDTH_TILE
    tokens = pairs[0][0].shape[0]
    counts = [right.shape[1] // width for _, right in pairs]
    starts = tuple(int(n) for n in np.cumsum([0] + counts[:-1]))
    tiles = sum(counts)
    first = ((1 - core) * (tiles // 2) if split else 0 * core).astype(jnp.int32).reshape(1)

    def right_spec(start, count):
        def at(step, at_ref):
            return 0, jnp.clip(lax.rem(step + at_ref[0], tiles) - start, 0, count - 1)

        return pl.BlockSpec((tokens, width), at)

    half = tiles // 2
    if split:
        out_specs = [
            pl.BlockSpec((D, width), lambda step, _: (0, jnp.minimum(step, half - 1))),
            pl.BlockSpec((D, width), lambda step, _: (0, jnp.maximum(step - half, 0))),
        ]
        out_shape = [like((D, half * width), LOW)] * 2
    else:
        out_specs = [pl.BlockSpec((D, width), lambda step, _: (0, step))]
        out_shape = [like((D, tiles * width), LOW)]
    return pl.pallas_call(
        functools.partial(weight_grad_body, tiles, starts, split),
        grid_spec=pltpu.PrefetchScalarGridSpec(
            num_scalar_prefetch=1,
            grid=(tiles,),
            in_specs=[whole((tokens, D)) for _ in pairs]
            + [right_spec(start, count) for start, count in zip(starts, counts)],
            out_specs=out_specs,
            scratch_shapes=[pltpu.VMEM((D, tokens), LOW) for _ in pairs],
        ),
        out_shape=out_shape,
        compiler_params=params(48),
        cost_estimate=cost(2 * D * tokens * tiles * width, 3 * D * tiles * width),
        name="weight_grad",
    )(first, *[left for left, _ in pairs], *[right for _, right in pairs])


def join_body(at_ref, *refs):
    *parts, out_ref, sem = refs
    for index, part in enumerate(parts):
        rows, width = part.shape[1:]
        for block in range(part.shape[0]):
            down = pl.multiple_of(at_ref[index, 2 * block] * 16, 16)
            right = pl.multiple_of(at_ref[index, 2 * block + 1] * 128, 128)
            target = out_ref.at[pl.ds(down, rows), pl.ds(right, width)]
            pltpu.make_async_copy(part.at[block], target, sem).start()
    pltpu.make_async_copy(out_ref, out_ref, sem).wait()


def join(places, parts, width):
    return pl.pallas_call(
        join_body,
        in_specs=[pl.BlockSpec(memory_space=pltpu.SMEM)]
        + [pl.BlockSpec(memory_space=pl.ANY)] * len(parts),
        out_specs=pl.BlockSpec(memory_space=pltpu.VMEM),
        out_shape=like((D, width), LOW),
        scratch_shapes=[pltpu.SemaphoreType.DMA],
        compiler_params=params(32),
        cost_estimate=cost(0, 4 * D * width),
        name="join",
    )(places, *parts)


def pick(value, at, axis):
    return lax.dynamic_index_in_dim(value, at, axis, keepdims=False)


def flipped(index, first, second, axis):
    return jnp.where(
        index == 0,
        jnp.concatenate([first, second], axis=axis),
        jnp.concatenate([second, first], axis=axis),
    )


class Plan:
    def __init__(self, mesh):
        n_dp, n_expert = mesh.devices.shape
        self.n_dp, self.groups = n_dp, n_expert
        self.wide = (n_dp, n_expert) == (4, 8)
        expert_shape, expert = ((2, 2, 2), ("y", "x", "c")) if self.wide else ((n_expert,), ("expert",))
        self.dp = ("dh", "dl")
        self.expert = expert
        self.axes = self.dp + expert
        self.mesh = Mesh(mesh.devices.reshape((2, n_dp // 2) + expert_shape), self.axes)

    def hop(self, value, axes, bit):
        size = lax.axis_size(axes)
        return lax.ppermute(value, axes, [(i, i ^ bit) for i in range(size)])

    def gather_depth(self, parts, *gates):
        parts = after(tuple(parts), *gates)
        if not self.wide:
            return jnp.concatenate(parts, axis=1)
        core = lax.axis_index("c")
        sides = [
            jnp.concatenate(
                [
                    lax.dynamic_slice_in_dim(part, side * self.cut(part)[0], self.cut(part)[0], 1)
                    for part in parts
                ],
                axis=1,
            )
            for side in (core, 1 - core)
        ]
        mine = flipped(core, sides[0], self.hop(sides[1], "c", 1), 0)
        return lax.all_gather(mine[None], self.dp, axis=0, tiled=True)

    def gather_split(self, deep, parts):
        if not self.wide:
            ends = np.cumsum([part.shape[1] for part in parts])
            return [deep[:, end - part.shape[1] : end] for end, part in zip(ends, parts)]
        pairs, at = [], 0
        for part in parts:
            half, quarter = self.cut(part)
            pairs.append((deep[:, :, at : at + quarter], deep[:, :, at + quarter : at + half]))
            at += half
        return pairs

    def cut(self, part):
        return part.shape[1] // 2, part.shape[1] // 512 * 128

    def gather_side(self, pair, step):
        if not self.wide:
            return pair
        left, right = lax.optimization_barrier(tuple(pair))
        axes = ("x", "y") if step == 0 else ("y", "x")
        came = lax.optimization_barrier((self.hop(left, axes[0], 1), self.hop(right, axes[1], 1)))
        return tuple(jnp.concatenate([own, new]) for own, new in zip((left, right), came))

    def gather_core(self, pair):
        if not self.wide:
            return pair
        return tuple(pair) + tuple(self.hop(value, "c", 1) for value in pair)

    def gather_join(self, four, part):
        if not self.wide:
            return lax.all_gather(four, self.axes, axis=0, tiled=True)
        rows, width = part.shape
        half, quarter = self.cut(part)
        core = lax.axis_index("c")
        steps = jnp.arange(16, dtype=jnp.int32)
        me = lax.axis_index("y") * 2 + lax.axis_index("x")
        first, second, turn = steps // 8, steps // 4 % 2, steps % 4
        left_at = (turn * 4 + first * 2 + second) ^ me
        right_at = (turn * 4 + second * 2 + first) ^ me

        def spots(at, side, side_core):
            across = jnp.broadcast_to((side_core * half + side * quarter) // 128, at.shape)
            return jnp.stack([at * (2 * rows // 16), across], axis=1).reshape(-1)

        places = jnp.stack(
            [
                spots(left_at, 0, core),
                spots(right_at, 1, core),
                spots(left_at, 0, 1 - core),
                spots(right_at, 1, 1 - core),
            ]
        ).astype(jnp.int32)
        return join(places, four, width)

    def scatter_swap(self, halves):
        if not self.wide:
            return halves[0]
        other, mine = halves
        height, half = mine.shape
        quarter = half // 256 * 128
        mine = self.plus(mine, self.hop(other, "c", 1))
        mine = mine.reshape(self.n_dp, 2, 2, height // 16, half)
        return mine[..., :quarter], mine[..., quarter:]

    def scatter_side(self, pair, step):
        if not self.wide:
            return pair
        y, x = lax.axis_index("y"), lax.axis_index("x")
        turns = ((("y", y, 1), ("x", x, 2)), (("x", x, 1), ("y", y, 1)))[step]
        kept = [pick(value, at, axis) for value, (_, at, axis) in zip(pair, turns)]
        sent = [pick(value, 1 - at, axis) for value, (_, at, axis) in zip(pair, turns)]
        sent = lax.optimization_barrier(tuple(sent))
        came = [self.hop(value, name, 1) for value, (name, _, _) in zip(sent, turns)]
        came = lax.optimization_barrier(tuple(came))
        return tuple(self.plus(one, two) for one, two in zip(kept, came))

    def scatter_stack(self, *pairs):
        if not self.wide:
            return jnp.concatenate(pairs, axis=1)
        return jnp.concatenate([value for pair in pairs for value in pair], axis=2)

    def scatter_send(self, deep):
        if not self.wide:
            return deep, deep[:1, :1]
        deep = deep.reshape((2, 2) + deep.shape[1:])
        high = lax.axis_index("dh")
        return pick(deep, high, 0), self.hop(pick(deep, 1 - high, 0), "dh", 1)

    def scatter_add(self, own, far):
        return self.plus(own, far) if self.wide else own

    def small_send(self, values):
        devices = self.n_dp * self.groups
        return lax.all_to_all(values.reshape(devices, -1), self.axes, 0, 0, tiled=True)

    def small_sum(self, pieces):
        return jnp.sum(pieces, axis=0).reshape(-1, 8)

    def scatter_join(self, *values):
        return jnp.concatenate(values, axis=1)

    def scatter_unstack(self, rows, *widths):
        if not self.wide:
            return jnp.split(rows, np.cumsum(widths[:-1]), axis=1)
        out, at, half = [], 0, rows.shape[1] // 2
        for width in widths:
            left = rows[:, at : at + width // 2]
            right = rows[:, half + at : half + at + width // 2]
            out.append(jnp.concatenate([left, right], axis=1))
            at += width // 2
        return out

    def scatter_near(self, deep):
        if not self.wide:
            return deep
        low = lax.axis_index("dl")
        return pick(deep, low, 0).astype(WIDE) + self.hop(pick(deep, 1 - low, 0), "dl", 1).astype(WIDE)

    def scatter_core(self, total):
        if not self.wide:
            return lax.psum_scatter(total, self.axes, scatter_dimension=0, tiled=True).astype(WIDE)
        core, rows = lax.axis_index("c"), total.shape[0] // 2
        away = self.hop(lax.dynamic_slice_in_dim(total, (1 - core) * rows, rows, 0), "c", 1)
        return flipped(core, lax.dynamic_slice_in_dim(total, core * rows, rows, 0), away, 1)

    def plus(self, one, two):
        return (one.astype(WIDE) + two.astype(WIDE)).astype(LOW)

    def fetch_near(self, part):
        upper = lax.axis_index("dh")
        same, other = part[0], part[1]
        same, other = jnp.where(upper == 0, same, other), jnp.where(upper == 0, other, same)
        return flipped(upper, same[None], self.hop(other, "dh", 1)[None], 0)

    def fetch_far(self, pair, *gates):
        pieces = lax.all_gather(after(pair, *gates), "dl", axis=1, tiled=True)
        return pieces.reshape(D, FF)

    def share_far(self, partial, *gates):
        pieces = after(partial, *gates).reshape(2, D // 2, FF)
        return lax.psum_scatter(pieces, "dl", scatter_dimension=1, tiled=True)

    def share_send(self, pair):
        upper = lax.axis_index("dh")
        own = lax.dynamic_index_in_dim(pair, upper, 0)
        return own, self.hop(lax.dynamic_index_in_dim(pair, 1 - upper, 0), "dh", 1)

    def share_sum(self, own, other):
        return flipped(lax.axis_index("dh"), own.astype(WIDE), other.astype(WIDE), 0)

    def to_experts(self, rows):
        chunks = rows.reshape(2 * self.groups, -1, D)
        return lax.all_to_all(chunks, ("dh",) + self.expert, 0, 0, tiled=True).reshape(-1, D)


def after(value, *others):
    return lax.optimization_barrier((value,) + others)[0]


def fenced(ready, body, *operands):
    shapes = jax.eval_shape(body, *operands)
    empty = lambda *_: jax.tree.map(lambda leaf: jnp.zeros(leaf.shape, leaf.dtype), shapes)
    return lax.cond(ready, body, empty, *operands)


def padded(rows, fill=0):
    shaped = rows.reshape(rows.shape[0] // SEQ, SEQ, rows.shape[1])
    return jnp.pad(shaped, ((0, 0), (0, LINES - SEQ), (0, 0)), constant_values=fill)


def unpadded(lines):
    return lines[:, :SEQ].reshape(-1, lines.shape[2])


def flat(lines):
    return lines.reshape(-1, lines.shape[2])


def local(plan, act_in, w_qkv, w_proj, w_up, w_down, norm_gain, norm_shift, exp_in, exp_out, gate, expert_index, cotangent):
    experts_all = EXP_DEV * plan.groups
    capacity = (TOP * TOK_DEV * 5 // (4 * experts_all) + 7) // 8 * 8
    slots = experts_all * capacity
    proj_t = jnp.swapaxes(w_proj, 1, 2).astype(LOW)
    qkv_low = w_qkv.astype(LOW)
    norms = jnp.concatenate([norm_gain, norm_shift]).T.astype(LOW)
    norms = jnp.pad(norms, ((0, 0), (0, 256 - norms.shape[1])))
    part_a = jnp.concatenate([qkv_low[0], proj_t[0], norms], axis=1)
    part_b = jnp.concatenate([w_up.astype(LOW), w_down.T.astype(LOW)], axis=1)
    part_c = jnp.concatenate([qkv_low[1], proj_t[1]], axis=1)
    ready = expert_index[0, 0] >= 0
    bar = lax.optimization_barrier
    core = lax.axis_index("c") if plan.wide else 0 * expert_index[0, 0]
    parts = (part_a, part_b, part_c)
    in_low = exp_in.astype(LOW)
    deep_a = plan.gather_depth(parts[:1])
    deep_bc = plan.gather_depth(parts[1:], deep_a)

    def zeroth_part(deep_a, part_a):
        (pair_a,) = plan.gather_split(deep_a, (part_a,))
        one_a = bar(plan.gather_side(pair_a, 0))
        return bar(plan.gather_side(one_a, 1))

    two_a = fenced(ready, zeroth_part, deep_a, part_a)
    expert_index, act_in = after((expert_index, act_in), two_a)

    def prepare(expert_index, gate, cotangent, act_in):
        flat_index = expert_index.reshape(-1)
        onehot = (flat_index[:, None] == jnp.arange(experts_all, dtype=jnp.int32)).astype(jnp.int32)
        before = jnp.cumsum(onehot, axis=0) - onehot
        holder = (flat_index % EXP_DEV) * plan.groups + flat_index // EXP_DEV
        spots = (holder * capacity + jnp.sum(onehot * before, axis=1)).reshape(-1, TOP)
        spots = padded(spots, -1)
        gates, cot, x_a = padded(gate), padded(cotangent), padded(act_in)
        grad_sent = dispatch_grad(flat(spots).T, flat(gates), flat(cot), slots)
        return spots, gates, cot, x_a, grad_sent

    spots, gates, cot, x_a, grad_sent = fenced(
        ready, prepare, expert_index, gate, cotangent, act_in
    )
    spot_rows = flat(spots).T

    out_low = jnp.swapaxes(exp_out, 1, 2).astype(LOW)
    in_low, x_a, grad_sent, deep_bc = bar((in_low, x_a, grad_sent, deep_bc))
    in_near = plan.fetch_near(in_low)

    def first_part(two_a, deep_bc, parts, x_a):
        part_a, part_b, part_c = parts
        pair_b, pair_c = plan.gather_split(deep_bc, (part_b, part_c))
        four_a, one_b = bar((plan.gather_core(two_a), plan.gather_side(pair_b, 0)))
        block_a = plan.gather_join(four_a, part_a)
        norms = block_a[:, 4 * D : 4 * D + 8].astype(WIDE).T
        gain, shift = norms[:4, None], norms[4:, None]
        x_b, packed_a, mixed_a = attend_forward(x_a, gain[0], shift[0], block_a)
        two_b, x_b = bar((plan.gather_side(one_b, 1), x_b))
        return gain, shift, block_a, x_b, packed_a, mixed_a, two_b, pair_c

    gain, shift, block_a, x_b, packed_a, mixed_a, two_b, pair_c = fenced(
        ready, first_part, two_a, deep_bc, parts, x_a
    )
    two_b, in_near, out_low = bar((two_b, in_near, out_low))
    weight_in = plan.fetch_far(in_near)
    out_near = plan.fetch_near(out_low)

    def second_part(x_b, gain, shift, two_b, pair_c, part_b):
        four_b, one_c = bar((plan.gather_core(two_b), plan.gather_side(pair_c, 0)))
        block_b = plan.gather_join(four_b, part_b)
        x_c, hidden_b, slope_b = mlp_forward(x_b, gain[1], shift[1], block_b)
        two_c, x_c = bar((plan.gather_side(one_c, 1), x_c))
        return block_b, x_c, hidden_b, slope_b, two_c

    block_b, x_c, hidden_b, slope_b, two_c = fenced(
        ready, second_part, x_b, gain, shift, two_b, pair_c, part_b
    )
    two_c, out_near = bar((two_c, out_near))
    weight_out = plan.fetch_far(out_near)

    def rows_part(x_c, gain, shift, two_c, part_c, spot_rows, grad_sent):
        grad_rows = plan.to_experts(grad_sent)
        block_c = plan.gather_join(bar(plan.gather_core(two_c)), part_c)
        x_d, packed_c, mixed_c = attend_forward(x_c, gain[2], shift[2], block_c)
        sent = dispatch(spot_rows, flat(x_d), gain[3], shift[3], slots)
        sent, grad_rows = bar((sent, grad_rows))
        return block_c, x_d, packed_c, mixed_c, plan.to_experts(sent), grad_rows

    block_c, x_d, packed_c, mixed_c, rows, grad_rows = fenced(
        ready, rows_part, x_c, gain, shift, two_c, part_c, spot_rows, grad_sent
    )
    hidden, slope = expert_forward(rows, weight_in)


    def experts_backward(grad_rows, hidden, slope, weight_in, weight_out):
        dinner, droutes = expert_backward(grad_rows, slope, weight_in, weight_out)
        (down_partial,) = weight_grad(False, core, (grad_rows, after(hidden, droutes)))
        return dinner, droutes, down_partial

    dinner, droutes, down_partial = fenced(
        ready, experts_backward, grad_rows, hidden, slope, weight_in, weight_out
    )
    down_pair = plan.share_far(down_partial)

    def experts_return(rows, dinner, droutes, hidden, weight_out):
        routes_home = plan.to_experts(droutes)
        (in_partial,) = weight_grad(False, core, (rows, dinner))
        result = mm_t(after(hidden, in_partial), weight_out).astype(LOW)
        routes_home, result = bar((routes_home, result))
        return routes_home, in_partial, result

    routes_home, in_partial, result = fenced(
        ready, experts_return, rows, dinner, droutes, hidden, weight_out
    )
    in_pair = plan.share_far(in_partial)
    home = plan.to_experts(after(result, routes_home))

    def third_part(gain, shift, block_c, x_c, x_d, packed_c, mixed_c, spots, cot, routes_home):
        dx_d, gain_d, shift_d = return_grad(spots, x_d, cot, gain[3], routes_home)
        dx_c, dpacked_c, normed_c, low_c, gain_c, shift_c = attend_backward(
            x_c, dx_d, packed_c, gain[2], shift[2], block_c
        )
        sum_c = weight_grad(
            plan.wide, core, (flat(normed_c), flat(dpacked_c)), (flat(low_c), flat(mixed_c))
        )
        return sum_c, dx_c, (gain_c, gain_d), (shift_c, shift_d)

    sum_c, dx_c, gains, shifts = fenced(
        ready, third_part, gain, shift, block_c, x_c, x_d, packed_c, mixed_c, spots, cot, routes_home
    )
    dx_c, down_pair = bar((dx_c, down_pair))
    down_own, down_other = plan.share_send(down_pair)

    def fourth_part(gain, shift, block_b, x_b, dx_c, sum_c, hidden_b, slope_b):
        dx_b, dinner_b, normed_b, low_b, gain_b, shift_b = mlp_backward(
            x_b, dx_c, slope_b, gain[1], shift[1], block_b
        )
        pair_c, dx_b, dinner_b = bar((plan.scatter_swap(sum_c), dx_b, dinner_b))
        sum_b = weight_grad(
            plan.wide, core, (flat(normed_b), flat(dinner_b)), (flat(low_b), flat(hidden_b))
        )
        pair_c, sum_b = bar((plan.scatter_side(pair_c, 0), sum_b))
        pair_c, pair_b = bar((plan.scatter_side(pair_c, 1), plan.scatter_swap(sum_b)))
        return pair_c, pair_b, dx_b, gain_b, shift_b

    pair_c, pair_b, dx_b, gain_b, shift_b = fenced(
        ready, fourth_part, gain, shift, block_b, x_b, dx_c, sum_c, hidden_b, slope_b
    )
    dx_b, home, down_other = bar((dx_b, home, down_other))

    def attend_part(gain, shift, block_a, x_a, packed_a, mixed_a, pair_b, pair_c, dx_b):
        own_c, far_c = plan.scatter_send(plan.scatter_stack(pair_c))
        dx_a, dpacked_a, normed_a, low_a, gain_a, shift_a = attend_backward(
            x_a, dx_b, packed_a, gain[0], shift[0], block_a
        )
        pair_b, dx_a, far_c = bar((plan.scatter_side(pair_b, 0), dx_a, far_c))
        pair_c = plan.scatter_add(own_c, far_c)
        return dx_a, dpacked_a, normed_a, low_a, gain_a, shift_a, pair_b, pair_c

    dx_a, dpacked_a, normed_a, low_a, gain_a, shift_a, pair_b, pair_c = fenced(
        ready, attend_part, gain, shift, block_a, x_a, packed_a, mixed_a, pair_b, pair_c, dx_b
    )
    pair_b, in_pair = bar((pair_b, in_pair))
    in_own, in_other = plan.share_send(in_pair)

    def combine_part(dpacked_a, normed_a, low_a, mixed_a, pair_b, pair_c, norms, x_d, spots, gates, cot, home):
        norm_grads = jnp.concatenate(norms).T
        act_out, grad_gate = combine(spots, gates, x_d, cot, home)
        sum_a = weight_grad(
            plan.wide, core, (flat(normed_a), flat(dpacked_a)), (flat(low_a), flat(mixed_a))
        )
        pair_b, sum_a, act_out = bar((plan.scatter_side(pair_b, 1), sum_a, act_out))
        return norm_grads, sum_a, plan.scatter_stack(pair_b), plan.scatter_near(pair_c), act_out, grad_gate

    norm_grads, sum_a, deep_b, near_c, act_out, grad_gate = fenced(
        ready, combine_part, dpacked_a, normed_a, low_a, mixed_a, pair_b, pair_c,
        (gain_a, gain_b) + gains + (shift_a, shift_b) + shifts, x_d, spots, gates, cot, home,
    )
    own_b, far_b = plan.scatter_send(deep_b)


    def fifth_part(sum_a, act_out, grad_gate, dx_a):
        pair_a = bar(plan.scatter_swap(sum_a))
        pair_a = bar(plan.scatter_side(pair_a, 0))
        deep_a = plan.scatter_stack(plan.scatter_side(pair_a, 1))
        return deep_a, unpadded(act_out), unpadded(grad_gate), unpadded(dx_a)

    deep_a, act_out, grad_gate, dx_a = fenced(
        ready, fifth_part, sum_a, act_out, grad_gate, dx_a
    )
    deep_a, own_b, far_b, in_other = bar((deep_a, own_b, far_b, in_other))

    def sixth_part(deep_a, own_b, far_b, near_c, norm_grads, shares):
        norm_pieces = plan.small_send(norm_grads)
        own_a, far_a = plan.scatter_send(deep_a)
        near_b = plan.scatter_near(plan.scatter_add(own_b, far_b))
        near_b, far_a = bar((near_b, far_a))
        grad_exp_in, grad_exp_out = [plan.share_sum(*share) for share in shares]
        near_a, mine_bc = bar(
            (plan.scatter_near(plan.scatter_add(own_a, far_a)), plan.scatter_core(plan.scatter_join(near_b, near_c)))
        )
        mine_norms = plan.small_sum(norm_pieces)
        return plan.scatter_core(near_a), mine_bc, mine_norms, grad_exp_in, grad_exp_out

    mine_a, mine_bc, mine_norms, grad_exp_in, grad_exp_out = fenced(
        ready, sixth_part, deep_a, own_b, far_b, near_c, norm_grads,
        ((in_own, in_other), (down_own, down_other)),
    )
    mine_b, mine_c = plan.scatter_unstack(mine_bc, 2 * FF, 4 * D)
    grad_exp_out = jnp.swapaxes(grad_exp_out, 1, 2)

    grad_qkv = jnp.stack([mine_a[:, : 3 * D], mine_c[:, : 3 * D]])
    grad_proj = jnp.stack([mine_a[:, 3 * D :], mine_c[:, 3 * D :]])
    return (
        act_out,
        dx_a,
        grad_qkv,
        jnp.swapaxes(grad_proj, 1, 2),
        mine_b[:, :FF],
        mine_b[:, FF:].T,
        mine_norms[:, :4].T,
        mine_norms[:, 4:].T,
        grad_exp_in,
        grad_exp_out,
        grad_gate,
    )


def solution(mesh):
    plan = Plan(mesh)
    rows, dp, expert = plan.axes, plan.dp, plan.expert
    in_specs = (
        P(rows, None),
        P(None, rows, None),
        P(None, None, rows),
        P(rows, None),
        P(None, rows),
        P(None, rows),
        P(None, rows),
        P(expert, dp, None),
        P(expert, None, dp),
        P(rows, None),
        P(rows, None),
        P(rows, None),
    )
    out_specs = (
        P(rows, None),
        P(rows, None),
        P(None, rows, None),
        P(None, None, rows),
        P(rows, None),
        P(None, rows),
        P(None, rows),
        P(None, rows),
        P(expert, dp, None),
        P(expert, None, dp),
        P(rows, None),
    )
    return jax.shard_map(
        functools.partial(local, plan),
        mesh=plan.mesh,
        in_specs=in_specs,
        out_specs=out_specs,
        check_vma=False,
    )
```

```python
import functools
import math

import jax
import jax.numpy as jnp
import numpy as np
from jax import lax
from jax.experimental import pallas as pl
from jax.experimental.pallas import tpu as pltpu
from jax.sharding import Mesh, PartitionSpec as P

D = 768
FF = 3072
HEADS = 12
HEAD = 64
SEQ = 197
LINES = 208
TOP = 2
EXP_DEV = 2
TOK_DEV = 591
EPS = 1e-06
LOW = jnp.bfloat16
WIDE = jnp.float32
SCALE = 1.0 / math.sqrt(HEAD)
RSQRT2 = 1.0 / math.sqrt(2.0)
RSQRT2PI = 1.0 / math.sqrt(2.0 * math.pi)
SLOT_TILE = 256
ROW_TILE = 256
WIDTH_TILE = 768
HINT = 4


def mm(left, right):
    return jnp.dot(left, right, preferred_element_type=WIDE)


def mm_t(left, right):
    return lax.dot_general(left, right, (((1,), (1,)), ((), ())), preferred_element_type=WIDE)


def t_mm(left, right):
    return lax.dot_general(left, right, (((0,), (0,)), ((), ())), preferred_element_type=WIDE)


def norm_parts(inputs):
    average = jnp.mean(inputs, axis=-1, keepdims=True)
    centred = inputs - average
    spread = jnp.mean(centred * centred, axis=-1, keepdims=True)
    inverse = lax.rsqrt(spread + EPS)
    return centred * inverse, inverse


def norm_low(inputs, gain_ref, shift_ref):
    xhat, _ = norm_parts(inputs)
    return (xhat * gain_ref[...] + shift_ref[...]).astype(LOW)


def norm_backward(dnormed, xhat, inverse, gain_ref, residual, dx_ref, dgain_ref, dshift_ref):
    scaled = dnormed * gain_ref[...]
    mean = jnp.mean(scaled, axis=-1, keepdims=True)
    tilt = jnp.mean(scaled * xhat, axis=-1, keepdims=True)
    dx_ref[0] = residual + inverse * (scaled - mean - xhat * tilt)

    @pl.when(pl.program_id(0) == 0)
    def _():
        dgain_ref[...] = jnp.zeros_like(dgain_ref)
        dshift_ref[...] = jnp.zeros_like(dshift_ref)

    dgain_ref[...] += jnp.sum(dnormed * xhat, axis=0, keepdims=True)
    dshift_ref[...] += jnp.sum(dnormed, axis=0, keepdims=True)


def gelu_both(inner):
    phi = 0.5 + 0.5 * lax.erf(inner * RSQRT2)
    slope = phi + inner * (RSQRT2PI * jnp.exp(-0.5 * inner * inner))
    return (inner * phi).astype(LOW), slope.astype(LOW)


def softmax_rows(query, key):
    scores = mm_t(query, key) * SCALE
    lane = lax.broadcasted_iota(jnp.int32, scores.shape, 1)
    scores = jnp.where(lane < SEQ, scores, -jnp.inf)
    peak = jnp.max(scores, axis=-1, keepdims=True)
    raised = jnp.exp(scores - peak)
    total = jnp.sum(raised, axis=-1, keepdims=True)
    return raised * (1.0 / total)


def whole(shape):
    return pl.BlockSpec(shape, lambda *_: (0,) * len(shape))


def window(width, at):
    return pl.BlockSpec((D, width), lambda *_: (0, at))


def image(width):
    return pl.BlockSpec((1, LINES, width), lambda i: (i, 0, 0))


def params(megabytes):
    return pltpu.CompilerParams(vmem_limit_bytes=megabytes << 20)


def like(shape, kind):
    return jax.ShapeDtypeStruct(shape, kind)


def cost(flops, moved, raised=0):
    return pl.CostEstimate(
        flops=flops // HINT, bytes_accessed=moved // HINT, transcendentals=raised // HINT
    )


def attend_forward_body(x_ref, gain_ref, shift_ref, qkv_ref, proj_ref, out_ref, packed_ref, mixed_ref):
    x = x_ref[0]
    packed_ref[0] = mm(norm_low(x, gain_ref, shift_ref), qkv_ref[...]).astype(LOW)
    first = lax.broadcasted_iota(jnp.int32, (LINES, 2 * HEAD), 1) < HEAD
    zero = jnp.zeros((LINES, 2 * HEAD), LOW)
    for pair in range(HEADS // 2):
        at = pair * 2 * HEAD
        query = packed_ref[0, :, at : at + 2 * HEAD]
        key = packed_ref[0, :, D + at : D + at + 2 * HEAD]
        value = packed_ref[0, :, 2 * D + at : 2 * D + at + 2 * HEAD]
        low = mm(softmax_rows(jnp.where(first, query, zero), key).astype(LOW), value)
        high = mm(softmax_rows(jnp.where(first, zero, query), key).astype(LOW), value)
        mixed_ref[0, :, at : at + 2 * HEAD] = jnp.where(first, low, high).astype(LOW)
    out_ref[0] = x + mm_t(mixed_ref[0], proj_ref[...])


def attend_forward(x, gain, shift, block):
    images = x.shape[0]
    return pl.pallas_call(
        attend_forward_body,
        grid=(images,),
        in_specs=[image(D), whole((1, D)), whole((1, D)), window(3 * D, 0), window(D, 3)],
        out_specs=[image(D), image(3 * D), image(D)],
        out_shape=[
            like((images, LINES, D), WIDE),
            like((images, LINES, 3 * D), LOW),
            like((images, LINES, D), LOW),
        ],
        compiler_params=params(48),
        cost_estimate=cost(3_700_000_000, 13_000_000, 1_600_000),
        name="attend_forward",
    )(x, gain, shift, block, block)


def attend_backward_body(
    x_ref, dy_ref, packed_ref, gain_ref, shift_ref, qkv_ref, proj_ref,
    dx_ref, dpacked_ref, normed_ref, low_ref, dgain_ref, dshift_ref,
    dmixed_ref,
):
    dy = dy_ref[0]
    grad_low = dy.astype(LOW)
    low_ref[0] = grad_low
    dmixed_ref[...] = mm(grad_low, proj_ref[...]).astype(LOW)
    first = lax.broadcasted_iota(jnp.int32, (LINES, 2 * HEAD), 1) < HEAD
    zero = jnp.zeros((LINES, 2 * HEAD), LOW)

    def one(query, key, value, upstream):
        probs = softmax_rows(query, key)
        dprobs = mm_t(upstream, value)
        inner = jnp.sum(probs * dprobs, axis=-1, keepdims=True)
        dscores = (probs * (dprobs - inner)).astype(LOW)
        return t_mm(probs.astype(LOW), upstream), mm(dscores, key), t_mm(dscores, query)

    for pair in range(HEADS // 2):
        at = pair * 2 * HEAD
        query = packed_ref[0, :, at : at + 2 * HEAD]
        key = packed_ref[0, :, D + at : D + at + 2 * HEAD]
        value = packed_ref[0, :, 2 * D + at : 2 * D + at + 2 * HEAD]
        upstream = dmixed_ref[:, at : at + 2 * HEAD]
        dv0, dq0, dk0 = one(
            jnp.where(first, query, zero), key, value, jnp.where(first, upstream, zero)
        )
        dv1, dq1, dk1 = one(
            jnp.where(first, zero, query), key, value, jnp.where(first, zero, upstream)
        )
        dpacked_ref[0, :, at : at + 2 * HEAD] = (jnp.where(first, dq0, dq1) * SCALE).astype(LOW)
        dpacked_ref[0, :, D + at : D + at + 2 * HEAD] = ((dk0 + dk1) * SCALE).astype(LOW)
        dpacked_ref[0, :, 2 * D + at : 2 * D + at + 2 * HEAD] = (dv0 + dv1).astype(LOW)
    xhat, inverse = norm_parts(x_ref[0])
    normed_ref[0] = (xhat * gain_ref[...] + shift_ref[...]).astype(LOW)
    dnormed = mm_t(dpacked_ref[0], qkv_ref[...])
    norm_backward(dnormed, xhat, inverse, gain_ref, dy, dx_ref, dgain_ref, dshift_ref)


def attend_backward(x, dy, packed, gain, shift, block):
    images = x.shape[0]
    return pl.pallas_call(
        attend_backward_body,
        grid=(images,),
        in_specs=[
            image(D), image(D), image(3 * D), whole((1, D)), whole((1, D)),
            window(3 * D, 0), window(D, 3),
        ],
        out_specs=[image(D), image(3 * D), image(D), image(D), whole((1, D)), whole((1, D))],
        out_shape=[
            like((images, LINES, D), WIDE),
            like((images, LINES, 3 * D), LOW),
            like((images, LINES, D), LOW),
            like((images, LINES, D), LOW),
            like((1, D), WIDE),
            like((1, D), WIDE),
        ],
        scratch_shapes=[pltpu.VMEM((LINES, D), LOW)],
        compiler_params=params(48),
        cost_estimate=cost(4_000_000_000, 22_000_000, 1_600_000),
        name="attend_backward",
    )(x, dy, packed, gain, shift, block, block)


def mlp_forward_body(x_ref, gain_ref, shift_ref, up_ref, down_ref, out_ref, hidden_ref, slope_ref):
    x = x_ref[0]
    normed = norm_low(x, gain_ref, shift_ref)
    total = x
    step = FF // 4
    for at in range(0, FF, step):
        hidden, slope = gelu_both(mm(normed, up_ref[:, at : at + step]))
        hidden_ref[0, :, at : at + step] = hidden
        slope_ref[0, :, at : at + step] = slope
        total = total + mm_t(hidden, down_ref[:, at : at + step])
    out_ref[0] = total


def mlp_forward(x, gain, shift, block):
    images = x.shape[0]
    return pl.pallas_call(
        mlp_forward_body,
        grid=(images,),
        in_specs=[image(D), whole((1, D)), whole((1, D)), window(FF, 0), window(FF, 1)],
        out_specs=[image(D), image(FF), image(FF)],
        out_shape=[
            like((images, LINES, D), WIDE),
            like((images, LINES, FF), LOW),
            like((images, LINES, FF), LOW),
        ],
        compiler_params=params(56),
        cost_estimate=cost(5_900_000_000, 21_000_000, 4_000_000),
        name="mlp_forward",
    )(x, gain, shift, block, block)


def mlp_backward_body(
    x_ref, dy_ref, slope_ref, gain_ref, shift_ref, up_ref, down_ref,
    dx_ref, dinner_ref, normed_ref, low_ref, dgain_ref, dshift_ref,
):
    dy = dy_ref[0]
    grad_low = dy.astype(LOW)
    low_ref[0] = grad_low
    step = FF // 4
    dnormed = jnp.zeros((LINES, D), WIDE)
    for at in range(0, FF, step):
        dhidden = mm(grad_low, down_ref[:, at : at + step])
        dinner = (dhidden * slope_ref[0, :, at : at + step].astype(WIDE)).astype(LOW)
        dinner_ref[0, :, at : at + step] = dinner
        dnormed = dnormed + mm_t(dinner, up_ref[:, at : at + step])
    xhat, inverse = norm_parts(x_ref[0])
    normed_ref[0] = (xhat * gain_ref[...] + shift_ref[...]).astype(LOW)
    norm_backward(dnormed, xhat, inverse, gain_ref, dy, dx_ref, dgain_ref, dshift_ref)


def mlp_backward(x, dy, slope, gain, shift, block):
    images = x.shape[0]
    return pl.pallas_call(
        mlp_backward_body,
        grid=(images,),
        in_specs=[
            image(D), image(D), image(FF), whole((1, D)), whole((1, D)),
            window(FF, 0), window(FF, 1),
        ],
        out_specs=[image(D), image(FF), image(D), image(D), whole((1, D)), whole((1, D))],
        out_shape=[
            like((images, LINES, D), WIDE),
            like((images, LINES, FF), LOW),
            like((images, LINES, D), LOW),
            like((images, LINES, D), LOW),
            like((1, D), WIDE),
            like((1, D), WIDE),
        ],
        compiler_params=params(56),
        cost_estimate=cost(5_900_000_000, 25_000_000),
        name="mlp_backward",
    )(x, dy, slope, gain, shift, block, block)


def chosen(places_ref, tile):
    tokens = places_ref.shape[1]
    slot = pl.program_id(0) * tile + lax.broadcasted_iota(jnp.int32, (tile, tokens), 0)
    return [jnp.where(slot == places_ref[k : k + 1, :], 1.0, 0.0) for k in range(TOP)]


def dispatch_body(places_ref, x_ref, gain_ref, shift_ref, out_ref, sent_ref):
    @pl.when(pl.program_id(0) == 0)
    def _():
        sent_ref[...] = norm_low(x_ref[...], gain_ref, shift_ref)

    picks = chosen(places_ref, SLOT_TILE)
    out_ref[...] = mm((picks[0] + picks[1]).astype(LOW), sent_ref[...]).astype(LOW)


def dispatch(places, x, gain, shift, slots):
    tokens = x.shape[0]
    return pl.pallas_call(
        dispatch_body,
        grid=(slots // SLOT_TILE,),
        in_specs=[whole((TOP, tokens)), whole((tokens, D)), whole((1, D)), whole((1, D))],
        out_specs=pl.BlockSpec((SLOT_TILE, D), lambda i: (i, 0)),
        out_shape=like((slots, D), LOW),
        scratch_shapes=[pltpu.VMEM((tokens, D), LOW)],
        compiler_params=params(32),
        cost_estimate=cost(1_500_000_000, 4_500_000),
        name="dispatch",
    )(places, x, gain, shift)


def dispatch_grad_body(places_ref, gate_ref, cot_ref, out_ref, sent_ref):
    @pl.when(pl.program_id(0) == 0)
    def _():
        for k in range(TOP):
            sent_ref[k] = (gate_ref[:, k : k + 1] * cot_ref[...]).astype(LOW)

    picks = chosen(places_ref, SLOT_TILE)
    total = mm(picks[0].astype(LOW), sent_ref[0]) + mm(picks[1].astype(LOW), sent_ref[1])
    out_ref[...] = total.astype(LOW)


def dispatch_grad(places, gate, cot, slots):
    tokens = cot.shape[0]
    return pl.pallas_call(
        dispatch_grad_body,
        grid=(slots // SLOT_TILE,),
        in_specs=[whole((TOP, tokens)), whole((tokens, TOP)), whole((tokens, D))],
        out_specs=pl.BlockSpec((SLOT_TILE, D), lambda i: (i, 0)),
        out_shape=like((slots, D), LOW),
        scratch_shapes=[pltpu.VMEM((TOP, tokens, D), LOW)],
        compiler_params=params(32),
        cost_estimate=cost(3_000_000_000, 4_500_000),
        name="dispatch_grad",
    )(places, gate, cot)


def picker(places_ref, k, slots):
    lane = lax.broadcasted_iota(jnp.int32, (LINES, slots), 1)
    return jnp.where(lane == places_ref[0, :, k : k + 1], 1.0, 0.0)


def combine_body(places_ref, gate_ref, x_ref, cot_ref, home_ref, out_ref, dgate_ref):
    slots = home_ref.shape[0]
    total = x_ref[0]
    for k in range(TOP):
        picked = mm(picker(places_ref, k, slots).astype(LOW), home_ref[...])
        total = total + gate_ref[0, :, k : k + 1] * picked
        dgate_ref[0, :, k : k + 1] = jnp.sum(cot_ref[0] * picked, axis=-1, keepdims=True)
    out_ref[0] = total


def combine(places, gate, x, cot, home):
    images, slots = x.shape[0], home.shape[0]
    return pl.pallas_call(
        combine_body,
        grid=(images,),
        in_specs=[image(TOP), image(TOP), image(D), image(D), whole((slots, D))],
        out_specs=[image(D), image(TOP)],
        out_shape=[like((images, LINES, D), WIDE), like((images, LINES, TOP), WIDE)],
        compiler_params=params(32),
        cost_estimate=cost(3_000_000_000, 8_000_000),
        name="combine",
    )(places, gate, x, cot, home)


def return_grad_body(places_ref, x_ref, cot_ref, gain_ref, home_ref, dx_ref, dgain_ref, dshift_ref):
    slots = home_ref.shape[0]
    picks = (picker(places_ref, 0, slots) + picker(places_ref, 1, slots)).astype(LOW)
    dsent = mm(picks, home_ref[...])
    xhat, inverse = norm_parts(x_ref[0])
    norm_backward(dsent, xhat, inverse, gain_ref, cot_ref[0], dx_ref, dgain_ref, dshift_ref)


def return_grad(places, x, cot, gain, home):
    images, slots = x.shape[0], home.shape[0]
    return pl.pallas_call(
        return_grad_body,
        grid=(images,),
        in_specs=[image(TOP), image(D), image(D), whole((1, D)), whole((slots, D))],
        out_specs=[image(D), whole((1, D)), whole((1, D))],
        out_shape=[like((images, LINES, D), WIDE), like((1, D), WIDE), like((1, D), WIDE)],
        compiler_params=params(32),
        cost_estimate=cost(1_500_000_000, 8_000_000),
        name="return_grad",
    )(places, x, cot, gain, home)


def expert_forward_body(rows_ref, in_ref, hidden_ref, slope_ref):
    step = FF // 4
    for at in range(0, FF, step):
        hidden, slope = gelu_both(mm(rows_ref[...], in_ref[:, at : at + step]))
        hidden_ref[:, at : at + step] = hidden
        slope_ref[:, at : at + step] = slope


def tiled(width):
    return pl.BlockSpec((ROW_TILE, width), lambda i: (i, 0))


def expert_forward(rows, weight):
    count = rows.shape[0]
    return pl.pallas_call(
        expert_forward_body,
        grid=(count // ROW_TILE,),
        in_specs=[tiled(D), whole((D, FF))],
        out_specs=[tiled(FF), tiled(FF)],
        out_shape=[like((count, FF), LOW), like((count, FF), LOW)],
        compiler_params=params(48),
        cost_estimate=cost(7_200_000_000, 26_000_000, 9_000_000),
        name="expert_forward",
    )(rows, weight)


def expert_backward_body(grad_ref, slope_ref, in_ref, out_ref, dinner_ref, dx_ref):
    step = FF // 4
    total = jnp.zeros((ROW_TILE, D), WIDE)
    for at in range(0, FF, step):
        dhidden = mm(grad_ref[...], out_ref[:, at : at + step])
        dinner = (dhidden * slope_ref[:, at : at + step].astype(WIDE)).astype(LOW)
        dinner_ref[:, at : at + step] = dinner
        total = total + mm_t(dinner, in_ref[:, at : at + step])
    dx_ref[...] = total.astype(LOW)


def expert_backward(grad, slope, weight_in, weight_out_t):
    count = grad.shape[0]
    return pl.pallas_call(
        expert_backward_body,
        grid=(count // ROW_TILE,),
        in_specs=[tiled(D), tiled(FF), whole((D, FF)), whole((D, FF))],
        out_specs=[tiled(FF), tiled(D)],
        out_shape=[like((count, FF), LOW), like((count, D), LOW)],
        compiler_params=params(48),
        cost_estimate=cost(14_400_000_000, 33_000_000),
        name="expert_backward",
    )(grad, slope, weight_in, weight_out_t)


def weight_grad_body(tiles, starts, split, at_ref, *refs):
    count = len(starts)
    lefts, rights = refs[:count], refs[count : 2 * count]
    outs, turned = refs[2 * count : -count], refs[-count:]
    step = pl.program_id(0)
    tile = lax.rem(step + at_ref[0], tiles)

    @pl.when(step == 0)
    def _():
        for left, scratch in zip(lefts, turned):
            scratch[...] = left[...].T

    for index, (left, right) in enumerate(zip(turned, rights)):
        stop = (starts + (tiles,))[index + 1]

        @pl.when((tile >= starts[index]) & (tile < stop))
        def _(left=left, right=right):
            value = mm(left[...], right[...]).astype(LOW)
            if split:

                @pl.when(step < tiles // 2)
                def _():
                    outs[0][...] = value

                @pl.when(step >= tiles // 2)
                def _():
                    outs[1][...] = value
            else:
                outs[0][...] = value


def weight_grad(split, core, *pairs):
    width = WIDTH_TILE
    tokens = pairs[0][0].shape[0]
    counts = [right.shape[1] // width for _, right in pairs]
    starts = tuple(int(n) for n in np.cumsum([0] + counts[:-1]))
    tiles = sum(counts)
    first = ((1 - core) * (tiles // 2) if split else 0 * core).astype(jnp.int32).reshape(1)

    def right_spec(start, count):
        def at(step, at_ref):
            return 0, jnp.clip(lax.rem(step + at_ref[0], tiles) - start, 0, count - 1)

        return pl.BlockSpec((tokens, width), at)

    half = tiles // 2
    if split:
        out_specs = [
            pl.BlockSpec((D, width), lambda step, _: (0, jnp.minimum(step, half - 1))),
            pl.BlockSpec((D, width), lambda step, _: (0, jnp.maximum(step - half, 0))),
        ]
        out_shape = [like((D, half * width), LOW)] * 2
    else:
        out_specs = [pl.BlockSpec((D, width), lambda step, _: (0, step))]
        out_shape = [like((D, tiles * width), LOW)]
    return pl.pallas_call(
        functools.partial(weight_grad_body, tiles, starts, split),
        grid_spec=pltpu.PrefetchScalarGridSpec(
            num_scalar_prefetch=1,
            grid=(tiles,),
            in_specs=[whole((tokens, D)) for _ in pairs]
            + [right_spec(start, count) for start, count in zip(starts, counts)],
            out_specs=out_specs,
            scratch_shapes=[pltpu.VMEM((D, tokens), LOW) for _ in pairs],
        ),
        out_shape=out_shape,
        compiler_params=params(48),
        cost_estimate=cost(2 * D * tokens * tiles * width, 3 * D * tiles * width),
        name="weight_grad",
    )(first, *[left for left, _ in pairs], *[right for _, right in pairs])


def join_body(at_ref, *refs):
    *parts, out_ref, sem = refs
    for index, part in enumerate(parts):
        rows, width = part.shape[1:]
        for block in range(part.shape[0]):
            down = pl.multiple_of(at_ref[index, 2 * block] * 16, 16)
            right = pl.multiple_of(at_ref[index, 2 * block + 1] * 128, 128)
            target = out_ref.at[pl.ds(down, rows), pl.ds(right, width)]
            pltpu.make_async_copy(part.at[block], target, sem).start()
    pltpu.make_async_copy(out_ref, out_ref, sem).wait()


def join(places, parts, width):
    return pl.pallas_call(
        join_body,
        in_specs=[pl.BlockSpec(memory_space=pltpu.SMEM)]
        + [pl.BlockSpec(memory_space=pl.ANY)] * len(parts),
        out_specs=pl.BlockSpec(memory_space=pltpu.VMEM),
        out_shape=like((D, width), LOW),
        scratch_shapes=[pltpu.SemaphoreType.DMA],
        compiler_params=params(32),
        cost_estimate=cost(0, 4 * D * width),
        name="join",
    )(places, *parts)


def pick(value, at, axis):
    return lax.dynamic_index_in_dim(value, at, axis, keepdims=False)


def flipped(index, first, second, axis):
    return jnp.where(
        index == 0,
        jnp.concatenate([first, second], axis=axis),
        jnp.concatenate([second, first], axis=axis),
    )


class Plan:
    def __init__(self, mesh):
        n_dp, n_expert = mesh.devices.shape
        self.n_dp, self.groups = n_dp, n_expert
        self.wide = (n_dp, n_expert) == (4, 8)
        expert_shape, expert = ((2, 2, 2), ("y", "x", "c")) if self.wide else ((n_expert,), ("expert",))
        self.dp = ("dh", "dl")
        self.expert = expert
        self.axes = self.dp + expert
        self.mesh = Mesh(mesh.devices.reshape((2, n_dp // 2) + expert_shape), self.axes)

    def hop(self, value, axes, bit):
        size = lax.axis_size(axes)
        return lax.ppermute(value, axes, [(i, i ^ bit) for i in range(size)])

    def gather_depth(self, parts, *gates):
        parts = after(tuple(parts), *gates)
        if not self.wide:
            return jnp.concatenate(parts, axis=1)
        core = lax.axis_index("c")
        sides = [
            jnp.concatenate(
                [
                    lax.dynamic_slice_in_dim(part, side * self.cut(part)[0], self.cut(part)[0], 1)
                    for part in parts
                ],
                axis=1,
            )
            for side in (core, 1 - core)
        ]
        mine = flipped(core, sides[0], self.hop(sides[1], "c", 1), 0)
        return lax.all_gather(mine[None], self.dp, axis=0, tiled=True)

    def gather_split(self, deep, parts):
        if not self.wide:
            ends = np.cumsum([part.shape[1] for part in parts])
            return [deep[:, end - part.shape[1] : end] for end, part in zip(ends, parts)]
        pairs, at = [], 0
        for part in parts:
            half, quarter = self.cut(part)
            pairs.append((deep[:, :, at : at + quarter], deep[:, :, at + quarter : at + half]))
            at += half
        return pairs

    def cut(self, part):
        return part.shape[1] // 2, part.shape[1] // 512 * 128

    def gather_side(self, pair, step):
        if not self.wide:
            return pair
        left, right = lax.optimization_barrier(tuple(pair))
        axes = ("x", "y") if step == 0 else ("y", "x")
        came = lax.optimization_barrier((self.hop(left, axes[0], 1), self.hop(right, axes[1], 1)))
        return tuple(jnp.concatenate([own, new]) for own, new in zip((left, right), came))

    def gather_core(self, pair):
        if not self.wide:
            return pair
        return tuple(pair) + tuple(self.hop(value, "c", 1) for value in pair)

    def gather_join(self, four, part):
        if not self.wide:
            return lax.all_gather(four, self.axes, axis=0, tiled=True)
        rows, width = part.shape
        half, quarter = self.cut(part)
        core = lax.axis_index("c")
        steps = jnp.arange(16, dtype=jnp.int32)
        me = lax.axis_index("y") * 2 + lax.axis_index("x")
        first, second, turn = steps // 8, steps // 4 % 2, steps % 4
        left_at = (turn * 4 + first * 2 + second) ^ me
        right_at = (turn * 4 + second * 2 + first) ^ me

        def spots(at, side, side_core):
            across = jnp.broadcast_to((side_core * half + side * quarter) // 128, at.shape)
            return jnp.stack([at * (2 * rows // 16), across], axis=1).reshape(-1)

        places = jnp.stack(
            [
                spots(left_at, 0, core),
                spots(right_at, 1, core),
                spots(left_at, 0, 1 - core),
                spots(right_at, 1, 1 - core),
            ]
        ).astype(jnp.int32)
        return join(places, four, width)

    def scatter_swap(self, halves):
        if not self.wide:
            return halves[0]
        other, mine = halves
        height, half = mine.shape
        quarter = half // 256 * 128
        mine = self.plus(mine, self.hop(other, "c", 1))
        mine = mine.reshape(self.n_dp, 2, 2, height // 16, half)
        return mine[..., :quarter], mine[..., quarter:]

    def scatter_side(self, pair, step):
        if not self.wide:
            return pair
        y, x = lax.axis_index("y"), lax.axis_index("x")
        turns = ((("y", y, 1), ("x", x, 2)), (("x", x, 1), ("y", y, 1)))[step]
        kept = [pick(value, at, axis) for value, (_, at, axis) in zip(pair, turns)]
        sent = [pick(value, 1 - at, axis) for value, (_, at, axis) in zip(pair, turns)]
        sent = lax.optimization_barrier(tuple(sent))
        came = [self.hop(value, name, 1) for value, (name, _, _) in zip(sent, turns)]
        came = lax.optimization_barrier(tuple(came))
        return tuple(self.plus(one, two) for one, two in zip(kept, came))

    def scatter_stack(self, *pairs):
        if not self.wide:
            return jnp.concatenate(pairs, axis=1)
        return jnp.concatenate([value for pair in pairs for value in pair], axis=2)

    def scatter_send(self, deep):
        if not self.wide:
            return deep, deep[:1, :1]
        deep = deep.reshape((2, 2) + deep.shape[1:])
        high = lax.axis_index("dh")
        return pick(deep, high, 0), self.hop(pick(deep, 1 - high, 0), "dh", 1)

    def scatter_add(self, own, far):
        return self.plus(own, far) if self.wide else own

    def small_send(self, values):
        devices = self.n_dp * self.groups
        return lax.all_to_all(values.reshape(devices, -1), self.axes, 0, 0, tiled=True)

    def small_sum(self, pieces):
        return jnp.sum(pieces, axis=0).reshape(-1, 8)

    def scatter_join(self, *values):
        return jnp.concatenate(values, axis=1)

    def scatter_unstack(self, rows, *widths):
        if not self.wide:
            return jnp.split(rows, np.cumsum(widths[:-1]), axis=1)
        out, at, half = [], 0, rows.shape[1] // 2
        for width in widths:
            left = rows[:, at : at + width // 2]
            right = rows[:, half + at : half + at + width // 2]
            out.append(jnp.concatenate([left, right], axis=1))
            at += width // 2
        return out

    def scatter_near(self, deep):
        if not self.wide:
            return deep
        low = lax.axis_index("dl")
        return pick(deep, low, 0).astype(WIDE) + self.hop(pick(deep, 1 - low, 0), "dl", 1).astype(WIDE)

    def scatter_core(self, total):
        if not self.wide:
            return lax.psum_scatter(total, self.axes, scatter_dimension=0, tiled=True).astype(WIDE)
        core, rows = lax.axis_index("c"), total.shape[0] // 2
        away = self.hop(lax.dynamic_slice_in_dim(total, (1 - core) * rows, rows, 0), "c", 1)
        return flipped(core, lax.dynamic_slice_in_dim(total, core * rows, rows, 0), away, 1)

    def plus(self, one, two):
        return (one.astype(WIDE) + two.astype(WIDE)).astype(LOW)

    def choose(self, part):
        upper = lax.axis_index("dh")
        first, second = part[0].astype(LOW), part[1].astype(LOW)
        return jnp.where(upper == 0, first, second), jnp.where(upper == 0, second, first)

    def fetch_near(self, same, other):
        upper = lax.axis_index("dh")
        return flipped(upper, same[None], self.hop(other, "dh", 1)[None], 0)

    def fetch_far(self, pair, *gates):
        pieces = lax.all_gather(after(pair, *gates), "dl", axis=1, tiled=True)
        return pieces.reshape(D, FF)

    def share_far(self, partial, *gates):
        pieces = after(partial, *gates).reshape(2, D // 2, FF)
        return lax.psum_scatter(pieces, "dl", scatter_dimension=1, tiled=True)

    def share_send(self, pair):
        upper = lax.axis_index("dh")
        own = lax.dynamic_index_in_dim(pair, upper, 0)
        return own, self.hop(lax.dynamic_index_in_dim(pair, 1 - upper, 0), "dh", 1)

    def share_sum(self, own, other):
        return flipped(lax.axis_index("dh"), own.astype(WIDE), other.astype(WIDE), 0)

    def to_experts(self, rows):
        chunks = rows.reshape(2 * self.groups, -1, D)
        return lax.all_to_all(chunks, ("dh",) + self.expert, 0, 0, tiled=True).reshape(-1, D)


def after(value, *others):
    return lax.optimization_barrier((value,) + others)[0]


def fenced(ready, body, *operands):
    shapes = jax.eval_shape(body, *operands)
    empty = lambda *_: jax.tree.map(lambda leaf: jnp.zeros(leaf.shape, leaf.dtype), shapes)
    return lax.cond(ready, body, empty, *operands)


def padded(rows, fill=0):
    shaped = rows.reshape(rows.shape[0] // SEQ, SEQ, rows.shape[1])
    return jnp.pad(shaped, ((0, 0), (0, LINES - SEQ), (0, 0)), constant_values=fill)


def unpadded(lines):
    return lines[:, :SEQ].reshape(-1, lines.shape[2])


def flat(lines):
    return lines.reshape(-1, lines.shape[2])


def local(plan, act_in, w_qkv, w_proj, w_up, w_down, norm_gain, norm_shift, exp_in, exp_out, gate, expert_index, cotangent):
    experts_all = EXP_DEV * plan.groups
    capacity = (TOP * TOK_DEV * 5 // (4 * experts_all) + 7) // 8 * 8
    slots = experts_all * capacity
    proj_t = jnp.swapaxes(w_proj, 1, 2).astype(LOW)
    qkv_low = w_qkv.astype(LOW)
    norms = jnp.concatenate([norm_gain, norm_shift]).T.astype(LOW)
    norms = jnp.pad(norms, ((0, 0), (0, 256 - norms.shape[1])))
    part_a = jnp.concatenate([qkv_low[0], proj_t[0], norms], axis=1)
    part_b = jnp.concatenate([w_up.astype(LOW), w_down.T.astype(LOW)], axis=1)
    part_c = jnp.concatenate([qkv_low[1], proj_t[1]], axis=1)
    ready = expert_index[0, 0] >= 0
    bar = lax.optimization_barrier
    core = lax.axis_index("c") if plan.wide else 0 * expert_index[0, 0]
    parts = (part_a, part_b, part_c)
    deep_a = plan.gather_depth(parts[:1])
    deep_bc = plan.gather_depth(parts[1:], deep_a)

    def zeroth_part(deep_a, part_a, exp_in, exp_out, expert_index, gate, cotangent, act_in):
        in_pair = plan.choose(exp_in)
        out_pair = plan.choose(jnp.swapaxes(exp_out, 1, 2))
        (pair_a,) = plan.gather_split(deep_a, (part_a,))
        one_a, in_pair, out_pair = bar((plan.gather_side(pair_a, 0), in_pair, out_pair))
        two_a = plan.gather_side(one_a, 1)
        expert_index, cotangent, act_in = after((expert_index, cotangent, act_in), one_a)
        flat_index = expert_index.reshape(-1)
        onehot = (flat_index[:, None] == jnp.arange(experts_all, dtype=jnp.int32)).astype(jnp.int32)
        before = jnp.cumsum(onehot, axis=0) - onehot
        holder = (flat_index % EXP_DEV) * plan.groups + flat_index // EXP_DEV
        spots = (holder * capacity + jnp.sum(onehot * before, axis=1)).reshape(-1, TOP)
        spots = padded(spots, -1)
        gates, cot, x_a = padded(gate), padded(cotangent), padded(act_in)
        grad_sent = dispatch_grad(flat(spots).T, flat(gates), flat(cot), slots)
        return two_a, in_pair, out_pair, spots, gates, cot, x_a, grad_sent

    two_a, in_pair, out_pair, spots, gates, cot, x_a, grad_sent = fenced(
        ready, zeroth_part, deep_a, part_a, exp_in, exp_out, expert_index, gate, cotangent, act_in
    )
    spot_rows = flat(spots).T
    in_pair, x_a, deep_bc = bar((in_pair, x_a, deep_bc))
    in_near = plan.fetch_near(*in_pair)

    def first_part(two_a, deep_bc, parts, x_a):
        part_a, part_b, part_c = parts
        pair_b, pair_c = plan.gather_split(deep_bc, (part_b, part_c))
        four_a, one_b = bar((plan.gather_core(two_a), plan.gather_side(pair_b, 0)))
        block_a = plan.gather_join(four_a, part_a)
        norms = block_a[:, 4 * D : 4 * D + 8].astype(WIDE).T
        gain, shift = norms[:4, None], norms[4:, None]
        x_b, packed_a, mixed_a = attend_forward(x_a, gain[0], shift[0], block_a)
        two_b, x_b = bar((plan.gather_side(one_b, 1), x_b))
        return gain, shift, block_a, x_b, packed_a, mixed_a, two_b, pair_c

    gain, shift, block_a, x_b, packed_a, mixed_a, two_b, pair_c = fenced(
        ready, first_part, two_a, deep_bc, parts, x_a
    )
    two_b, in_near, out_pair = bar((two_b, in_near, out_pair))
    weight_in = plan.fetch_far(in_near)
    out_near = plan.fetch_near(*out_pair)

    def second_part(x_b, gain, shift, two_b, pair_c, part_b):
        four_b, one_c = bar((plan.gather_core(two_b), plan.gather_side(pair_c, 0)))
        block_b = plan.gather_join(four_b, part_b)
        x_c, hidden_b, slope_b = mlp_forward(x_b, gain[1], shift[1], block_b)
        two_c, x_c = bar((plan.gather_side(one_c, 1), x_c))
        return block_b, x_c, hidden_b, slope_b, two_c

    block_b, x_c, hidden_b, slope_b, two_c = fenced(
        ready, second_part, x_b, gain, shift, two_b, pair_c, part_b
    )
    two_c, out_near = bar((two_c, out_near))
    weight_out = plan.fetch_far(out_near)

    def rows_part(x_c, gain, shift, two_c, part_c, spot_rows, grad_sent):
        grad_rows = plan.to_experts(grad_sent)
        block_c = plan.gather_join(bar(plan.gather_core(two_c)), part_c)
        x_d, packed_c, mixed_c = attend_forward(x_c, gain[2], shift[2], block_c)
        sent = dispatch(spot_rows, flat(x_d), gain[3], shift[3], slots)
        sent, grad_rows = bar((sent, grad_rows))
        return block_c, x_d, packed_c, mixed_c, plan.to_experts(sent), grad_rows

    block_c, x_d, packed_c, mixed_c, rows, grad_rows = fenced(
        ready, rows_part, x_c, gain, shift, two_c, part_c, spot_rows, grad_sent
    )
    hidden, slope = expert_forward(rows, weight_in)


    def experts_backward(grad_rows, hidden, slope, weight_in, weight_out):
        dinner, droutes = expert_backward(grad_rows, slope, weight_in, weight_out)
        (down_partial,) = weight_grad(False, core, (grad_rows, after(hidden, droutes)))
        return dinner, droutes, down_partial

    dinner, droutes, down_partial = fenced(
        ready, experts_backward, grad_rows, hidden, slope, weight_in, weight_out
    )
    down_pair = plan.share_far(down_partial)

    def experts_return(rows, dinner, droutes, hidden, weight_out):
        routes_home = plan.to_experts(droutes)
        (in_partial,) = weight_grad(False, core, (rows, dinner))
        result = mm_t(after(hidden, in_partial), weight_out).astype(LOW)
        routes_home, result = bar((routes_home, result))
        return routes_home, in_partial, result

    routes_home, in_partial, result = fenced(
        ready, experts_return, rows, dinner, droutes, hidden, weight_out
    )
    in_pair = plan.share_far(in_partial)
    home = plan.to_experts(after(result, routes_home))

    def third_part(gain, shift, block_c, x_c, x_d, packed_c, mixed_c, spots, cot, routes_home):
        dx_d, gain_d, shift_d = return_grad(spots, x_d, cot, gain[3], routes_home)
        dx_c, dpacked_c, normed_c, low_c, gain_c, shift_c = attend_backward(
            x_c, dx_d, packed_c, gain[2], shift[2], block_c
        )
        sum_c = weight_grad(
            plan.wide, core, (flat(normed_c), flat(dpacked_c)), (flat(low_c), flat(mixed_c))
        )
        return sum_c, dx_c, (gain_c, gain_d), (shift_c, shift_d)

    sum_c, dx_c, gains, shifts = fenced(
        ready, third_part, gain, shift, block_c, x_c, x_d, packed_c, mixed_c, spots, cot, routes_home
    )
    dx_c, down_pair = bar((dx_c, down_pair))
    down_own, down_other = plan.share_send(down_pair)

    def fourth_part(gain, shift, block_b, x_b, dx_c, sum_c, hidden_b, slope_b):
        dx_b, dinner_b, normed_b, low_b, gain_b, shift_b = mlp_backward(
            x_b, dx_c, slope_b, gain[1], shift[1], block_b
        )
        pair_c, dx_b, dinner_b = bar((plan.scatter_swap(sum_c), dx_b, dinner_b))
        sum_b = weight_grad(
            plan.wide, core, (flat(normed_b), flat(dinner_b)), (flat(low_b), flat(hidden_b))
        )
        pair_c, sum_b = bar((plan.scatter_side(pair_c, 0), sum_b))
        pair_c, pair_b = bar((plan.scatter_side(pair_c, 1), plan.scatter_swap(sum_b)))
        return pair_c, pair_b, dx_b, gain_b, shift_b

    pair_c, pair_b, dx_b, gain_b, shift_b = fenced(
        ready, fourth_part, gain, shift, block_b, x_b, dx_c, sum_c, hidden_b, slope_b
    )
    dx_b, home, down_other = bar((dx_b, home, down_other))

    def attend_part(gain, shift, block_a, x_a, packed_a, mixed_a, pair_b, pair_c, dx_b):
        own_c, far_c = plan.scatter_send(plan.scatter_stack(pair_c))
        dx_a, dpacked_a, normed_a, low_a, gain_a, shift_a = attend_backward(
            x_a, dx_b, packed_a, gain[0], shift[0], block_a
        )
        pair_b, dx_a, far_c = bar((plan.scatter_side(pair_b, 0), dx_a, far_c))
        pair_c = plan.scatter_add(own_c, far_c)
        return dx_a, dpacked_a, normed_a, low_a, gain_a, shift_a, pair_b, pair_c

    dx_a, dpacked_a, normed_a, low_a, gain_a, shift_a, pair_b, pair_c = fenced(
        ready, attend_part, gain, shift, block_a, x_a, packed_a, mixed_a, pair_b, pair_c, dx_b
    )
    pair_b, in_pair = bar((pair_b, in_pair))
    in_own, in_other = plan.share_send(in_pair)

    def combine_part(dpacked_a, normed_a, low_a, mixed_a, pair_b, pair_c, norms, x_d, spots, gates, cot, home):
        norm_grads = jnp.concatenate(norms).T
        act_out, grad_gate = combine(spots, gates, x_d, cot, home)
        sum_a = weight_grad(
            plan.wide, core, (flat(normed_a), flat(dpacked_a)), (flat(low_a), flat(mixed_a))
        )
        pair_b, sum_a, act_out = bar((plan.scatter_side(pair_b, 1), sum_a, act_out))
        return norm_grads, sum_a, plan.scatter_stack(pair_b), plan.scatter_near(pair_c), act_out, grad_gate

    norm_grads, sum_a, deep_b, near_c, act_out, grad_gate = fenced(
        ready, combine_part, dpacked_a, normed_a, low_a, mixed_a, pair_b, pair_c,
        (gain_a, gain_b) + gains + (shift_a, shift_b) + shifts, x_d, spots, gates, cot, home,
    )
    own_b, far_b = plan.scatter_send(deep_b)


    def fifth_part(sum_a, act_out, grad_gate, dx_a):
        pair_a = bar(plan.scatter_swap(sum_a))
        pair_a = bar(plan.scatter_side(pair_a, 0))
        deep_a = plan.scatter_stack(plan.scatter_side(pair_a, 1))
        return deep_a, unpadded(act_out), unpadded(grad_gate), unpadded(dx_a)

    deep_a, act_out, grad_gate, dx_a = fenced(
        ready, fifth_part, sum_a, act_out, grad_gate, dx_a
    )
    deep_a, own_b, far_b, in_other = bar((deep_a, own_b, far_b, in_other))

    def sixth_part(deep_a, own_b, far_b, near_c, norm_grads, shares):
        norm_pieces = plan.small_send(norm_grads)
        own_a, far_a = plan.scatter_send(deep_a)
        near_b = plan.scatter_near(plan.scatter_add(own_b, far_b))
        near_b, far_a = bar((near_b, far_a))
        grad_exp_in, grad_exp_out = [plan.share_sum(*share) for share in shares]
        near_a, mine_bc = bar(
            (plan.scatter_near(plan.scatter_add(own_a, far_a)), plan.scatter_core(plan.scatter_join(near_b, near_c)))
        )
        mine_norms = plan.small_sum(norm_pieces)
        return plan.scatter_core(near_a), mine_bc, mine_norms, grad_exp_in, grad_exp_out

    mine_a, mine_bc, mine_norms, grad_exp_in, grad_exp_out = fenced(
        ready, sixth_part, deep_a, own_b, far_b, near_c, norm_grads,
        ((in_own, in_other), (down_own, down_other)),
    )
    mine_b, mine_c = plan.scatter_unstack(mine_bc, 2 * FF, 4 * D)
    grad_exp_out = jnp.swapaxes(grad_exp_out, 1, 2)

    grad_qkv = jnp.stack([mine_a[:, : 3 * D], mine_c[:, : 3 * D]])
    grad_proj = jnp.stack([mine_a[:, 3 * D :], mine_c[:, 3 * D :]])
    return (
        act_out,
        dx_a,
        grad_qkv,
        jnp.swapaxes(grad_proj, 1, 2),
        mine_b[:, :FF],
        mine_b[:, FF:].T,
        mine_norms[:, :4].T,
        mine_norms[:, 4:].T,
        grad_exp_in,
        grad_exp_out,
        grad_gate,
    )


def solution(mesh):
    plan = Plan(mesh)
    rows, dp, expert = plan.axes, plan.dp, plan.expert
    in_specs = (
        P(rows, None),
        P(None, rows, None),
        P(None, None, rows),
        P(rows, None),
        P(None, rows),
        P(None, rows),
        P(None, rows),
        P(expert, dp, None),
        P(expert, None, dp),
        P(rows, None),
        P(rows, None),
        P(rows, None),
    )
    out_specs = (
        P(rows, None),
        P(rows, None),
        P(None, rows, None),
        P(None, None, rows),
        P(rows, None),
        P(None, rows),
        P(None, rows),
        P(None, rows),
        P(expert, dp, None),
        P(expert, None, dp),
        P(rows, None),
    )
    return jax.shard_map(
        functools.partial(local, plan),
        mesh=plan.mesh,
        in_specs=in_specs,
        out_specs=out_specs,
        check_vma=False,
    )
```

```python
import functools
import math

import jax
import jax.numpy as jnp
import numpy as np
from jax import lax
from jax.experimental import pallas as pl
from jax.experimental.pallas import tpu as pltpu
from jax.sharding import Mesh, PartitionSpec as P

D = 768
FF = 3072
HEADS = 12
HEAD = 64
SEQ = 197
LINES = 208
TOP = 2
EXP_DEV = 2
TOK_DEV = 591
EPS = 1e-06
LOW = jnp.bfloat16
WIDE = jnp.float32
SCALE = 1.0 / math.sqrt(HEAD)
RSQRT2 = 1.0 / math.sqrt(2.0)
RSQRT2PI = 1.0 / math.sqrt(2.0 * math.pi)
SLOT_TILE = 256
ROW_TILE = 256
WIDTH_TILE = 768
HINT = 4


def mm(left, right):
    return jnp.dot(left, right, preferred_element_type=WIDE)


def mm_t(left, right):
    return lax.dot_general(left, right, (((1,), (1,)), ((), ())), preferred_element_type=WIDE)


def t_mm(left, right):
    return lax.dot_general(left, right, (((0,), (0,)), ((), ())), preferred_element_type=WIDE)


def norm_parts(inputs):
    average = jnp.mean(inputs, axis=-1, keepdims=True)
    centred = inputs - average
    spread = jnp.mean(centred * centred, axis=-1, keepdims=True)
    inverse = lax.rsqrt(spread + EPS)
    return centred * inverse, inverse


def norm_low(inputs, gain_ref, shift_ref):
    xhat, _ = norm_parts(inputs)
    return (xhat * gain_ref[...] + shift_ref[...]).astype(LOW)


def norm_backward(dnormed, xhat, inverse, gain_ref, residual, dx_ref, dgain_ref, dshift_ref):
    scaled = dnormed * gain_ref[...]
    mean = jnp.mean(scaled, axis=-1, keepdims=True)
    tilt = jnp.mean(scaled * xhat, axis=-1, keepdims=True)
    dx_ref[0] = residual + inverse * (scaled - mean - xhat * tilt)

    @pl.when(pl.program_id(0) == 0)
    def _():
        dgain_ref[...] = jnp.zeros_like(dgain_ref)
        dshift_ref[...] = jnp.zeros_like(dshift_ref)

    dgain_ref[...] += jnp.sum(dnormed * xhat, axis=0, keepdims=True)
    dshift_ref[...] += jnp.sum(dnormed, axis=0, keepdims=True)


def gelu_both(inner):
    phi = 0.5 + 0.5 * lax.erf(inner * RSQRT2)
    slope = phi + inner * (RSQRT2PI * jnp.exp(-0.5 * inner * inner))
    return (inner * phi).astype(LOW), slope.astype(LOW)


def softmax_rows(query, key):
    scores = mm_t(query, key) * SCALE
    lane = lax.broadcasted_iota(jnp.int32, scores.shape, 1)
    scores = jnp.where(lane < SEQ, scores, -jnp.inf)
    peak = jnp.max(scores, axis=-1, keepdims=True)
    raised = jnp.exp(scores - peak)
    total = jnp.sum(raised, axis=-1, keepdims=True)
    return raised * (1.0 / total)


def whole(shape):
    return pl.BlockSpec(shape, lambda *_: (0,) * len(shape))


def window(width, at):
    return pl.BlockSpec((D, width), lambda *_: (0, at))


def image(width):
    return pl.BlockSpec((1, LINES, width), lambda i: (i, 0, 0))


def params(megabytes):
    return pltpu.CompilerParams(vmem_limit_bytes=megabytes << 20)


def like(shape, kind):
    return jax.ShapeDtypeStruct(shape, kind)


def cost(flops, moved, raised=0):
    return pl.CostEstimate(
        flops=flops // HINT, bytes_accessed=moved // HINT, transcendentals=raised // HINT
    )


def attend_forward_body(x_ref, gain_ref, shift_ref, qkv_ref, proj_ref, out_ref, packed_ref, mixed_ref):
    x = x_ref[0]
    packed_ref[0] = mm(norm_low(x, gain_ref, shift_ref), qkv_ref[...]).astype(LOW)
    first = lax.broadcasted_iota(jnp.int32, (LINES, 2 * HEAD), 1) < HEAD
    zero = jnp.zeros((LINES, 2 * HEAD), LOW)
    for pair in range(HEADS // 2):
        at = pair * 2 * HEAD
        query = packed_ref[0, :, at : at + 2 * HEAD]
        key = packed_ref[0, :, D + at : D + at + 2 * HEAD]
        value = packed_ref[0, :, 2 * D + at : 2 * D + at + 2 * HEAD]
        low = mm(softmax_rows(jnp.where(first, query, zero), key).astype(LOW), value)
        high = mm(softmax_rows(jnp.where(first, zero, query), key).astype(LOW), value)
        mixed_ref[0, :, at : at + 2 * HEAD] = jnp.where(first, low, high).astype(LOW)
    out_ref[0] = x + mm_t(mixed_ref[0], proj_ref[...])


def attend_forward(x, gain, shift, block):
    images = x.shape[0]
    return pl.pallas_call(
        attend_forward_body,
        grid=(images,),
        in_specs=[image(D), whole((1, D)), whole((1, D)), window(3 * D, 0), window(D, 3)],
        out_specs=[image(D), image(3 * D), image(D)],
        out_shape=[
            like((images, LINES, D), WIDE),
            like((images, LINES, 3 * D), LOW),
            like((images, LINES, D), LOW),
        ],
        compiler_params=params(48),
        cost_estimate=cost(3_700_000_000, 13_000_000, 1_600_000),
        name="attend_forward",
    )(x, gain, shift, block, block)


def attend_backward_body(
    x_ref, dy_ref, packed_ref, gain_ref, shift_ref, qkv_ref, proj_ref,
    dx_ref, dpacked_ref, normed_ref, low_ref, dgain_ref, dshift_ref,
    dmixed_ref,
):
    dy = dy_ref[0]
    grad_low = dy.astype(LOW)
    low_ref[0] = grad_low
    dmixed_ref[...] = mm(grad_low, proj_ref[...]).astype(LOW)
    first = lax.broadcasted_iota(jnp.int32, (LINES, 2 * HEAD), 1) < HEAD
    zero = jnp.zeros((LINES, 2 * HEAD), LOW)

    def one(query, key, value, upstream):
        probs = softmax_rows(query, key)
        dprobs = mm_t(upstream, value)
        inner = jnp.sum(probs * dprobs, axis=-1, keepdims=True)
        dscores = (probs * (dprobs - inner)).astype(LOW)
        return t_mm(probs.astype(LOW), upstream), mm(dscores, key), t_mm(dscores, query)

    for pair in range(HEADS // 2):
        at = pair * 2 * HEAD
        query = packed_ref[0, :, at : at + 2 * HEAD]
        key = packed_ref[0, :, D + at : D + at + 2 * HEAD]
        value = packed_ref[0, :, 2 * D + at : 2 * D + at + 2 * HEAD]
        upstream = dmixed_ref[:, at : at + 2 * HEAD]
        dv0, dq0, dk0 = one(
            jnp.where(first, query, zero), key, value, jnp.where(first, upstream, zero)
        )
        dv1, dq1, dk1 = one(
            jnp.where(first, zero, query), key, value, jnp.where(first, zero, upstream)
        )
        dpacked_ref[0, :, at : at + 2 * HEAD] = (jnp.where(first, dq0, dq1) * SCALE).astype(LOW)
        dpacked_ref[0, :, D + at : D + at + 2 * HEAD] = ((dk0 + dk1) * SCALE).astype(LOW)
        dpacked_ref[0, :, 2 * D + at : 2 * D + at + 2 * HEAD] = (dv0 + dv1).astype(LOW)
    xhat, inverse = norm_parts(x_ref[0])
    normed_ref[0] = (xhat * gain_ref[...] + shift_ref[...]).astype(LOW)
    dnormed = mm_t(dpacked_ref[0], qkv_ref[...])
    norm_backward(dnormed, xhat, inverse, gain_ref, dy, dx_ref, dgain_ref, dshift_ref)


def attend_backward(x, dy, packed, gain, shift, block):
    images = x.shape[0]
    return pl.pallas_call(
        attend_backward_body,
        grid=(images,),
        in_specs=[
            image(D), image(D), image(3 * D), whole((1, D)), whole((1, D)),
            window(3 * D, 0), window(D, 3),
        ],
        out_specs=[image(D), image(3 * D), image(D), image(D), whole((1, D)), whole((1, D))],
        out_shape=[
            like((images, LINES, D), WIDE),
            like((images, LINES, 3 * D), LOW),
            like((images, LINES, D), LOW),
            like((images, LINES, D), LOW),
            like((1, D), WIDE),
            like((1, D), WIDE),
        ],
        scratch_shapes=[pltpu.VMEM((LINES, D), LOW)],
        compiler_params=params(48),
        cost_estimate=cost(4_000_000_000, 22_000_000, 1_600_000),
        name="attend_backward",
    )(x, dy, packed, gain, shift, block, block)


def mlp_forward_body(x_ref, gain_ref, shift_ref, up_ref, down_ref, out_ref, hidden_ref, slope_ref):
    x = x_ref[0]
    normed = norm_low(x, gain_ref, shift_ref)
    total = x
    step = FF // 4
    for at in range(0, FF, step):
        hidden, slope = gelu_both(mm(normed, up_ref[:, at : at + step]))
        hidden_ref[0, :, at : at + step] = hidden
        slope_ref[0, :, at : at + step] = slope
        total = total + mm_t(hidden, down_ref[:, at : at + step])
    out_ref[0] = total


def mlp_forward(x, gain, shift, block):
    images = x.shape[0]
    return pl.pallas_call(
        mlp_forward_body,
        grid=(images,),
        in_specs=[image(D), whole((1, D)), whole((1, D)), window(FF, 0), window(FF, 1)],
        out_specs=[image(D), image(FF), image(FF)],
        out_shape=[
            like((images, LINES, D), WIDE),
            like((images, LINES, FF), LOW),
            like((images, LINES, FF), LOW),
        ],
        compiler_params=params(56),
        cost_estimate=cost(5_900_000_000, 21_000_000, 4_000_000),
        name="mlp_forward",
    )(x, gain, shift, block, block)


def mlp_backward_body(
    x_ref, dy_ref, slope_ref, gain_ref, shift_ref, up_ref, down_ref,
    dx_ref, dinner_ref, normed_ref, low_ref, dgain_ref, dshift_ref,
):
    dy = dy_ref[0]
    grad_low = dy.astype(LOW)
    low_ref[0] = grad_low
    step = FF // 4
    dnormed = jnp.zeros((LINES, D), WIDE)
    for at in range(0, FF, step):
        dhidden = mm(grad_low, down_ref[:, at : at + step])
        dinner = (dhidden * slope_ref[0, :, at : at + step].astype(WIDE)).astype(LOW)
        dinner_ref[0, :, at : at + step] = dinner
        dnormed = dnormed + mm_t(dinner, up_ref[:, at : at + step])
    xhat, inverse = norm_parts(x_ref[0])
    normed_ref[0] = (xhat * gain_ref[...] + shift_ref[...]).astype(LOW)
    norm_backward(dnormed, xhat, inverse, gain_ref, dy, dx_ref, dgain_ref, dshift_ref)


def mlp_backward(x, dy, slope, gain, shift, block):
    images = x.shape[0]
    return pl.pallas_call(
        mlp_backward_body,
        grid=(images,),
        in_specs=[
            image(D), image(D), image(FF), whole((1, D)), whole((1, D)),
            window(FF, 0), window(FF, 1),
        ],
        out_specs=[image(D), image(FF), image(D), image(D), whole((1, D)), whole((1, D))],
        out_shape=[
            like((images, LINES, D), WIDE),
            like((images, LINES, FF), LOW),
            like((images, LINES, D), LOW),
            like((images, LINES, D), LOW),
            like((1, D), WIDE),
            like((1, D), WIDE),
        ],
        compiler_params=params(56),
        cost_estimate=cost(5_900_000_000, 25_000_000),
        name="mlp_backward",
    )(x, dy, slope, gain, shift, block, block)


def chosen(places_ref, tile):
    tokens = places_ref.shape[1]
    slot = pl.program_id(0) * tile + lax.broadcasted_iota(jnp.int32, (tile, tokens), 0)
    return [jnp.where(slot == places_ref[k : k + 1, :], 1.0, 0.0) for k in range(TOP)]


def dispatch_body(places_ref, x_ref, gain_ref, shift_ref, out_ref, sent_ref):
    @pl.when(pl.program_id(0) == 0)
    def _():
        sent_ref[...] = norm_low(x_ref[...], gain_ref, shift_ref)

    picks = chosen(places_ref, SLOT_TILE)
    out_ref[...] = mm((picks[0] + picks[1]).astype(LOW), sent_ref[...]).astype(LOW)


def dispatch(places, x, gain, shift, slots):
    tokens = x.shape[0]
    return pl.pallas_call(
        dispatch_body,
        grid=(slots // SLOT_TILE,),
        in_specs=[whole((TOP, tokens)), whole((tokens, D)), whole((1, D)), whole((1, D))],
        out_specs=pl.BlockSpec((SLOT_TILE, D), lambda i: (i, 0)),
        out_shape=like((slots, D), LOW),
        scratch_shapes=[pltpu.VMEM((tokens, D), LOW)],
        compiler_params=params(32),
        cost_estimate=cost(1_500_000_000, 4_500_000),
        name="dispatch",
    )(places, x, gain, shift)


def dispatch_grad_body(places_ref, gate_ref, cot_ref, out_ref, sent_ref):
    @pl.when(pl.program_id(0) == 0)
    def _():
        for k in range(TOP):
            sent_ref[k] = (gate_ref[:, k : k + 1] * cot_ref[...]).astype(LOW)

    picks = chosen(places_ref, SLOT_TILE)
    total = mm(picks[0].astype(LOW), sent_ref[0]) + mm(picks[1].astype(LOW), sent_ref[1])
    out_ref[...] = total.astype(LOW)


def dispatch_grad(places, gate, cot, slots):
    tokens = cot.shape[0]
    return pl.pallas_call(
        dispatch_grad_body,
        grid=(slots // SLOT_TILE,),
        in_specs=[whole((TOP, tokens)), whole((tokens, TOP)), whole((tokens, D))],
        out_specs=pl.BlockSpec((SLOT_TILE, D), lambda i: (i, 0)),
        out_shape=like((slots, D), LOW),
        scratch_shapes=[pltpu.VMEM((TOP, tokens, D), LOW)],
        compiler_params=params(32),
        cost_estimate=cost(3_000_000_000, 4_500_000),
        name="dispatch_grad",
    )(places, gate, cot)


def picker(places_ref, k, slots):
    lane = lax.broadcasted_iota(jnp.int32, (LINES, slots), 1)
    return jnp.where(lane == places_ref[0, :, k : k + 1], 1.0, 0.0)


def combine_body(places_ref, gate_ref, x_ref, cot_ref, home_ref, out_ref, dgate_ref):
    slots = home_ref.shape[0]
    total = x_ref[0]
    for k in range(TOP):
        picked = mm(picker(places_ref, k, slots).astype(LOW), home_ref[...])
        total = total + gate_ref[0, :, k : k + 1] * picked
        dgate_ref[0, :, k : k + 1] = jnp.sum(cot_ref[0] * picked, axis=-1, keepdims=True)
    out_ref[0] = total


def combine(places, gate, x, cot, home):
    images, slots = x.shape[0], home.shape[0]
    return pl.pallas_call(
        combine_body,
        grid=(images,),
        in_specs=[image(TOP), image(TOP), image(D), image(D), whole((slots, D))],
        out_specs=[image(D), image(TOP)],
        out_shape=[like((images, LINES, D), WIDE), like((images, LINES, TOP), WIDE)],
        compiler_params=params(32),
        cost_estimate=cost(3_000_000_000, 8_000_000),
        name="combine",
    )(places, gate, x, cot, home)


def return_grad_body(places_ref, x_ref, cot_ref, gain_ref, home_ref, dx_ref, dgain_ref, dshift_ref):
    slots = home_ref.shape[0]
    picks = (picker(places_ref, 0, slots) + picker(places_ref, 1, slots)).astype(LOW)
    dsent = mm(picks, home_ref[...])
    xhat, inverse = norm_parts(x_ref[0])
    norm_backward(dsent, xhat, inverse, gain_ref, cot_ref[0], dx_ref, dgain_ref, dshift_ref)


def return_grad(places, x, cot, gain, home):
    images, slots = x.shape[0], home.shape[0]
    return pl.pallas_call(
        return_grad_body,
        grid=(images,),
        in_specs=[image(TOP), image(D), image(D), whole((1, D)), whole((slots, D))],
        out_specs=[image(D), whole((1, D)), whole((1, D))],
        out_shape=[like((images, LINES, D), WIDE), like((1, D), WIDE), like((1, D), WIDE)],
        compiler_params=params(32),
        cost_estimate=cost(1_500_000_000, 8_000_000),
        name="return_grad",
    )(places, x, cot, gain, home)


def expert_forward_body(rows_ref, in_ref, hidden_ref, slope_ref):
    step = FF // 4
    for at in range(0, FF, step):
        hidden, slope = gelu_both(mm(rows_ref[...], in_ref[:, at : at + step]))
        hidden_ref[:, at : at + step] = hidden
        slope_ref[:, at : at + step] = slope


def tiled(width):
    return pl.BlockSpec((ROW_TILE, width), lambda i: (i, 0))


def expert_forward(rows, weight):
    count = rows.shape[0]
    return pl.pallas_call(
        expert_forward_body,
        grid=(count // ROW_TILE,),
        in_specs=[tiled(D), whole((D, FF))],
        out_specs=[tiled(FF), tiled(FF)],
        out_shape=[like((count, FF), LOW), like((count, FF), LOW)],
        compiler_params=params(48),
        cost_estimate=cost(7_200_000_000, 26_000_000, 9_000_000),
        name="expert_forward",
    )(rows, weight)


def expert_backward_body(grad_ref, slope_ref, in_ref, out_ref, dinner_ref, dx_ref):
    step = FF // 4
    total = jnp.zeros((ROW_TILE, D), WIDE)
    for at in range(0, FF, step):
        dhidden = mm(grad_ref[...], out_ref[:, at : at + step])
        dinner = (dhidden * slope_ref[:, at : at + step].astype(WIDE)).astype(LOW)
        dinner_ref[:, at : at + step] = dinner
        total = total + mm_t(dinner, in_ref[:, at : at + step])
    dx_ref[...] = total.astype(LOW)


def expert_backward(grad, slope, weight_in, weight_out_t):
    count = grad.shape[0]
    return pl.pallas_call(
        expert_backward_body,
        grid=(count // ROW_TILE,),
        in_specs=[tiled(D), tiled(FF), whole((D, FF)), whole((D, FF))],
        out_specs=[tiled(FF), tiled(D)],
        out_shape=[like((count, FF), LOW), like((count, D), LOW)],
        compiler_params=params(48),
        cost_estimate=cost(14_400_000_000, 33_000_000),
        name="expert_backward",
    )(grad, slope, weight_in, weight_out_t)


def weight_grad_body(tiles, starts, split, at_ref, *refs):
    count = len(starts)
    lefts, rights = refs[:count], refs[count : 2 * count]
    outs, turned = refs[2 * count : -count], refs[-count:]
    step = pl.program_id(0)
    tile = lax.rem(step + at_ref[0], tiles)

    @pl.when(step == 0)
    def _():
        for left, scratch in zip(lefts, turned):
            scratch[...] = left[...].T

    for index, (left, right) in enumerate(zip(turned, rights)):
        stop = (starts + (tiles,))[index + 1]

        @pl.when((tile >= starts[index]) & (tile < stop))
        def _(left=left, right=right):
            value = mm(left[...], right[...]).astype(LOW)
            if split:

                @pl.when(step < tiles // 2)
                def _():
                    outs[0][...] = value

                @pl.when(step >= tiles // 2)
                def _():
                    outs[1][...] = value
            else:
                outs[0][...] = value


def weight_grad(split, core, *pairs):
    width = WIDTH_TILE
    tokens = pairs[0][0].shape[0]
    counts = [right.shape[1] // width for _, right in pairs]
    starts = tuple(int(n) for n in np.cumsum([0] + counts[:-1]))
    tiles = sum(counts)
    first = ((1 - core) * (tiles // 2) if split else 0 * core).astype(jnp.int32).reshape(1)

    def right_spec(start, count):
        def at(step, at_ref):
            return 0, jnp.clip(lax.rem(step + at_ref[0], tiles) - start, 0, count - 1)

        return pl.BlockSpec((tokens, width), at)

    half = tiles // 2
    if split:
        out_specs = [
            pl.BlockSpec((D, width), lambda step, _: (0, jnp.minimum(step, half - 1))),
            pl.BlockSpec((D, width), lambda step, _: (0, jnp.maximum(step - half, 0))),
        ]
        out_shape = [like((D, half * width), LOW)] * 2
    else:
        out_specs = [pl.BlockSpec((D, width), lambda step, _: (0, step))]
        out_shape = [like((D, tiles * width), LOW)]
    return pl.pallas_call(
        functools.partial(weight_grad_body, tiles, starts, split),
        grid_spec=pltpu.PrefetchScalarGridSpec(
            num_scalar_prefetch=1,
            grid=(tiles,),
            in_specs=[whole((tokens, D)) for _ in pairs]
            + [right_spec(start, count) for start, count in zip(starts, counts)],
            out_specs=out_specs,
            scratch_shapes=[pltpu.VMEM((D, tokens), LOW) for _ in pairs],
        ),
        out_shape=out_shape,
        compiler_params=params(48),
        cost_estimate=cost(2 * D * tokens * tiles * width, 3 * D * tiles * width),
        name="weight_grad",
    )(first, *[left for left, _ in pairs], *[right for _, right in pairs])


def join_body(at_ref, *refs):
    *parts, out_ref, sem = refs
    for index, part in enumerate(parts):
        rows, width = part.shape[1:]
        for block in range(part.shape[0]):
            down = pl.multiple_of(at_ref[index, 2 * block] * 16, 16)
            right = pl.multiple_of(at_ref[index, 2 * block + 1] * 128, 128)
            target = out_ref.at[pl.ds(down, rows), pl.ds(right, width)]
            pltpu.make_async_copy(part.at[block], target, sem).start()
    pltpu.make_async_copy(out_ref, out_ref, sem).wait()


def join(places, parts, width):
    return pl.pallas_call(
        join_body,
        in_specs=[pl.BlockSpec(memory_space=pltpu.SMEM)]
        + [pl.BlockSpec(memory_space=pl.ANY)] * len(parts),
        out_specs=pl.BlockSpec(memory_space=pltpu.VMEM),
        out_shape=like((D, width), LOW),
        scratch_shapes=[pltpu.SemaphoreType.DMA],
        compiler_params=params(32),
        cost_estimate=cost(0, 4 * D * width),
        name="join",
    )(places, *parts)


def pick(value, at, axis):
    return lax.dynamic_index_in_dim(value, at, axis, keepdims=False)


def flipped(index, first, second, axis):
    return jnp.where(
        index == 0,
        jnp.concatenate([first, second], axis=axis),
        jnp.concatenate([second, first], axis=axis),
    )


class Plan:
    def __init__(self, mesh):
        n_dp, n_expert = mesh.devices.shape
        self.n_dp, self.groups = n_dp, n_expert
        self.wide = (n_dp, n_expert) == (4, 8)
        expert_shape, expert = ((2, 2, 2), ("y", "x", "c")) if self.wide else ((n_expert,), ("expert",))
        self.dp = ("dh", "dl")
        self.expert = expert
        self.axes = self.dp + expert
        self.mesh = Mesh(mesh.devices.reshape((2, n_dp // 2) + expert_shape), self.axes)

    def hop(self, value, axes, bit):
        size = lax.axis_size(axes)
        return lax.ppermute(value, axes, [(i, i ^ bit) for i in range(size)])

    def gather_depth(self, parts, *gates):
        parts = after(tuple(parts), *gates)
        if not self.wide:
            return jnp.concatenate(parts, axis=1)
        core = lax.axis_index("c")
        sides = [
            jnp.concatenate(
                [
                    lax.dynamic_slice_in_dim(part, side * self.cut(part)[0], self.cut(part)[0], 1)
                    for part in parts
                ],
                axis=1,
            )
            for side in (core, 1 - core)
        ]
        mine = flipped(core, sides[0], self.hop(sides[1], "c", 1), 0)
        return lax.all_gather(mine[None], self.dp, axis=0, tiled=True)

    def gather_split(self, deep, parts):
        if not self.wide:
            ends = np.cumsum([part.shape[1] for part in parts])
            return [deep[:, end - part.shape[1] : end] for end, part in zip(ends, parts)]
        pairs, at = [], 0
        for part in parts:
            half, quarter = self.cut(part)
            pairs.append((deep[:, :, at : at + quarter], deep[:, :, at + quarter : at + half]))
            at += half
        return pairs

    def cut(self, part):
        return part.shape[1] // 2, part.shape[1] // 512 * 128

    def gather_side(self, pair, step):
        if not self.wide:
            return pair
        left, right = lax.optimization_barrier(tuple(pair))
        axes = ("x", "y") if step == 0 else ("y", "x")
        came = lax.optimization_barrier((self.hop(left, axes[0], 1), self.hop(right, axes[1], 1)))
        return tuple(jnp.concatenate([own, new]) for own, new in zip((left, right), came))

    def gather_core(self, pair):
        if not self.wide:
            return pair
        return tuple(pair) + tuple(self.hop(value, "c", 1) for value in pair)

    def gather_join(self, four, part):
        if not self.wide:
            return lax.all_gather(four, self.axes, axis=0, tiled=True)
        rows, width = part.shape
        half, quarter = self.cut(part)
        core = lax.axis_index("c")
        steps = jnp.arange(16, dtype=jnp.int32)
        me = lax.axis_index("y") * 2 + lax.axis_index("x")
        first, second, turn = steps // 8, steps // 4 % 2, steps % 4
        left_at = (turn * 4 + first * 2 + second) ^ me
        right_at = (turn * 4 + second * 2 + first) ^ me

        def spots(at, side, side_core):
            across = jnp.broadcast_to((side_core * half + side * quarter) // 128, at.shape)
            return jnp.stack([at * (2 * rows // 16), across], axis=1).reshape(-1)

        places = jnp.stack(
            [
                spots(left_at, 0, core),
                spots(right_at, 1, core),
                spots(left_at, 0, 1 - core),
                spots(right_at, 1, 1 - core),
            ]
        ).astype(jnp.int32)
        return join(places, four, width)

    def scatter_swap(self, halves):
        if not self.wide:
            return halves[0]
        other, mine = halves
        height, half = mine.shape
        quarter = half // 256 * 128
        mine = self.plus(mine, self.hop(other, "c", 1))
        mine = mine.reshape(self.n_dp, 2, 2, height // 16, half)
        return mine[..., :quarter], mine[..., quarter:]

    def scatter_side(self, pair, step):
        if not self.wide:
            return pair
        y, x = lax.axis_index("y"), lax.axis_index("x")
        turns = ((("y", y, 1), ("x", x, 2)), (("x", x, 1), ("y", y, 1)))[step]
        kept = [pick(value, at, axis) for value, (_, at, axis) in zip(pair, turns)]
        sent = [pick(value, 1 - at, axis) for value, (_, at, axis) in zip(pair, turns)]
        sent = lax.optimization_barrier(tuple(sent))
        came = [self.hop(value, name, 1) for value, (name, _, _) in zip(sent, turns)]
        came = lax.optimization_barrier(tuple(came))
        return tuple(self.plus(one, two) for one, two in zip(kept, came))

    def scatter_stack(self, *pairs):
        if not self.wide:
            return jnp.concatenate(pairs, axis=1)
        return jnp.concatenate([value for pair in pairs for value in pair], axis=2)

    def scatter_send(self, deep):
        if not self.wide:
            return deep, deep[:1, :1]
        deep = deep.reshape((2, 2) + deep.shape[1:])
        high = lax.axis_index("dh")
        return pick(deep, high, 0), self.hop(pick(deep, 1 - high, 0), "dh", 1)

    def scatter_add(self, own, far):
        return self.plus(own, far) if self.wide else own

    def small_send(self, values):
        devices = self.n_dp * self.groups
        return lax.all_to_all(values.reshape(devices, -1), self.axes, 0, 0, tiled=True)

    def small_sum(self, pieces):
        return jnp.sum(pieces, axis=0).reshape(-1, 8)

    def scatter_join(self, *values):
        return jnp.concatenate(values, axis=1)

    def scatter_unstack(self, rows, *widths):
        if not self.wide:
            return jnp.split(rows, np.cumsum(widths[:-1]), axis=1)
        out, at, half = [], 0, rows.shape[1] // 2
        for width in widths:
            left = rows[:, at : at + width // 2]
            right = rows[:, half + at : half + at + width // 2]
            out.append(jnp.concatenate([left, right], axis=1))
            at += width // 2
        return out

    def scatter_near(self, deep):
        if not self.wide:
            return deep
        low = lax.axis_index("dl")
        return pick(deep, low, 0).astype(WIDE) + self.hop(pick(deep, 1 - low, 0), "dl", 1).astype(WIDE)

    def scatter_core(self, total):
        if not self.wide:
            return lax.psum_scatter(total, self.axes, scatter_dimension=0, tiled=True).astype(WIDE)
        core, rows = lax.axis_index("c"), total.shape[0] // 2
        away = self.hop(lax.dynamic_slice_in_dim(total, (1 - core) * rows, rows, 0), "c", 1)
        return flipped(core, lax.dynamic_slice_in_dim(total, core * rows, rows, 0), away, 1)

    def plus(self, one, two):
        return (one.astype(WIDE) + two.astype(WIDE)).astype(LOW)

    def choose(self, part):
        upper = lax.axis_index("dh")
        first, second = part[0].astype(LOW), part[1].astype(LOW)
        return jnp.where(upper == 0, first, second), jnp.where(upper == 0, second, first)

    def fetch_near(self, same, other):
        upper = lax.axis_index("dh")
        return flipped(upper, same[None], self.hop(other, "dh", 1)[None], 0)

    def fetch_far(self, pair, *gates):
        pieces = lax.all_gather(after(pair, *gates), "dl", axis=1, tiled=True)
        return pieces.reshape(D, FF)

    def share_far(self, partial, *gates):
        pieces = after(partial, *gates).reshape(2, D // 2, FF)
        return lax.psum_scatter(pieces, "dl", scatter_dimension=1, tiled=True)

    def share_send(self, pair):
        upper = lax.axis_index("dh")
        own = lax.dynamic_index_in_dim(pair, upper, 0)
        return own, self.hop(lax.dynamic_index_in_dim(pair, 1 - upper, 0), "dh", 1)

    def share_sum(self, own, other):
        return flipped(lax.axis_index("dh"), own.astype(WIDE), other.astype(WIDE), 0)

    def to_experts(self, rows):
        chunks = rows.reshape(2 * self.groups, -1, D)
        return lax.all_to_all(chunks, ("dh",) + self.expert, 0, 0, tiled=True).reshape(-1, D)


def after(value, *others):
    return lax.optimization_barrier((value,) + others)[0]


def fenced(ready, body, *operands):
    shapes = jax.eval_shape(body, *operands)
    empty = lambda *_: jax.tree.map(lambda leaf: jnp.zeros(leaf.shape, leaf.dtype), shapes)
    return lax.cond(ready, body, empty, *operands)


def padded(rows, fill=0):
    shaped = rows.reshape(rows.shape[0] // SEQ, SEQ, rows.shape[1])
    return jnp.pad(shaped, ((0, 0), (0, LINES - SEQ), (0, 0)), constant_values=fill)


def unpadded(lines):
    return lines[:, :SEQ].reshape(-1, lines.shape[2])


def flat(lines):
    return lines.reshape(-1, lines.shape[2])


def local(plan, act_in, w_qkv, w_proj, w_up, w_down, norm_gain, norm_shift, exp_in, exp_out, gate, expert_index, cotangent):
    experts_all = EXP_DEV * plan.groups
    capacity = (TOP * TOK_DEV * 5 // (4 * experts_all) + 7) // 8 * 8
    slots = experts_all * capacity
    proj_t = jnp.swapaxes(w_proj, 1, 2).astype(LOW)
    qkv_low = w_qkv.astype(LOW)
    norms = jnp.concatenate([norm_gain, norm_shift]).T.astype(LOW)
    norms = jnp.pad(norms, ((0, 0), (0, 256 - norms.shape[1])))
    part_a = jnp.concatenate([qkv_low[0], proj_t[0], norms], axis=1)
    part_b = jnp.concatenate([w_up.astype(LOW), w_down.T.astype(LOW)], axis=1)
    part_c = jnp.concatenate([qkv_low[1], proj_t[1]], axis=1)
    ready = expert_index[0, 0] >= 0
    bar = lax.optimization_barrier
    core = lax.axis_index("c") if plan.wide else 0 * expert_index[0, 0]
    parts = (part_a, part_b, part_c)
    deep_a = plan.gather_depth(parts[:1])
    deep_bc = plan.gather_depth(parts[1:], deep_a)

    def zeroth_part(deep_a, part_a, exp_in, exp_out, expert_index, gate, cotangent, act_in):
        in_pair = plan.choose(exp_in)
        out_pair = plan.choose(jnp.swapaxes(exp_out, 1, 2))
        (pair_a,) = plan.gather_split(deep_a, (part_a,))
        one_a, in_pair, out_pair = bar((plan.gather_side(pair_a, 0), in_pair, out_pair))
        two_a = plan.gather_side(one_a, 1)
        expert_index, cotangent, act_in = after((expert_index, cotangent, act_in), one_a)
        flat_index = expert_index.reshape(-1)
        onehot = (flat_index[:, None] == jnp.arange(experts_all, dtype=jnp.int32)).astype(jnp.int32)
        before = jnp.cumsum(onehot, axis=0) - onehot
        holder = (flat_index % EXP_DEV) * plan.groups + flat_index // EXP_DEV
        spots = (holder * capacity + jnp.sum(onehot * before, axis=1)).reshape(-1, TOP)
        spots = padded(spots, -1)
        gates, cot, x_a = padded(gate), padded(cotangent), padded(act_in)
        grad_sent = dispatch_grad(flat(spots).T, flat(gates), flat(cot), slots)
        return two_a, in_pair, out_pair, spots, gates, cot, x_a, grad_sent

    two_a, in_pair, out_pair, spots, gates, cot, x_a, grad_sent = fenced(
        ready, zeroth_part, deep_a, part_a, exp_in, exp_out, expert_index, gate, cotangent, act_in
    )
    spot_rows = flat(spots).T
    in_pair, x_a, deep_bc = bar((in_pair, x_a, deep_bc))
    in_near = plan.fetch_near(*in_pair)

    def first_part(two_a, deep_bc, parts, x_a):
        part_a, part_b, part_c = parts
        pair_b, pair_c = plan.gather_split(deep_bc, (part_b, part_c))
        four_a, one_b = bar((plan.gather_core(two_a), plan.gather_side(pair_b, 0)))
        block_a = plan.gather_join(four_a, part_a)
        norms = block_a[:, 4 * D : 4 * D + 8].astype(WIDE).T
        gain, shift = norms[:4, None], norms[4:, None]
        x_b, packed_a, mixed_a = attend_forward(x_a, gain[0], shift[0], block_a)
        two_b, x_b = bar((plan.gather_side(one_b, 1), x_b))
        return gain, shift, block_a, x_b, packed_a, mixed_a, two_b, pair_c

    gain, shift, block_a, x_b, packed_a, mixed_a, two_b, pair_c = fenced(
        ready, first_part, two_a, deep_bc, parts, x_a
    )
    two_b, in_near, out_pair = bar((two_b, in_near, out_pair))
    weight_in = plan.fetch_far(in_near)
    out_near = plan.fetch_near(*out_pair)

    def second_part(x_b, gain, shift, two_b, pair_c, part_b):
        four_b, one_c = bar((plan.gather_core(two_b), plan.gather_side(pair_c, 0)))
        block_b = plan.gather_join(four_b, part_b)
        x_c, hidden_b, slope_b = mlp_forward(x_b, gain[1], shift[1], block_b)
        two_c, x_c = bar((plan.gather_side(one_c, 1), x_c))
        return block_b, x_c, hidden_b, slope_b, two_c

    block_b, x_c, hidden_b, slope_b, two_c = fenced(
        ready, second_part, x_b, gain, shift, two_b, pair_c, part_b
    )
    two_c, out_near = bar((two_c, out_near))
    weight_out = plan.fetch_far(out_near)

    def rows_part(x_c, gain, shift, two_c, part_c, spot_rows, grad_sent):
        grad_rows = plan.to_experts(grad_sent)
        block_c = plan.gather_join(bar(plan.gather_core(two_c)), part_c)
        x_d, packed_c, mixed_c = attend_forward(x_c, gain[2], shift[2], block_c)
        sent = dispatch(spot_rows, flat(x_d), gain[3], shift[3], slots)
        sent, grad_rows = bar((sent, grad_rows))
        return block_c, x_d, packed_c, mixed_c, plan.to_experts(sent), grad_rows

    block_c, x_d, packed_c, mixed_c, rows, grad_rows = fenced(
        ready, rows_part, x_c, gain, shift, two_c, part_c, spot_rows, grad_sent
    )
    hidden, slope = expert_forward(rows, weight_in)


    def experts_backward(grad_rows, hidden, slope, weight_in, weight_out):
        dinner, droutes = expert_backward(grad_rows, slope, weight_in, weight_out)
        (down_partial,) = weight_grad(False, core, (grad_rows, after(hidden, droutes)))
        return dinner, droutes, down_partial

    dinner, droutes, down_partial = fenced(
        ready, experts_backward, grad_rows, hidden, slope, weight_in, weight_out
    )
    down_pair = plan.share_far(down_partial)

    def experts_return(rows, dinner, droutes, hidden, weight_out):
        routes_home = plan.to_experts(droutes)
        (in_partial,) = weight_grad(False, core, (rows, dinner))
        result = mm_t(after(hidden, in_partial), weight_out).astype(LOW)
        routes_home, result = bar((routes_home, result))
        return routes_home, in_partial, result

    routes_home, in_partial, result = fenced(
        ready, experts_return, rows, dinner, droutes, hidden, weight_out
    )
    in_pair = plan.share_far(in_partial)
    home = plan.to_experts(after(result, routes_home))

    def third_part(gain, shift, block_c, x_c, x_d, packed_c, mixed_c, spots, cot, routes_home):
        dx_d, gain_d, shift_d = return_grad(spots, x_d, cot, gain[3], routes_home)
        dx_c, dpacked_c, normed_c, low_c, gain_c, shift_c = attend_backward(
            x_c, dx_d, packed_c, gain[2], shift[2], block_c
        )
        sum_c = weight_grad(
            plan.wide, core, (flat(normed_c), flat(dpacked_c)), (flat(low_c), flat(mixed_c))
        )
        return sum_c, dx_c, (gain_c, gain_d), (shift_c, shift_d)

    sum_c, dx_c, gains, shifts = fenced(
        ready, third_part, gain, shift, block_c, x_c, x_d, packed_c, mixed_c, spots, cot, routes_home
    )
    dx_c, down_pair = bar((dx_c, down_pair))
    down_own, down_other = plan.share_send(down_pair)

    def fourth_part(gain, shift, block_b, x_b, dx_c, sum_c, hidden_b, slope_b):
        dx_b, dinner_b, normed_b, low_b, gain_b, shift_b = mlp_backward(
            x_b, dx_c, slope_b, gain[1], shift[1], block_b
        )
        pair_c, dx_b, dinner_b = bar((plan.scatter_swap(sum_c), dx_b, dinner_b))
        sum_b = weight_grad(
            plan.wide, core, (flat(normed_b), flat(dinner_b)), (flat(low_b), flat(hidden_b))
        )
        pair_c, sum_b = bar((plan.scatter_side(pair_c, 0), sum_b))
        pair_c, pair_b = bar((plan.scatter_side(pair_c, 1), plan.scatter_swap(sum_b)))
        return pair_c, pair_b, dx_b, gain_b, shift_b

    pair_c, pair_b, dx_b, gain_b, shift_b = fenced(
        ready, fourth_part, gain, shift, block_b, x_b, dx_c, sum_c, hidden_b, slope_b
    )
    dx_b, home, down_other = bar((dx_b, home, down_other))

    def attend_part(gain, shift, block_a, x_a, packed_a, mixed_a, pair_b, pair_c, dx_b):
        own_c, far_c = plan.scatter_send(plan.scatter_stack(pair_c))
        dx_a, dpacked_a, normed_a, low_a, gain_a, shift_a = attend_backward(
            x_a, dx_b, packed_a, gain[0], shift[0], block_a
        )
        pair_b, dx_a, far_c = bar((plan.scatter_side(pair_b, 0), dx_a, far_c))
        pair_c = plan.scatter_add(own_c, far_c)
        return dx_a, dpacked_a, normed_a, low_a, gain_a, shift_a, pair_b, pair_c

    dx_a, dpacked_a, normed_a, low_a, gain_a, shift_a, pair_b, pair_c = fenced(
        ready, attend_part, gain, shift, block_a, x_a, packed_a, mixed_a, pair_b, pair_c, dx_b
    )
    pair_b, in_pair = bar((pair_b, in_pair))
    in_own, in_other = plan.share_send(in_pair)

    def combine_part(dpacked_a, normed_a, low_a, mixed_a, pair_b, pair_c, norms, x_d, spots, gates, cot, home):
        norm_grads = jnp.concatenate(norms).T
        act_out, grad_gate = combine(spots, gates, x_d, cot, home)
        sum_a = weight_grad(
            plan.wide, core, (flat(normed_a), flat(dpacked_a)), (flat(low_a), flat(mixed_a))
        )
        pair_b, sum_a, act_out = bar((plan.scatter_side(pair_b, 1), sum_a, act_out))
        return norm_grads, sum_a, plan.scatter_stack(pair_b), plan.scatter_near(pair_c), act_out, grad_gate

    norm_grads, sum_a, deep_b, near_c, act_out, grad_gate = fenced(
        ready, combine_part, dpacked_a, normed_a, low_a, mixed_a, pair_b, pair_c,
        (gain_a, gain_b) + gains + (shift_a, shift_b) + shifts, x_d, spots, gates, cot, home,
    )
    own_b, far_b = plan.scatter_send(deep_b)


    def fifth_part(sum_a, act_out, grad_gate, dx_a, down_share):
        grad_exp_out = plan.share_sum(*down_share)
        pair_a = bar(plan.scatter_swap(sum_a))
        pair_a = bar(plan.scatter_side(pair_a, 0))
        deep_a = plan.scatter_stack(plan.scatter_side(pair_a, 1))
        return deep_a, unpadded(act_out), unpadded(grad_gate), unpadded(dx_a), grad_exp_out

    deep_a, act_out, grad_gate, dx_a, grad_exp_out = fenced(
        ready, fifth_part, sum_a, act_out, grad_gate, dx_a, (down_own, down_other)
    )
    deep_a, own_b, far_b, in_other = bar((deep_a, own_b, far_b, in_other))

    def sixth_part(deep_a, own_b, far_b, near_c, norm_grads, in_share):
        norm_pieces = plan.small_send(norm_grads)
        own_a, far_a = plan.scatter_send(deep_a)
        near_b = plan.scatter_near(plan.scatter_add(own_b, far_b))
        near_b, far_a = bar((near_b, far_a))
        grad_exp_in = plan.share_sum(*in_share)
        near_a, mine_bc = bar(
            (plan.scatter_near(plan.scatter_add(own_a, far_a)), plan.scatter_core(plan.scatter_join(near_b, near_c)))
        )
        mine_norms = plan.small_sum(norm_pieces)
        return plan.scatter_core(near_a), mine_bc, mine_norms, grad_exp_in

    mine_a, mine_bc, mine_norms, grad_exp_in = fenced(
        ready, sixth_part, deep_a, own_b, far_b, near_c, norm_grads,
        (in_own, in_other),
    )
    mine_b, mine_c = plan.scatter_unstack(mine_bc, 2 * FF, 4 * D)
    grad_exp_out = jnp.swapaxes(grad_exp_out, 1, 2)

    grad_qkv = jnp.stack([mine_a[:, : 3 * D], mine_c[:, : 3 * D]])
    grad_proj = jnp.stack([mine_a[:, 3 * D :], mine_c[:, 3 * D :]])
    return (
        act_out,
        dx_a,
        grad_qkv,
        jnp.swapaxes(grad_proj, 1, 2),
        mine_b[:, :FF],
        mine_b[:, FF:].T,
        mine_norms[:, :4].T,
        mine_norms[:, 4:].T,
        grad_exp_in,
        grad_exp_out,
        grad_gate,
    )


def solution(mesh):
    plan = Plan(mesh)
    rows, dp, expert = plan.axes, plan.dp, plan.expert
    in_specs = (
        P(rows, None),
        P(None, rows, None),
        P(None, None, rows),
        P(rows, None),
        P(None, rows),
        P(None, rows),
        P(None, rows),
        P(expert, dp, None),
        P(expert, None, dp),
        P(rows, None),
        P(rows, None),
        P(rows, None),
    )
    out_specs = (
        P(rows, None),
        P(rows, None),
        P(None, rows, None),
        P(None, None, rows),
        P(rows, None),
        P(None, rows),
        P(None, rows),
        P(None, rows),
        P(expert, dp, None),
        P(expert, None, dp),
        P(rows, None),
    )
    return jax.shard_map(
        functools.partial(local, plan),
        mesh=plan.mesh,
        in_specs=in_specs,
        out_specs=out_specs,
        check_vma=False,
    )
```
